32 devices in a mesh: req: 8 (over y, x, core), tp: 4 (over z).
Axes of the slice: x: 2, y: 2, z: 4, core: 2. Of those that a mesh axis runs over, the one named last changes fastest.
Arguments:
- new_query: bfloat16 [1024, 2560], P('req', 'tp'), may hold values from -64 to 64
- new_keyval: bfloat16 [1024, 1280], P('req', 'tp'), may hold values from -24 to 24
- residual_in: bfloat16 [1024, 2560], P('req'), may hold values from -64 to 64
- leaf_cache: bfloat16 [128, 32, 1280], P('req', None, 'tp'), may hold values from -6 to 6
- leaf_length: int32 [128], P('req'), may hold values from 1 to 32
- new_counts: int32 [8, 16], P('req'), may hold values from 1 to 16, as said below
- request_mid: int32 [128], P('req'), may hold values from 0 to 5
- mid_root: int32 [6], replicated, may hold values from 0 to 1, as said below
- node_length: int32 [8], replicated, may hold values from 1 to 1744, as said below
- prefix_pool: bfloat16 [256, 16, 1280], P('req', None, 'tp'), may hold values from -6 to 6
- page_node: int32 [256], P('req'), may hold values from -1 to 7, as said below
- page_rank: int32 [256], P('req'), may hold values from 0 to 108, as said below
- out_weight: bfloat16 [2560, 2560], P('tp'), may hold values from -0.125 to 0.125
- norm_gain: bfloat16 [2560], replicated, may hold values from 0.5 to 1.5
- gate_weight: bfloat16 [2560, 3584], P(None, 'tp'), may hold values from -0.125 to 0.125
- up_weight: bfloat16 [2560, 3584], P(None, 'tp'), may hold values from -0.125 to 0.125
- down_weight: bfloat16 [3584, 2560], P('tp'), may hold values from -0.09375 to 0.09375
- next_gain: bfloat16 [2560], replicated, may hold values from 0.5 to 1.5
- query_weight: bfloat16 [2560, 2560], P(None, 'tp'), may hold values from -0.125 to 0.125
- keyval_weight: bfloat16 [2560, 1280], P(None, 'tp'), may hold values from -0.125 to 0.125
Outputs:
- attention: bfloat16 [1024, 2560], P('req', 'tp')
- residual_out: bfloat16 [1024, 2560], P(('req', 'tp'))
- next_query: bfloat16 [1024, 2560], P('req', 'tp')
- next_keyval: bfloat16 [1024, 1280], P('req', 'tp')
The draws below stay inside these ranges and needn't reach their ends.
Inputs may be any that keep to these rules, and one draw needn't show every extreme that they name: `new_counts`: each row sums to 128 and holds one request of exactly 16 new tokens. `mid_root`: each root is the parent of 3 mid-level nodes. `node_length`: A node of k pages has more than 16 * (k - 1) and at most 16 * k prefix tokens; a node with the most pages has exactly 16 * k. `page_node`: every node owns one page or more; 32 pages are free (-1). `page_rank`: the k pages of a node carry the ranks 0 to k - 1, each once; free pages carry 0.
All inputs are finite; a program needn't handle non-finite values.
Results may differ from the reference program's by a relative error of at most 0.015.
Values may be sent and summed in bfloat16 or wider, within the bound.
No kernel may reach another device: no remote copies, remote signals or barrier semaphores. Data moves between devices by JAX's collectives and lax.ppermute only.
A program may use at most 128 MiB of HBM per device.

```python
import math
import jax
import jax.numpy as jnp
import numpy as np
from jax import lax

D = 2560
H = 32
KVH = 8
HD = 80
FW = 3584
TOK_DEV = 128
MAXNEW = 16
R_DEV = 16
LEAF = 32
PAGE = 16
ROOTS = 2
MIDS = 6
NODES = 8
HOLDERS = 8
TOKENS = 1024
REQUESTS = 128
POOL = 256
N_REQ = 8


def pair_counts(key):
    base = jax.random.fold_in(key, 11)
    first_key, second_key, order_key = jax.random.split(base, 3)
    half = R_DEV // 2
    firsts = jax.random.randint(first_key, (HOLDERS, half), 1, MAXNEW, dtype=jnp.int32)
    lifted = jax.random.randint(second_key, (HOLDERS,), 2, MAXNEW, dtype=jnp.int32)
    firsts = firsts.at[:, 0].set(MAXNEW - 1)
    firsts = firsts.at[:, 1].set(lifted)
    seconds = MAXNEW - firsts
    firsts = firsts.at[:, 0].add(1)
    firsts = firsts.at[:, 1].add(-1)
    counts = jnp.concatenate([firsts, seconds], axis=1)
    ranking = jax.random.randint(order_key, (HOLDERS, R_DEV), 0, 1 << 20, dtype=jnp.int32) * R_DEV + jnp.arange(R_DEV, dtype=jnp.int32)[None, :]
    order = jnp.argsort(ranking, axis=1, stable=True)
    return jnp.take_along_axis(counts, order, axis=1).astype(jnp.int32)


def pool_tables(key):
    base = jax.random.fold_in(key, 37)
    level_key, label_key, length_key, place_key = jax.random.split(base, 4)
    spare = POOL // 8
    used = POOL - spare
    extra = used - NODES
    heavy = (extra + 1) // 2
    rest = extra - heavy
    level_draw = jax.random.randint(level_key, (rest,), 1, 2 ** (NODES - 1), dtype=jnp.int32)
    powers = 2 ** jnp.arange(1, NODES - 1, dtype=jnp.int32)
    levels = (1 + jnp.sum((level_draw[:, None] >= powers[None, :]).astype(jnp.int32), axis=1)).astype(jnp.int32)
    labels_raw = jnp.concatenate([jnp.arange(NODES, dtype=jnp.int32), jnp.zeros((heavy,), jnp.int32), levels])
    relabel = jax.random.permutation(label_key, NODES).astype(jnp.int32)
    labels = relabel[labels_raw]
    onehot = (labels[:, None] == jnp.arange(NODES, dtype=jnp.int32)[None, :]).astype(jnp.int32)
    ranks = jnp.sum((jnp.cumsum(onehot, axis=0) - onehot) * onehot, axis=1).astype(jnp.int32)
    counts = jnp.sum(onehot, axis=0).astype(jnp.int32)
    tails = jax.random.randint(length_key, (NODES,), 1, PAGE + 1, dtype=jnp.int32)
    tails = jnp.where(counts == jnp.max(counts), PAGE, tails).astype(jnp.int32)
    lengths = (counts - 1) * PAGE + tails
    node_full = jnp.concatenate([labels, jnp.full((spare,), -1, jnp.int32)])
    rank_full = jnp.concatenate([ranks, jnp.zeros((spare,), jnp.int32)])
    shuffle = jax.random.permutation(place_key, POOL)
    return (node_full[shuffle].astype(jnp.int32), rank_full[shuffle].astype(jnp.int32), lengths.astype(jnp.int32))


def noise(key, shape):
    return jnp.clip(jax.random.normal(key, shape, jnp.float32), -6.0, 6.0)


def query_keyval(key):
    base = jax.random.fold_in(key, 53)
    common_key, query_key, keyed, value_key = jax.random.split(base, 4)
    group = H // KVH
    common = noise(common_key, (TOKENS, KVH, HD))
    query = common[:, :, None, :] + noise(query_key, (TOKENS, KVH, group, HD))
    keys = 0.7 * common + 0.7 * noise(keyed, (TOKENS, KVH, HD))
    values = noise(value_key, (TOKENS, KVH, HD))
    query_out = query.reshape(TOKENS, H * HD)
    keyval = jnp.stack([keys, values], axis=2).reshape(TOKENS, KVH * 2 * HD)
    return (query_out, keyval)


def draw_new_query(key, part):
    return query_keyval(key)[0].astype(jnp.bfloat16)


def draw_new_keyval(key, part):
    return query_keyval(key)[1].astype(jnp.bfloat16)


def draw_residual_in(key, part):
    base = jax.random.fold_in(key, 71)
    row_key, column_key, main_key = jax.random.split(base, 3)
    row_scale = jnp.exp(jax.random.uniform(row_key, (TOKENS, 1), jnp.float32, math.log(0.3), math.log(3.0)))
    column_scale = jnp.exp(jax.random.uniform(column_key, (1, D), jnp.float32, math.log(0.3), math.log(3.0)))
    values = jnp.clip(jax.random.normal(main_key, (TOKENS, D), jnp.float32), -6.0, 6.0)
    return (values * row_scale * column_scale).astype(jnp.bfloat16)


def draw_new_counts(key, part):
    return pair_counts(key)


def draw_mid_root(key, part):
    order = jax.random.permutation(jax.random.fold_in(key, 23), MIDS).astype(jnp.int32)
    return (order % ROOTS).astype(jnp.int32)


def draw_node_length(key, part):
    return pool_tables(key)[2]


def draw_page_node(key, part):
    return pool_tables(key)[0]


def draw_page_rank(key, part):
    return pool_tables(key)[1]


def touch_ends(result, rng, low, largest):
    longest = result.shape.index(max(result.shape))
    spots = []
    for shift in (0, 1):
        where = [jax.random.randint(jax.random.fold_in(rng, axis), (), 0, length) for axis, length in enumerate(result.shape)]
        where[longest] = (where[longest] + shift) % result.shape[longest]
        spots.append(tuple(where))
    return result.at[spots[0]].set(low).at[spots[1]].set(largest)


def block_levels(own_key, shape, cuts, smallest, largest):
    level, own = 1.0, jax.random.fold_in(own_key, 6)
    for axis_at, shards_of in cuts:
        heights = jnp.exp(jax.random.uniform(jax.random.fold_in(own, axis_at), (shards_of,), jnp.float32, smallest / len(cuts), largest / len(cuts)))
        level = level * jnp.repeat(heights, shape[axis_at] // shards_of).reshape([-1 if axis == axis_at else 1 for axis in range(len(shape))])
    return level


def rank_table(number_of, lean):
    loads = [(1 << 20) // math.isqrt(grade ** lean) + 1 for grade in range(1, number_of + 1)]
    spread = 1 + sum(loads) // (1 << 30)
    return np.cumsum(np.array([max(1, weight // spread) for weight in loads]))


def ranked(stream_key, shape, count, lean):
    grid = rank_table(count, lean)
    lot = jax.random.randint(jax.random.fold_in(stream_key, 1), shape, 0, int(grid[count - 1]))
    rank = jnp.searchsorted(jnp.asarray(grid, jnp.int32), lot, side="right")
    return jax.random.permutation(jax.random.fold_in(stream_key, 2), count)[rank].astype(jnp.int32)


def scatter_about(own_key, dims, width, bound, pieces=(), kind=jnp.bfloat16):
    array = jax.random.normal(own_key, dims, jnp.float32) * width
    if len(pieces) > 0:
        array = block_levels(own_key, dims, pieces, -0.22, 0.18) * array
    return jnp.clip(array, min=-bound, max=bound).astype(kind)


def setup_inputs(seed: int = 0) -> dict:
    streams_of = jax.random.split(jax.random.key(seed), 21)
    new_query = draw_new_query(jax.random.fold_in(streams_of[20], 71), 0)
    new_keyval = draw_new_keyval(jax.random.fold_in(streams_of[20], 71), 0)
    residual_in = draw_residual_in(jax.random.fold_in(streams_of[20], 71), 0)
    leaf_cache = scatter_about(streams_of[3], (REQUESTS, LEAF, KVH * 2 * HD), 1.0, 6.0, ((0, 8), (2, 4)))
    leaf_length = touch_ends(jax.random.randint(streams_of[4], (REQUESTS,), 1, LEAF + 1), jax.random.fold_in(streams_of[4], 1), 1, LEAF).astype(jnp.int32)
    new_counts = draw_new_counts(jax.random.fold_in(streams_of[20], 71), 0)
    request_mid = touch_ends(ranked(streams_of[6], (REQUESTS,), MIDS, 2), jax.random.fold_in(streams_of[6], 3), 0, MIDS - 1).astype(jnp.int32)
    mid_root = draw_mid_root(jax.random.fold_in(streams_of[20], 71), 0)
    node_length = draw_node_length(jax.random.fold_in(streams_of[20], 71), 0)
    prefix_pool = scatter_about(streams_of[9], (POOL, PAGE, KVH * 2 * HD), 1.0, 6.0, ((0, 8), (2, 4)))
    page_node = draw_page_node(jax.random.fold_in(streams_of[20], 71), 0)
    page_rank = draw_page_rank(jax.random.fold_in(streams_of[20], 71), 0)
    out_weight = scatter_about(streams_of[12], (H * HD, D), (H * HD) ** -0.5, 0.125, ((0, 4),))
    norm_gain = jnp.clip(1.0 + 0.1 * jax.random.normal(streams_of[13], (D,), jnp.float32), 0.5, 1.5).astype(jnp.bfloat16)
    gate_weight = scatter_about(streams_of[14], (D, FW), D ** -0.5, 0.125, ((1, 4),))
    up_weight = scatter_about(streams_of[15], (D, FW), D ** -0.5, 0.125, ((1, 4),))
    down_weight = scatter_about(streams_of[16], (FW, D), FW ** -0.5, 0.09375, ((0, 4),))
    next_gain = jnp.clip(1.0 + 0.1 * jax.random.normal(streams_of[17], (D,), jnp.float32), 0.5, 1.5).astype(jnp.bfloat16)
    query_weight = scatter_about(streams_of[18], (D, H * HD), D ** -0.5, 0.125, ((1, 4),))
    keyval_weight = scatter_about(streams_of[19], (D, KVH * 2 * HD), D ** -0.5, 0.125, ((1, 4),))
    return {"new_query": new_query, "new_keyval": new_keyval, "residual_in": residual_in, "leaf_cache": leaf_cache, "leaf_length": leaf_length, "new_counts": new_counts, "request_mid": request_mid, "mid_root": mid_root, "node_length": node_length, "prefix_pool": prefix_pool, "page_node": page_node, "page_rank": page_rank, "out_weight": out_weight, "norm_gain": norm_gain, "gate_weight": gate_weight, "up_weight": up_weight, "down_weight": down_weight, "next_gain": next_gain, "query_weight": query_weight, "keyval_weight": keyval_weight}


MASKED = -1e+30
EPSILON = 1e-05

def rms_scale(values_in, gain):
    values = values_in.astype(jnp.float32)
    scale = lax.rsqrt(lax.optimization_barrier(jnp.mean(values * values, axis=-1, keepdims=True)) + EPSILON)
    return (values * scale * gain.astype(jnp.float32)).astype(jnp.bfloat16)

def token_tables(counts, mids_of_requests, mid_root, node_length):
    starts = (jnp.cumsum(counts) - counts).astype(jnp.int32)
    index = jnp.arange(TOK_DEV, dtype=jnp.int32)
    owner = (lax.optimization_barrier(jnp.sum((index[:, None] >= starts[None, :]).astype(jnp.int32), axis=1)) - 1).astype(jnp.int32)
    pick = (owner[:, None] == jnp.arange(R_DEV, dtype=jnp.int32)[None, :]).astype(jnp.int32)
    offset = (index - lax.optimization_barrier(jnp.sum(pick * starts[None, :], axis=1))).astype(jnp.int32)
    token_mid = lax.optimization_barrier(jnp.sum(pick * mids_of_requests[None, :], axis=1)).astype(jnp.int32)
    mid_pick = (token_mid[:, None] == jnp.arange(MIDS, dtype=jnp.int32)[None, :]).astype(jnp.int32)
    token_root = lax.optimization_barrier(jnp.sum(mid_pick * mid_root[None, :], axis=1)).astype(jnp.int32)
    mid_node = (token_mid + ROOTS).astype(jnp.int32)
    node_ids = jnp.arange(NODES, dtype=jnp.int32)
    root_len = lax.optimization_barrier(jnp.sum((token_root[:, None] == node_ids[None, :]).astype(jnp.int32) * node_length[None, :], axis=1)).astype(jnp.int32)
    mid_len = lax.optimization_barrier(jnp.sum((mid_node[:, None] == node_ids[None, :]).astype(jnp.int32) * node_length[None, :], axis=1)).astype(jnp.int32)
    return (starts, owner, offset, token_root, mid_node, root_len, mid_len)

def reference(new_query, new_keyval, residual_in, leaf_cache, leaf_length, new_counts, request_mid, mid_root, node_length, prefix_pool, page_node, page_rank, out_weight, norm_gain, gate_weight, up_weight, down_weight, next_gain, query_weight, keyval_weight):
    group = H // KVH
    scale = 1.0 / math.sqrt(HD)
    pool_flat = prefix_pool.astype(jnp.float32).reshape(POOL * PAGE, KVH, 2, HD)
    pool_keys = pool_flat[:, :, 0]
    pool_values = pool_flat[:, :, 1]
    key_node = jnp.repeat(page_node, PAGE, total_repeat_length=POOL * PAGE)
    key_pos = (page_rank[:, None] * PAGE + jnp.arange(PAGE, dtype=jnp.int32)[None, :]).reshape(POOL * PAGE)

    def device_block(items):
        query, keyval, leaf, leaf_len, counts, mids_of_requests = items
        starts, owner, offset, token_root, mid_node, root_len, mid_len = token_tables(counts, mids_of_requests, mid_root, node_length)
        heads = query.astype(jnp.float32).reshape(TOK_DEV, KVH, group, HD)
        shared_scores = jnp.einsum('tkgd,mkd->tkgm', heads, pool_keys) * scale
        root_hit = (key_node[None, :] == token_root[:, None]) & (key_pos[None, :] < root_len[:, None])
        mid_hit = (key_node[None, :] == mid_node[:, None]) & (key_pos[None, :] < mid_len[:, None])
        shared_ok = (root_hit | mid_hit)[:, None, None, :]
        slot = jnp.arange(MAXNEW, dtype=jnp.int32)
        row_index = jnp.clip(starts[:, None] + slot[None, :], 0, TOK_DEV - 1).astype(jnp.int32)
        pad_query = heads[row_index]
        pad_keyval = keyval.astype(jnp.float32)[row_index].reshape(R_DEV, MAXNEW, KVH, 2, HD)
        leaf_values = leaf.astype(jnp.float32).reshape(R_DEV, LEAF, KVH, 2, HD)
        joined = jnp.concatenate([leaf_values, pad_keyval], axis=1)
        local_scores = jnp.einsum('rskgd,rmkd->rskgm', pad_query, joined[:, :, :, 0]) * scale
        leaf_ok = jnp.broadcast_to(jnp.arange(LEAF, dtype=jnp.int32)[None, None, :] < leaf_len[:, None, None], (R_DEV, MAXNEW, LEAF))
        causal = jnp.broadcast_to(slot[None, None, :] <= slot[None, :, None], (R_DEV, MAXNEW, MAXNEW))
        local_ok = jnp.concatenate([leaf_ok, causal], axis=2)[:, :, None, None, :]
        flat = (owner * MAXNEW + offset).astype(jnp.int32)
        shared_top = lax.optimization_barrier(jnp.max(jnp.where(shared_ok, shared_scores, MASKED), axis=-1))
        local_top = lax.optimization_barrier(jnp.max(jnp.where(local_ok, local_scores, MASKED), axis=-1))
        top = jnp.maximum(shared_top, local_top.reshape(R_DEV * MAXNEW, KVH, group)[flat])
        shared_exp = jnp.where(shared_ok, jnp.exp(shared_scores - top[..., None]), 0.0)
        local_exp = jnp.where(local_ok, jnp.exp(local_scores - top[row_index][..., None]), 0.0)
        shared_weights = lax.optimization_barrier(shared_exp.astype(jnp.bfloat16)).astype(jnp.float32)
        local_weights = lax.optimization_barrier(local_exp.astype(jnp.bfloat16)).astype(jnp.float32)
        shared_sum = jnp.einsum('tkgm,mkd->tkgd', shared_weights, pool_values)
        local_sum = jnp.einsum('rskgm,rmkd->rskgd', local_weights, joined[:, :, :, 1])
        total = lax.optimization_barrier(jnp.sum(shared_exp, axis=-1)) + lax.optimization_barrier(jnp.sum(local_exp, axis=-1)).reshape(R_DEV * MAXNEW, KVH, group)[flat]
        weighted = shared_sum + local_sum.reshape(R_DEV * MAXNEW, KVH, group, HD)[flat]
        return (weighted / total[..., None]).reshape(TOK_DEV, H * HD).astype(jnp.bfloat16)
    blocks = lax.map(device_block, (new_query.reshape(N_REQ, TOK_DEV, H * HD), new_keyval.reshape(N_REQ, TOK_DEV, KVH * 2 * HD), leaf_cache.reshape(N_REQ, R_DEV, LEAF, KVH * 2 * HD), leaf_length.reshape(N_REQ, R_DEV), new_counts, request_mid.reshape(N_REQ, R_DEV)))
    attention = blocks.reshape(TOKENS, H * HD)
    attn_proj = jnp.dot(attention, out_weight, preferred_element_type=jnp.float32)
    mixed = (residual_in.astype(jnp.float32) + attn_proj).astype(jnp.bfloat16)
    normed = rms_scale(mixed, norm_gain)
    gate = jnp.dot(normed, gate_weight, preferred_element_type=jnp.float32)
    upward = jnp.dot(normed, up_weight, preferred_element_type=jnp.float32)
    hidden = (jax.nn.silu(gate) * upward).astype(jnp.bfloat16)
    mlp_proj = jnp.dot(hidden, down_weight, preferred_element_type=jnp.float32)
    residual_out = (mixed.astype(jnp.float32) + mlp_proj).astype(jnp.bfloat16)
    final = rms_scale(residual_out, next_gain)
    next_query = jnp.dot(final, query_weight, preferred_element_type=jnp.float32).astype(jnp.bfloat16)
    next_keyval = jnp.dot(final, keyval_weight, preferred_element_type=jnp.float32).astype(jnp.bfloat16)
    return (attention, residual_out, next_query, next_keyval)
```

```python
import functools
import math

import jax
import jax.numpy as jnp
from jax import lax
from jax.experimental import pallas as pl
from jax.experimental.pallas import tpu as pltpu
from jax.sharding import PartitionSpec as P

HD = 80
ROOTS = 2
MIDS = 6
LANES = 128
MASKED = -1e30
EPSILON = 1e-05
RATE = math.log2(math.e) / math.sqrt(HD)

bf16 = jnp.bfloat16
f32 = jnp.float32
i32 = jnp.int32
VMEM = pl.BlockSpec(memory_space=pltpu.VMEM)
SMEM = pl.BlockSpec(memory_space=pltpu.SMEM)
PARAMS = pltpu.CompilerParams(vmem_limit_bytes=48 * 1024 * 1024)


def padded(width):
    return -(-width // LANES) * LANES


def key_start(c):
    return c * 2 * HD // LANES * LANES


def key_shift(c):
    return c * 2 * HD % LANES


def value_start(c):
    return (c * 2 * HD + HD) // LANES * LANES


def value_shift(c):
    return (c * 2 * HD + HD) % LANES


def key_window(ref, c):
    first = ref[:, key_start(c) : key_start(c) + LANES]
    last = ref[:, ref.shape[1] - LANES :]
    return jnp.concatenate([first, last], axis=1)


def value_window(ref, c):
    stop = min(value_start(c) + 2 * LANES, ref.shape[1])
    return ref[:, value_start(c) : stop]


def scores_of(query, keys):
    return lax.dot_general(query, keys, (((1,), (1,)), ((), ())), preferred_element_type=f32)


def prep_kernel(node_ref, rank_ref, length_ref, root_ref, pool_ref, out_ref):
    pages, size, width = pool_ref.shape
    free = out_ref.shape[1] - width
    lane = lax.broadcasted_iota(i32, (size, free), 1)
    slot = lax.broadcasted_iota(i32, (size, free), 0)
    root = jnp.full((size, free), -2, i32)
    for m in range(MIDS):
        root = jnp.where(lane == m, root_ref[m], root)
    hidden = jnp.where(lane < MIDS, MASKED, 0.0)
    for p in range(pages):
        node = node_ref[p]
        left = length_ref[jnp.maximum(node, 0)] - size * rank_ref[p]
        seen = ((root == node) | (lane + ROOTS == node)) & (slot < left)
        rows = slice(p * size, (p + 1) * size)
        out_ref[rows, :width] = pool_ref[p]
        out_ref[rows, width:] = jnp.where(seen, 0.0, hidden).astype(bf16)


def prepare(page_node, page_rank, node_length, mid_root, prefix_pool):
    pages, size, width = prefix_pool.shape
    return pl.pallas_call(
        prep_kernel,
        out_shape=jax.ShapeDtypeStruct((pages * size, padded(width + MIDS)), bf16),
        in_specs=[SMEM, SMEM, SMEM, SMEM, VMEM],
        out_specs=VMEM,
        compiler_params=PARAMS,
        name="pool_rows",
    )(page_node, page_rank, node_length, mid_root, prefix_pool)


def fold(scores, values, state):
    top = functools.reduce(jnp.maximum, [jnp.max(s, axis=1, keepdims=True) for s in scores])
    if state is not None:
        top = jnp.maximum(top, state[0])
    total, weighted = None, None
    for s, v in zip(scores, values):
        raised = jnp.exp2((s - top) * RATE)
        part = jnp.sum(raised, axis=1, keepdims=True)
        mixed = jnp.dot(raised.astype(bf16), v, preferred_element_type=f32)
        total = part if total is None else total + part
        if weighted is None:
            weighted = mixed
        else:
            weighted = weighted + mixed
    if state is not None:
        factor = jnp.exp2((state[0] - top) * RATE)
        total = total + state[1] * factor
        weighted = weighted + state[2] * factor
    return top, total, weighted


def pack(top, total, weighted):
    lane = lax.broadcasted_iota(i32, weighted.shape, 1)
    return jnp.where(lane == 0, top, jnp.where(lane == 1, total, weighted))


def unpack(state):
    return state[:, 0:1], state[:, 1:2], state


def write_out(out_ref, state, c, group, rows):
    _, total, weighted = state
    shift = value_shift(c)
    result = (weighted[:, shift : shift + HD] / total).astype(bf16)
    for g in range(group):
        h = c * group + g
        out_ref[:, h * HD : (h + 1) * HD] = result[g * rows : (g + 1) * rows]


def local_kernel(count_ref, mid_ref, leaf_len_ref, query_ref, keyval_ref, leaf_ref, *refs, chunks):
    pool_refs, (aug_ref, state_ref) = refs[:chunks], refs[chunks:]
    rows = query_ref.shape[0]
    width = keyval_ref.shape[1]
    requests, slots, _ = leaf_ref.shape
    kv_local = width // (2 * HD)
    group = query_ref.shape[1] // (kv_local * HD)
    row = lax.broadcasted_iota(i32, (rows, LANES), 0)
    lane = lax.broadcasted_iota(i32, (rows, LANES), 1)
    zero = jnp.zeros((rows, LANES), i32)
    start, low, high, mid = zero, zero, zero, zero
    begin = jnp.int32(0)
    for r in range(requests):
        here = row >= begin
        start = jnp.where(here, begin, start)
        low = jnp.where(here, r * slots, low)
        high = jnp.where(here, r * slots + leaf_len_ref[r], high)
        mid = jnp.where(here, mid_ref[r], mid)
        begin = begin + count_ref[0, r]
    chosen = jnp.where(lane == width % LANES + mid, 1.0, 0.0).astype(bf16)

    leaf_all = leaf_ref[...].reshape(requests * slots, width)
    leaf_at = lax.broadcasted_iota(i32, (rows, requests * slots), 1)
    leaf_ok = (leaf_at >= low[:, 0:1]) & (leaf_at < high[:, 0:1])
    new_ok = (lane >= start) & (lane <= row)
    for c in range(kv_local):
        base = c * group * rows
        key0, val0 = key_start(c), value_start(c)
        shift = key_shift(c)
        for g in range(group):
            h = c * group + g
            at = slice(base + g * rows, base + (g + 1) * rows)
            aug_ref[at, :LANES] = jnp.zeros((rows, LANES), bf16)
            aug_ref[at, shift : shift + HD] = query_ref[:, h * HD : (h + 1) * HD]
            aug_ref[at, LANES:] = chosen
        query = aug_ref[base : base + group * rows, :]
        narrow = query[:, :LANES]
        s_leaf = scores_of(narrow, leaf_all[:, key0 : key0 + LANES])
        s_leaf = jnp.where(leaf_ok[None], s_leaf.reshape(group, rows, -1), MASKED)
        s_new = scores_of(narrow, keyval_ref[:, key0 : key0 + LANES])
        s_new = jnp.where(new_ok[None], s_new.reshape(group, rows, -1), MASKED)
        scores = [s_leaf.reshape(group * rows, -1), s_new.reshape(group * rows, -1)]
        stop = min(val0 + 2 * LANES, width)
        fill = val0 + 2 * LANES - stop
        values = [leaf_all[:, val0:stop], keyval_ref[:, val0:stop]]
        if fill:
            values = [
                jnp.concatenate([v, jnp.zeros((v.shape[0], fill), bf16)], axis=1) for v in values
            ]
        for ref in pool_refs:
            scores.append(scores_of(query, key_window(ref, c)))
            values.append(value_window(ref, c))
        state_ref[base : base + group * rows, :] = pack(*fold(scores, values, None))


def chunk_kernel(*refs, last, kv_local, rows):
    aug_ref, state_ref = refs[:2]
    pool_refs, out_ref = refs[2:-1], refs[-1]
    block = aug_ref.shape[0] // kv_local
    for c in range(kv_local):
        at = slice(c * block, (c + 1) * block)
        query = aug_ref[at, :]
        scores = [scores_of(query, key_window(ref, c)) for ref in pool_refs]
        values = [value_window(ref, c) for ref in pool_refs]
        state = fold(scores, values, unpack(state_ref[at, :]))
        if last:
            write_out(out_ref, state, c, block // rows, rows)
        else:
            out_ref[at, :] = pack(*state)


def start_attention(new_query, new_keyval, leaf, leaf_length, counts, request_mid, pools):
    rows, query_width = new_query.shape
    heads = query_width // HD
    return pl.pallas_call(
        functools.partial(local_kernel, chunks=len(pools)),
        out_shape=(
            jax.ShapeDtypeStruct((heads * rows, 2 * LANES), bf16),
            jax.ShapeDtypeStruct((heads * rows, 2 * LANES), f32),
        ),
        in_specs=[SMEM] * 3 + [VMEM] * (3 + len(pools)),
        out_specs=(VMEM, VMEM),
        compiler_params=PARAMS,
        name="attend_local",
    )(counts, request_mid, leaf_length, new_query, new_keyval, leaf, *pools)


def extend_attention(aug, state, pools, last, kv_local, rows):
    if last:
        shape = jax.ShapeDtypeStruct((rows, aug.shape[0] // rows * HD), bf16)
    else:
        shape = jax.ShapeDtypeStruct(state.shape, f32)
    return pl.pallas_call(
        functools.partial(chunk_kernel, last=last, kv_local=kv_local, rows=rows),
        out_shape=shape,
        in_specs=[VMEM] * (2 + len(pools)),
        out_specs=VMEM,
        compiler_params=PARAMS,
        name="attend_pages",
    )(aug, state, *pools)


def trade(value, axis, bit):
    size = lax.axis_size(axis)
    return lax.ppermute(value, axis, [(i, i ^ bit) for i in range(size)])


def total_over_tp(partial):
    if lax.axis_size("tp") != 4:
        return lax.psum(partial, "tp")
    half = partial.shape[1] // 2
    first, second = partial[:, :half].astype(bf16), partial[:, half:].astype(bf16)
    first_in, second_in = trade(first, "tp", 3), trade(second, "tp", 1)
    first = (first.astype(f32) + first_in.astype(f32)).astype(bf16)
    second = (second.astype(f32) + second_in.astype(f32)).astype(bf16)
    first_in, second_in = trade(first, "tp", 1), trade(second, "tp", 3)
    first = first.astype(f32) + first_in.astype(f32)
    second = second.astype(f32) + second_in.astype(f32)
    return jnp.concatenate([first, second], axis=1)


def rms_scale(values_in, gain):
    values = values_in.astype(f32)
    scale = lax.rsqrt(jnp.mean(values * values, axis=-1, keepdims=True) + EPSILON)
    return (values * scale * gain.astype(f32)).astype(bf16)


def per_device(
    new_query,
    new_keyval,
    residual_in,
    leaf_cache,
    leaf_length,
    new_counts,
    request_mid,
    mid_root,
    node_length,
    prefix_pool,
    page_node,
    page_rank,
    out_weight,
    norm_gain,
    gate_weight,
    up_weight,
    down_weight,
    next_gain,
    query_weight,
    keyval_weight,
):
    row_count = new_query.shape[0]
    kv_local = new_keyval.shape[1] // (2 * HD)
    pool = prepare(page_node, page_rank, node_length, mid_root, prefix_pool)
    local_args = (new_query, new_keyval, leaf_cache, leaf_length, new_counts, request_mid)
    if lax.axis_size("req") == 8:
        far = [trade(pool, "req", bit) for bit in (2, 4, 6)]
        beside = trade(pool, "req", 1)
        aug, state = start_attention(*local_args, [pool, beside])
        other = [trade(item, "req", 1) for item in far]
        state = extend_attention(aug, state, far, False, kv_local, row_count)
        attention = extend_attention(aug, state, other, True, kv_local, row_count)
    else:
        every = lax.all_gather(pool, "req", axis=0)
        aug, state = start_attention(*local_args, [])
        step = 4
        for i in range(0, every.shape[0], step):
            chunk = [every[i : i + step].reshape(-1, pool.shape[1])]
            last = i + step >= every.shape[0]
            state = extend_attention(aug, state, chunk, last, kv_local, row_count)
        attention = state

    share = row_count // lax.axis_size("tp")
    mine = lax.axis_index("tp") * share
    attn_proj = total_over_tp(jnp.dot(attention, out_weight, preferred_element_type=f32))
    mixed = (residual_in.astype(f32) + attn_proj).astype(bf16)
    normed = rms_scale(mixed, norm_gain)
    gate = jnp.dot(normed, gate_weight, preferred_element_type=f32)
    upward = jnp.dot(normed, up_weight, preferred_element_type=f32)
    hidden = (jax.nn.silu(gate) * upward).astype(bf16)
    mlp_proj = total_over_tp(jnp.dot(hidden, down_weight, preferred_element_type=f32))
    layer_rows = (mixed.astype(f32) + mlp_proj).astype(bf16)
    residual_out = lax.dynamic_slice_in_dim(layer_rows, mine, share, 0)
    final = rms_scale(layer_rows, next_gain)
    next_query = jnp.dot(final, query_weight, preferred_element_type=f32).astype(bf16)
    next_keyval = jnp.dot(final, keyval_weight, preferred_element_type=f32).astype(bf16)
    return (attention, residual_out, next_query, next_keyval)


def solution(mesh):
    in_specs = (
        P("req", "tp"),
        P("req", "tp"),
        P("req", None),
        P("req", None, "tp"),
        P("req"),
        P("req", None),
        P("req"),
        P(),
        P(),
        P("req", None, "tp"),
        P("req"),
        P("req"),
        P("tp", None),
        P(),
        P(None, "tp"),
        P(None, "tp"),
        P("tp", None),
        P(),
        P(None, "tp"),
        P(None, "tp"),
    )
    out_specs = (P("req", "tp"), P(("req", "tp"), None), P("req", "tp"), P("req", "tp"))
    return jax.shard_map(
        per_device, mesh=mesh, in_specs=in_specs, out_specs=out_specs, check_vma=False
    )
```

```python
import functools
import math

import jax
import jax.numpy as jnp
from jax import lax
from jax.experimental import pallas as pl
from jax.experimental.pallas import tpu as pltpu
from jax.sharding import PartitionSpec as P

HD = 80
ROOTS = 2
MIDS = 6
LANES = 128
MASKED = -1e30
EPSILON = 1e-05
RATE = math.log2(math.e) / math.sqrt(HD)

bf16 = jnp.bfloat16
f32 = jnp.float32
i32 = jnp.int32
ANY = pl.BlockSpec(memory_space=pl.ANY)
VMEM = pl.BlockSpec(memory_space=pltpu.VMEM)
SMEM = pl.BlockSpec(memory_space=pltpu.SMEM)
PARAMS = pltpu.CompilerParams(vmem_limit_bytes=48 * 1024 * 1024)


def padded(width):
    return -(-width // LANES) * LANES


def key_start(c):
    return c * 2 * HD // LANES * LANES


def key_shift(c):
    return c * 2 * HD % LANES


def value_start(c):
    return (c * 2 * HD + HD) // LANES * LANES


def value_shift(c):
    return (c * 2 * HD + HD) % LANES


def key_window(ref, c):
    first = ref[:, key_start(c) : key_start(c) + LANES]
    last = ref[:, ref.shape[1] - LANES :]
    return jnp.concatenate([first, last], axis=1)


def value_window(ref, c):
    stop = min(value_start(c) + 2 * LANES, ref.shape[1])
    return ref[:, value_start(c) : stop]


def scores_of(query, keys):
    return lax.dot_general(query, keys, (((1,), (1,)), ((), ())), preferred_element_type=f32)


def fetch(pairs, sems):
    copies = [pltpu.make_async_copy(a, b, sems.at[i]) for i, (a, b) in enumerate(pairs)]
    for copy in copies:
        copy.start()
    return copies


def prep_kernel(
    node_hbm, rank_hbm, length_hbm, root_hbm, pool_ref, out_ref, node_ref, rank_ref, length_ref, root_ref, sems
):
    pairs = ((node_hbm, node_ref), (rank_hbm, rank_ref), (length_hbm, length_ref), (root_hbm, root_ref))
    for copy in fetch(pairs, sems):
        copy.wait()
    pages, size, width = pool_ref.shape
    free = out_ref.shape[1] - width
    lane = lax.broadcasted_iota(i32, (size, free), 1)
    slot = lax.broadcasted_iota(i32, (size, free), 0)
    root = jnp.full((size, free), -2, i32)
    for m in range(MIDS):
        root = jnp.where(lane == m, root_ref[m], root)
    hidden = jnp.where(lane < MIDS, MASKED, 0.0)
    for p in range(pages):
        node = node_ref[p]
        left = length_ref[jnp.maximum(node, 0)] - size * rank_ref[p]
        seen = ((root == node) | (lane + ROOTS == node)) & (slot < left)
        rows = slice(p * size, (p + 1) * size)
        out_ref[rows, :width] = pool_ref[p]
        out_ref[rows, width:] = jnp.where(seen, 0.0, hidden).astype(bf16)


def prepare(page_node, page_rank, node_length, mid_root, prefix_pool):
    pages, size, width = prefix_pool.shape
    tables = (page_node, page_rank, node_length, mid_root)
    return pl.pallas_call(
        prep_kernel,
        out_shape=jax.ShapeDtypeStruct((pages * size, padded(width + MIDS)), bf16),
        in_specs=[ANY] * 4 + [VMEM],
        out_specs=VMEM,
        scratch_shapes=[pltpu.SMEM(t.shape, i32) for t in tables] + [pltpu.SemaphoreType.DMA((4,))],
        compiler_params=PARAMS,
        name="pool_rows",
    )(*tables, prefix_pool)


def half_start(rows, half):
    parity = lax.rem(lax.axis_index("tp"), 2)
    return (parity if half else 1 - parity) * (rows // 2)


def fold(scores, values, state):
    top = functools.reduce(jnp.maximum, [jnp.max(s, axis=1, keepdims=True) for s in scores])
    if state is not None:
        top = jnp.maximum(top, state[0])
    total, weighted = None, None
    for s, v in zip(scores, values):
        raised = jnp.exp2((s - top) * RATE)
        part = jnp.sum(raised, axis=1, keepdims=True)
        mixed = jnp.dot(raised.astype(bf16), v, preferred_element_type=f32)
        total = part if total is None else total + part
        weighted = mixed if weighted is None else weighted + mixed
    if state is not None:
        factor = jnp.exp2((state[0] - top) * RATE)
        total = total + state[1] * factor
        weighted = weighted + state[2] * factor
    return top, total, weighted


def pack(top, total, weighted):
    lane = lax.broadcasted_iota(i32, weighted.shape, 1)
    return jnp.where(lane == 0, top, jnp.where(lane == 1, total, weighted))


def unpack(state):
    return state[:, 0:1], state[:, 1:2], state


def local_kernel(
    count_hbm, mid_hbm, leaf_len_hbm, query_ref, keyval_ref, leaf_ref, pool_ref, aug_ref, state_ref,
    count_ref, mid_ref, leaf_len_ref, sems,
):
    pairs = ((count_hbm, count_ref), (mid_hbm, mid_ref), (leaf_len_hbm, leaf_len_ref))
    for copy in fetch(pairs, sems):
        copy.wait()
    rows = query_ref.shape[0]
    part = rows // 2
    width = keyval_ref.shape[1]
    requests, slots, _ = leaf_ref.shape
    kv_local = width // (2 * HD)
    group = query_ref.shape[1] // (kv_local * HD)
    lane = lax.broadcasted_iota(i32, (part, LANES), 1)
    zero = jnp.zeros((part, LANES), i32)
    leaf_all = leaf_ref[...].reshape(requests * slots, width)
    leaf_at = lax.broadcasted_iota(i32, (part, requests * slots), 1)
    for half in range(2):
        first = half_start(rows, half)
        row = lax.broadcasted_iota(i32, (part, LANES), 0) + first
        start, low, high, mid = zero, zero, zero, zero
        begin = jnp.int32(0)
        for r in range(requests):
            here = row >= begin
            start = jnp.where(here, begin, start)
            low = jnp.where(here, r * slots, low)
            high = jnp.where(here, r * slots + leaf_len_ref[r], high)
            mid = jnp.where(here, mid_ref[r], mid)
            begin = begin + count_ref[0, r]
        chosen = jnp.where(lane == width % LANES + mid, 1.0, 0.0).astype(bf16)
        leaf_ok = (leaf_at >= low[:, 0:1]) & (leaf_at < high[:, 0:1])
        new_ok = (lane >= start) & (lane <= row)
        tokens = query_ref[pl.ds(pl.multiple_of(first, part), part), :]
        for c in range(kv_local):
            base = (half * kv_local + c) * group * part
            block = slice(base, base + group * part)
            key0, val0 = key_start(c), value_start(c)
            shift = key_shift(c)
            for g in range(group):
                h = c * group + g
                at = slice(base + g * part, base + (g + 1) * part)
                aug_ref[at, :LANES] = jnp.zeros((part, LANES), bf16)
                aug_ref[at, shift : shift + HD] = tokens[:, h * HD : (h + 1) * HD]
                aug_ref[at, LANES:] = chosen
            query = aug_ref[block, :]
            narrow = query[:, :LANES]
            s_leaf = scores_of(narrow, leaf_all[:, key0 : key0 + LANES])
            s_leaf = jnp.where(leaf_ok[None], s_leaf.reshape(group, part, -1), MASKED)
            s_new = scores_of(narrow, keyval_ref[:, key0 : key0 + LANES])
            s_new = jnp.where(new_ok[None], s_new.reshape(group, part, -1), MASKED)
            scores = [s_leaf.reshape(group * part, -1), s_new.reshape(group * part, -1)]
            stop = min(val0 + 2 * LANES, width)
            fill = val0 + 2 * LANES - stop
            values = [leaf_all[:, val0:stop], keyval_ref[:, val0:stop]]
            if fill:
                values = [
                    jnp.concatenate([v, jnp.zeros((v.shape[0], fill), bf16)], axis=1) for v in values
                ]
            scores.append(scores_of(query, key_window(pool_ref, c)))
            values.append(value_window(pool_ref, c))
            state_ref[block, :] = pack(*fold(scores, values, None))


def start_attention(new_query, new_keyval, leaf, leaf_length, counts, request_mid, pool):
    rows, query_width = new_query.shape
    heads = query_width // HD
    tables = (counts, request_mid, leaf_length)
    keys = leaf.shape[0] * leaf.shape[1] + rows + pool.shape[0]
    return pl.pallas_call(
        local_kernel,
        out_shape=(
            jax.ShapeDtypeStruct((heads * rows, 2 * LANES), bf16),
            jax.ShapeDtypeStruct((heads * rows, 2 * LANES), f32),
        ),
        in_specs=[ANY] * 3 + [VMEM] * 4,
        out_specs=(VMEM, VMEM),
        scratch_shapes=[pltpu.SMEM(t.shape, i32) for t in tables] + [pltpu.SemaphoreType.DMA((3,))],
        compiler_params=PARAMS,
        cost_estimate=attention_cost(heads * rows, keys),
        name="attend_local",
    )(*tables, new_query, new_keyval, leaf, pool)


def attention_cost(rows, keys):
    return pl.CostEstimate(
        flops=8 * LANES * rows * keys, bytes_accessed=8 * rows * 2 * LANES, transcendentals=rows * keys
    )


def extended(query, state, pool_refs, c):
    scores = [scores_of(query, key_window(ref, c)) for ref in pool_refs]
    values = [value_window(ref, c) for ref in pool_refs]
    return fold(scores, values, unpack(state))


def chunk_kernel(*refs, blocks):
    aug_ref, state_ref = refs[:2]
    pool_refs, out_ref = refs[2:-1], refs[-1]
    size = aug_ref.shape[0] // blocks
    for b in range(blocks):
        at = slice(b * size, (b + 1) * size)
        state = extended(aug_ref[at, :], state_ref[at, :], pool_refs, b % (blocks // 2))
        out_ref[at, :] = pack(*state)


def extend_attention(aug, state, pools, kv_local):
    keys = sum(item.shape[0] for item in pools)
    return pl.pallas_call(
        functools.partial(chunk_kernel, blocks=2 * kv_local),
        out_shape=jax.ShapeDtypeStruct(state.shape, f32),
        in_specs=[VMEM] * (2 + len(pools)),
        out_specs=VMEM,
        compiler_params=PARAMS,
        cost_estimate=attention_cost(aug.shape[0], keys),
        name="attend_pages",
    )(aug, state, *pools)


def finish_kernel(*refs, half, kv_local, chunks, width):
    aug_ref, state_ref = refs[:2]
    pool_refs = refs[2 : 2 + chunks]
    weight_hbm = refs[2 + chunks]
    part = aug_ref.shape[0] // (2 * width // HD)
    rest = refs[3 + chunks :]
    if half:
        other_ref, att_ref, proj_ref, weight_ref, mine_ref, sem = rest
    else:
        att_ref, proj_ref, weight_ref, mine_ref, sem = rest
    copy = pltpu.make_async_copy(weight_hbm, weight_ref, sem)
    copy.start()
    group = width // (kv_local * HD)
    size = group * part
    for c in range(kv_local):
        at = slice((half * kv_local + c) * size, (half * kv_local + c + 1) * size)
        if chunks:
            state = extended(aug_ref[at, :], state_ref[at, :], pool_refs, c)
        else:
            state = unpack(state_ref[at, :])
        shift = value_shift(c)
        result = (state[2][:, shift : shift + HD] / state[1]).astype(bf16)
        for g in range(group):
            h = c * group + g
            mine_ref[:, h * HD : (h + 1) * HD] = result[g * part : (g + 1) * part]
    if half:
        mine = pl.multiple_of(half_start(2 * part, 1), part)
        theirs = pl.multiple_of(half_start(2 * part, 0), part)
        att_ref[pl.ds(mine, part), :] = mine_ref[...]
        att_ref[pl.ds(theirs, part), :] = other_ref[...]
    else:
        att_ref[...] = mine_ref[...]
    copy.wait()
    proj = jnp.dot(mine_ref[...], weight_ref[...], preferred_element_type=f32)
    proj_ref[...] = proj.astype(proj_ref.dtype)


def finish_attention(aug, state, pools, out_weight, half, kv_local, rows, other):
    width = out_weight.shape[0]
    part = rows // 2
    keys = sum(item.shape[0] for item in pools)
    return pl.pallas_call(
        functools.partial(
            finish_kernel, half=half, kv_local=kv_local, chunks=len(pools), width=width
        ),
        out_shape=(
            jax.ShapeDtypeStruct((rows if half else part, width), bf16),
            jax.ShapeDtypeStruct((part, out_weight.shape[1]), f32 if half else bf16),
        ),
        in_specs=[VMEM] * (2 + len(pools)) + [ANY] + [VMEM] * half,
        out_specs=(VMEM, VMEM),
        scratch_shapes=[
            pltpu.VMEM(out_weight.shape, bf16),
            pltpu.VMEM((part, width), bf16),
            pltpu.SemaphoreType.DMA,
        ],
        compiler_params=PARAMS,
        cost_estimate=attention_cost(aug.shape[0] // 2, keys + 512),
        name="attend_finish",
    )(aug, state, *pools, out_weight, *other)


def normalized(values_in, gain):
    values = values_in.astype(f32)
    scale = lax.rsqrt(jnp.mean(values * values, axis=-1, keepdims=True) + EPSILON)
    return (values * scale * gain.astype(f32)).astype(bf16)


def block_width(width):
    return LANES if width % LANES == 0 else width


def mlp_kernel(rows_ref, gain_ref, gate_ref, up_ref, down_ref, out_ref, normed_ref, sum_ref):
    step = pl.program_id(0)

    @pl.when(step == 0)
    def _():
        normed_ref[...] = normalized(rows_ref[...], gain_ref[...])
        sum_ref[...] = jnp.zeros_like(sum_ref)

    normed = normed_ref[...]
    gate = jnp.dot(normed, gate_ref[...], preferred_element_type=f32)
    upward = jnp.dot(normed, up_ref[...], preferred_element_type=f32)
    hidden = (jax.nn.silu(gate) * upward).astype(bf16)
    sum_ref[...] += jnp.dot(hidden, down_ref[...], preferred_element_type=f32)

    @pl.when(step == pl.num_programs(0) - 1)
    def _():
        out_ref[...] = sum_ref[...].astype(out_ref.dtype)


def feed_forward(rows, gain, gate_weight, up_weight, down_weight, dtype):
    count, depth = rows.shape
    width = gate_weight.shape[1]
    step = block_width(width)
    return pl.pallas_call(
        mlp_kernel,
        out_shape=jax.ShapeDtypeStruct((count, depth), dtype),
        grid=(width // step,),
        in_specs=[
            pl.BlockSpec((count, depth), lambda i: (0, 0)),
            pl.BlockSpec((1, depth), lambda i: (0, 0)),
            pl.BlockSpec((depth, step), lambda i: (0, i)),
            pl.BlockSpec((depth, step), lambda i: (0, i)),
            pl.BlockSpec((step, depth), lambda i: (i, 0)),
        ],
        out_specs=pl.BlockSpec((count, depth), lambda i: (0, 0)),
        scratch_shapes=[pltpu.VMEM((count, depth), bf16), pltpu.VMEM((count, depth), f32)],
        compiler_params=PARAMS,
        cost_estimate=pl.CostEstimate(
            flops=6 * count * depth * width, bytes_accessed=6 * depth * width, transcendentals=0
        ),
        name="feed_forward",
    )(rows, gain.reshape(1, depth), gate_weight, up_weight, down_weight)


def next_kernel(rows_ref, gain_ref, query_ref, keyval_ref, *refs, half):
    if half:
        query_in, keyval_in, query_out, keyval_out, normed_ref, query_sum, keyval_sum = refs
    else:
        query_out, keyval_out, normed_ref, query_sum, keyval_sum = refs
    step = pl.program_id(0)
    depth = query_ref.shape[0]

    @pl.when(step == 0)
    def _():
        normed = normalized(rows_ref[...], gain_ref[...])
        for k in range(normed_ref.shape[0]):
            normed_ref[k] = normed[:, k * depth : (k + 1) * depth]
        query_sum[...] = jnp.zeros_like(query_sum)
        keyval_sum[...] = jnp.zeros_like(keyval_sum)

    normed = normed_ref[step]
    query_sum[...] += jnp.dot(normed, query_ref[...], preferred_element_type=f32)
    keyval_sum[...] += jnp.dot(normed, keyval_ref[...], preferred_element_type=f32)

    @pl.when(step == pl.num_programs(0) - 1)
    def _():
        query, keyval = query_sum[...].astype(bf16), keyval_sum[...].astype(bf16)
        if half:
            part = query.shape[0]
            mine = pl.multiple_of(half_start(2 * part, 1), part)
            theirs = pl.multiple_of(half_start(2 * part, 0), part)
            query_out[pl.ds(mine, part), :] = query
            query_out[pl.ds(theirs, part), :] = query_in[...]
            keyval_out[pl.ds(mine, part), :] = keyval
            keyval_out[pl.ds(theirs, part), :] = keyval_in[...]
        else:
            query_out[...] = query
            keyval_out[...] = keyval


def next_projections(rows, gain, query_weight, keyval_weight, other):
    count, depth = rows.shape
    steps = 5
    block = depth // steps
    widths = (query_weight.shape[1], keyval_weight.shape[1])
    half = len(other) > 0
    out_rows = 2 * count if half else count
    return pl.pallas_call(
        functools.partial(next_kernel, half=half),
        out_shape=tuple(jax.ShapeDtypeStruct((out_rows, w), bf16) for w in widths),
        grid=(steps,),
        in_specs=[
            pl.BlockSpec((count, depth), lambda i: (0, 0)),
            pl.BlockSpec((1, depth), lambda i: (0, 0)),
        ]
        + [pl.BlockSpec((block, w), lambda i: (i, 0)) for w in widths]
        + [pl.BlockSpec(item.shape, lambda i: (0, 0)) for item in other],
        out_specs=tuple(pl.BlockSpec((out_rows, w), lambda i: (0, 0)) for w in widths),
        scratch_shapes=[pltpu.VMEM((steps, count, block), bf16)]
        + [pltpu.VMEM((count, w), f32) for w in widths],
        compiler_params=PARAMS,
        cost_estimate=pl.CostEstimate(
            flops=2 * count * depth * sum(widths),
            bytes_accessed=2 * depth * sum(widths),
            transcendentals=0,
        ),
        name="next_layer",
    )(rows, gain.reshape(1, depth), query_weight, keyval_weight, *other)


def trade(value, axis, bit):
    size = lax.axis_size(axis)
    return lax.ppermute(value, axis, [(i, i ^ bit) for i in range(size)])


def cross(value, even_bit, odd_bit):
    size = lax.axis_size("req")
    pairs = [(i, i ^ (odd_bit if i % 2 else even_bit)) for i in range(size)]
    return lax.ppermute(value, "req", pairs)


def wide(value):
    return value.astype(f32)


def per_device(
    new_query,
    new_keyval,
    residual_in,
    leaf_cache,
    leaf_length,
    new_counts,
    request_mid,
    mid_root,
    node_length,
    prefix_pool,
    page_node,
    page_rank,
    out_weight,
    norm_gain,
    gate_weight,
    up_weight,
    down_weight,
    next_gain,
    query_weight,
    keyval_weight,
):
    rows = new_query.shape[0]
    part = rows // 2
    kv_local = new_keyval.shape[1] // (2 * HD)
    pool = prepare(page_node, page_rank, node_length, mid_root, prefix_pool)
    local_args = (new_query, new_keyval, leaf_cache, leaf_length, new_counts, request_mid, pool)
    if lax.axis_size("req") == 8:
        first = cross(pool, 2, 4)
        second = cross(pool, 4, 2)
        beside = trade(pool, "req", 1)
        aug, state = start_attention(*local_args)
        corner = cross(first, 4, 2)
        first_other = trade(first, "req", 1)
        second_other = trade(second, "req", 1)
        state = extend_attention(aug, state, [beside, first, second], kv_local)
        state = extend_attention(aug, state, [first_other, second_other], kv_local)
        corner_other = trade(corner, "req", 1)
        state = extend_attention(aug, state, [corner], kv_local)
        pools = [corner_other]
    else:
        every = lax.all_gather(pool, "req", axis=0)
        holders = every.shape[0]
        aug, state = start_attention(*local_args)
        places = (lax.axis_index("req") + 1 + jnp.arange(holders - 1)) % holders
        step = 4
        for i in range(0, holders - 1, step):
            chunk = every[places[i : i + step]].reshape(-1, pool.shape[1])
            state = extend_attention(aug, state, [chunk], kv_local)
        pools = []

    theirs_att, theirs_proj = finish_attention(
        aug, state, pools, out_weight, 0, kv_local, rows, ()
    )
    attention, mine_proj = finish_attention(
        aug, state, pools, out_weight, 1, kv_local, rows, (theirs_att,)
    )

    mine = half_start(rows, 1)
    theirs = half_start(rows, 0)
    share = rows // lax.axis_size("tp")
    place = lax.axis_index("tp") * share
    res_mine = lax.dynamic_slice_in_dim(residual_in, mine, part, 0)
    if lax.axis_size("tp") == 4:
        got = trade(theirs_proj, "tp", 1)
        pair = (mine_proj + wide(got)).astype(bf16)
        got = trade(pair, "tp", 2)
        mixed_mine = (wide(res_mine) + (wide(pair) + wide(got))).astype(bf16)
        mixed_theirs = trade(mixed_mine, "tp", 1)
        mlp = (norm_gain, gate_weight, up_weight, down_weight)
        mlp_mine = feed_forward(mixed_mine, *mlp, bf16)
        got = trade(mlp_mine, "tp", 1)
        mlp_theirs = feed_forward(mixed_theirs, *mlp, f32)
        pair = (mlp_theirs + wide(got)).astype(bf16)
        got = trade(pair, "tp", 2)
        layer_theirs = (wide(mixed_theirs) + (wide(pair) + wide(got))).astype(bf16)
        layer_mine = trade(layer_theirs, "tp", 1)
    else:
        res_theirs = lax.dynamic_slice_in_dim(residual_in, theirs, part, 0)
        order = jnp.where(mine == 0, 1, 0)

        def in_order(theirs_part, mine_part):
            both = jnp.stack([theirs_part, mine_part])
            return jnp.where(order == 1, both[::-1], both).reshape(rows, -1)

        total = lax.psum(in_order(wide(theirs_proj), mine_proj), "tp")
        mixed = (wide(in_order(res_theirs, res_mine)) + total).astype(bf16)
        mlp = feed_forward(mixed, norm_gain, gate_weight, up_weight, down_weight, f32)
        layer = (wide(mixed) + lax.psum(mlp, "tp")).astype(bf16)
        layer_mine = lax.dynamic_slice_in_dim(layer, mine, part, 0)
        layer_theirs = lax.dynamic_slice_in_dim(layer, theirs, part, 0)
    weights = (next_gain, query_weight, keyval_weight)
    other = next_projections(layer_theirs, *weights, ())
    next_query, next_keyval = next_projections(layer_mine, *weights, other)
    at = lax.rem(place, part)
    held = (place >= mine) & (place < mine + part)
    residual_out = jnp.where(
        held,
        lax.dynamic_slice_in_dim(layer_mine, at, share, 0),
        lax.dynamic_slice_in_dim(layer_theirs, at, share, 0),
    )
    return (attention, residual_out, next_query, next_keyval)


def solution(mesh):
    in_specs = (
        P("req", "tp"),
        P("req", "tp"),
        P("req", None),
        P("req", None, "tp"),
        P("req"),
        P("req", None),
        P("req"),
        P(),
        P(),
        P("req", None, "tp"),
        P("req"),
        P("req"),
        P("tp", None),
        P(),
        P(None, "tp"),
        P(None, "tp"),
        P("tp", None),
        P(),
        P(None, "tp"),
        P(None, "tp"),
    )
    out_specs = (P("req", "tp"), P(("req", "tp"), None), P("req", "tp"), P("req", "tp"))
    return jax.shard_map(
        per_device, mesh=mesh, in_specs=in_specs, out_specs=out_specs, check_vma=False
    )
```

```python
import functools
import math

import jax
import jax.numpy as jnp
from jax import lax
from jax.experimental import pallas as pl
from jax.experimental.pallas import tpu as pltpu
from jax.sharding import PartitionSpec as P

HD = 80
ROOTS = 2
MIDS = 6
LANES = 128
MASKED = -1e30
EPSILON = 1e-05
RATE = math.log2(math.e) / math.sqrt(HD)

bf16 = jnp.bfloat16
f32 = jnp.float32
i32 = jnp.int32
HBM = pl.BlockSpec(memory_space=pltpu.HBM)
VMEM = pl.BlockSpec(memory_space=pltpu.VMEM)
SMEM = pl.BlockSpec(memory_space=pltpu.SMEM)
PARAMS = pltpu.CompilerParams(vmem_limit_bytes=24 * 1024 * 1024)


def padded(width):
    return -(-width // LANES) * LANES


def key_start(c):
    return c * 2 * HD // LANES * LANES


def key_shift(c):
    return c * 2 * HD % LANES


def value_start(c):
    return (c * 2 * HD + HD) // LANES * LANES


def value_shift(c):
    return (c * 2 * HD + HD) % LANES


def key_window(ref, c):
    first = ref[:, key_start(c) : key_start(c) + LANES]
    last = ref[:, ref.shape[1] - LANES :]
    return jnp.concatenate([first, last], axis=1)


def value_window(ref, c):
    stop = min(value_start(c) + 2 * LANES, ref.shape[1])
    return ref[:, value_start(c) : stop]


def scores_of(query, keys):
    return lax.dot_general(query, keys, (((1,), (1,)), ((), ())), preferred_element_type=f32)


def fetch(pairs, sems):
    copies = [pltpu.make_async_copy(a, b, sems.at[i]) for i, (a, b) in enumerate(pairs)]
    for copy in copies:
        copy.start()
    return copies


def in_hbm(values):
    return [pltpu.with_memory_space_constraint(value, pltpu.HBM) for value in values]


def in_vmem(values):
    return [pltpu.with_memory_space_constraint(value, pltpu.VMEM) for value in values]


def prep_kernel(
    node_hbm, rank_hbm, length_hbm, root_hbm, pool_ref, out_ref, node_ref, rank_ref, length_ref, root_ref, sems
):
    pairs = ((node_hbm, node_ref), (rank_hbm, rank_ref), (length_hbm, length_ref), (root_hbm, root_ref))
    for copy in fetch(pairs, sems):
        copy.wait()
    pages, size, width = pool_ref.shape
    free = out_ref.shape[1] - width
    lane = lax.broadcasted_iota(i32, (size, free), 1)
    slot = lax.broadcasted_iota(i32, (size, free), 0)
    root = jnp.full((size, free), -2, i32)
    for m in range(MIDS):
        root = jnp.where(lane == m, root_ref[m], root)
    hidden = jnp.where(lane < MIDS, MASKED, 0.0)
    for p in range(pages):
        node = node_ref[p]
        left = length_ref[jnp.maximum(node, 0)] - size * rank_ref[p]
        seen = ((root == node) | (lane + ROOTS == node)) & (slot < left)
        rows = slice(p * size, (p + 1) * size)
        out_ref[rows, :width] = pool_ref[p]
        out_ref[rows, width:] = jnp.where(seen, 0.0, hidden).astype(bf16)


def prepare(page_node, page_rank, node_length, mid_root, prefix_pool):
    pages, size, width = prefix_pool.shape
    tables = (page_node, page_rank, node_length, mid_root)
    return pl.pallas_call(
        prep_kernel,
        out_shape=jax.ShapeDtypeStruct((pages * size, padded(width + MIDS)), bf16),
        in_specs=[HBM] * 4 + [VMEM],
        out_specs=VMEM,
        scratch_shapes=[pltpu.SMEM(t.shape, i32) for t in tables] + [pltpu.SemaphoreType.DMA((4,))],
        compiler_params=PARAMS,
        name="pool_rows",
    )(*in_hbm(tables), prefix_pool)


def half_start(rows, half):
    parity = lax.rem(lax.axis_index("tp"), 2)
    return (parity if half else 1 - parity) * (rows // 2)


def fold(scores, values, state):
    top = functools.reduce(jnp.maximum, [jnp.max(s, axis=1, keepdims=True) for s in scores])
    if state is not None:
        top = jnp.maximum(top, state[0])
    total, weighted = None, None
    for s, v in zip(scores, values):
        raised = jnp.exp2((s - top) * RATE)
        part = jnp.sum(raised, axis=1, keepdims=True)
        mixed = jnp.dot(raised.astype(bf16), v, preferred_element_type=f32)
        total = part if total is None else total + part
        weighted = mixed if weighted is None else weighted + mixed
    if state is not None:
        factor = jnp.exp2((state[0] - top) * RATE)
        total = total + state[1] * factor
        weighted = weighted + state[2] * factor
    return top, total, weighted


def pack(top, total, weighted):
    lane = lax.broadcasted_iota(i32, weighted.shape, 1)
    return jnp.where(lane == 0, top, jnp.where(lane == 1, total, weighted))


def unpack(state):
    return state[:, 0:1], state[:, 1:2], state


def local_kernel(
    count_hbm, mid_hbm, leaf_len_hbm, query_ref, keyval_ref, leaf_ref, *refs, chunks
):
    pool_refs = refs[:chunks]
    aug_ref, state_ref, count_ref, mid_ref, leaf_len_ref, sems = refs[chunks:]
    pairs = ((count_hbm, count_ref), (mid_hbm, mid_ref), (leaf_len_hbm, leaf_len_ref))
    for copy in fetch(pairs, sems):
        copy.wait()
    rows = query_ref.shape[0]
    part = rows // 2
    width = keyval_ref.shape[1]
    requests, slots, _ = leaf_ref.shape
    kv_local = width // (2 * HD)
    group = query_ref.shape[1] // (kv_local * HD)
    lane = lax.broadcasted_iota(i32, (part, LANES), 1)
    zero = jnp.zeros((part, LANES), i32)
    leaf_all = leaf_ref[...].reshape(requests * slots, width)
    leaf_at = lax.broadcasted_iota(i32, (part, requests * slots), 1)
    for half in range(2):
        first = half_start(rows, half)
        row = lax.broadcasted_iota(i32, (part, LANES), 0) + first
        start, low, high, mid = zero, zero, zero, zero
        begin = jnp.int32(0)
        for r in range(requests):
            here = row >= begin
            start = jnp.where(here, begin, start)
            low = jnp.where(here, r * slots, low)
            high = jnp.where(here, r * slots + leaf_len_ref[r], high)
            mid = jnp.where(here, mid_ref[r], mid)
            begin = begin + count_ref[0, r]
        chosen = jnp.where(lane == width % LANES + mid, 1.0, 0.0).astype(bf16)
        leaf_ok = (leaf_at >= low[:, 0:1]) & (leaf_at < high[:, 0:1])
        new_ok = (lane >= start) & (lane <= row)
        tokens = query_ref[pl.ds(pl.multiple_of(first, part), part), :]
        for c in range(kv_local):
            base = (half * kv_local + c) * group * part
            block = slice(base, base + group * part)
            key0, val0 = key_start(c), value_start(c)
            shift = key_shift(c)
            for g in range(group):
                h = c * group + g
                at = slice(base + g * part, base + (g + 1) * part)
                aug_ref[at, :LANES] = jnp.zeros((part, LANES), bf16)
                aug_ref[at, shift : shift + HD] = tokens[:, h * HD : (h + 1) * HD]
                aug_ref[at, LANES:] = chosen
            query = aug_ref[block, :]
            narrow = query[:, :LANES]
            s_leaf = scores_of(narrow, leaf_all[:, key0 : key0 + LANES])
            s_leaf = jnp.where(leaf_ok[None], s_leaf.reshape(group, part, -1), MASKED)
            s_new = scores_of(narrow, keyval_ref[:, key0 : key0 + LANES])
            s_new = jnp.where(new_ok[None], s_new.reshape(group, part, -1), MASKED)
            scores = [s_leaf.reshape(group * part, -1), s_new.reshape(group * part, -1)]
            stop = min(val0 + 2 * LANES, width)
            fill = val0 + 2 * LANES - stop
            values = [leaf_all[:, val0:stop], keyval_ref[:, val0:stop]]
            if fill:
                values = [
                    jnp.concatenate([v, jnp.zeros((v.shape[0], fill), bf16)], axis=1) for v in values
                ]
            for pool_ref in pool_refs:
                scores.append(scores_of(query, key_window(pool_ref, c)))
                values.append(value_window(pool_ref, c))
            state_ref[block, :] = pack(*fold(scores, values, None))


def start_attention(new_query, new_keyval, leaf, leaf_length, counts, request_mid, pools):
    rows, query_width = new_query.shape
    heads = query_width // HD
    tables = (counts, request_mid, leaf_length)
    keys = leaf.shape[0] * leaf.shape[1] + rows + sum(item.shape[0] for item in pools)
    return pl.pallas_call(
        functools.partial(local_kernel, chunks=len(pools)),
        out_shape=(
            jax.ShapeDtypeStruct((heads * rows, 2 * LANES), bf16),
            jax.ShapeDtypeStruct((heads * rows, 2 * LANES), f32),
        ),
        in_specs=[HBM] * 3 + [VMEM] * (3 + len(pools)),
        out_specs=(VMEM, VMEM),
        scratch_shapes=[pltpu.SMEM(t.shape, i32) for t in tables] + [pltpu.SemaphoreType.DMA((3,))],
        compiler_params=PARAMS,
        cost_estimate=attention_cost(heads * rows, keys),
        name="attend_local",
    )(*in_hbm(tables), new_query, new_keyval, leaf, *pools)


def attention_cost(rows, keys):
    return pl.CostEstimate(
        flops=8 * LANES * rows * keys, bytes_accessed=8 * rows * 2 * LANES, transcendentals=rows * keys
    )


def extended(query, state, pool_refs, c):
    scores = [scores_of(query, key_window(ref, c)) for ref in pool_refs]
    values = [value_window(ref, c) for ref in pool_refs]
    return fold(scores, values, unpack(state))


def chunk_kernel(*refs, blocks):
    aug_ref, state_ref = refs[:2]
    pool_refs, out_ref = refs[2:-1], refs[-1]
    size = aug_ref.shape[0] // blocks
    for b in range(blocks):
        at = slice(b * size, (b + 1) * size)
        state = extended(aug_ref[at, :], state_ref[at, :], pool_refs, b % (blocks // 2))
        out_ref[at, :] = pack(*state)


def extend_attention(aug, state, pools, kv_local):
    keys = sum(item.shape[0] for item in pools)
    return pl.pallas_call(
        functools.partial(chunk_kernel, blocks=2 * kv_local),
        out_shape=jax.ShapeDtypeStruct(state.shape, f32),
        in_specs=[VMEM] * (2 + len(pools)),
        out_specs=VMEM,
        compiler_params=PARAMS,
        cost_estimate=attention_cost(aug.shape[0], keys),
        name="attend_pages",
    )(aug, state, *pools)


def finish_kernel(*refs, half, kv_local, chunks, width):
    aug_ref, state_ref = refs[:2]
    pool_refs = refs[2 : 2 + chunks]
    weight_ref = refs[2 + chunks]
    part = aug_ref.shape[0] // (2 * width // HD)
    rest = refs[3 + chunks :]
    if half:
        other_ref, att_ref, proj_ref, mine_ref = rest
    else:
        att_ref, proj_ref, mine_ref = rest
    group = width // (kv_local * HD)
    size = group * part
    for c in range(kv_local):
        at = slice((half * kv_local + c) * size, (half * kv_local + c + 1) * size)
        if chunks:
            state = extended(aug_ref[at, :], state_ref[at, :], pool_refs, c)
        else:
            state = unpack(state_ref[at, :])
        shift = value_shift(c)
        result = (state[2][:, shift : shift + HD] / state[1]).astype(bf16)
        for g in range(group):
            h = c * group + g
            mine_ref[:, h * HD : (h + 1) * HD] = result[g * part : (g + 1) * part]
    if half:
        mine = pl.multiple_of(half_start(2 * part, 1), part)
        theirs = pl.multiple_of(half_start(2 * part, 0), part)
        att_ref[pl.ds(mine, part), :] = mine_ref[...]
        att_ref[pl.ds(theirs, part), :] = other_ref[...]
    else:
        att_ref[...] = mine_ref[...]
    proj = jnp.dot(mine_ref[...], weight_ref[...], preferred_element_type=f32)
    proj_ref[...] = proj.astype(proj_ref.dtype)


def finish_attention(aug, state, pools, out_weight, half, kv_local, rows, other):
    width = out_weight.shape[0]
    part = rows // 2
    keys = sum(item.shape[0] for item in pools)
    return pl.pallas_call(
        functools.partial(
            finish_kernel, half=half, kv_local=kv_local, chunks=len(pools), width=width
        ),
        out_shape=(
            jax.ShapeDtypeStruct((rows if half else part, width), bf16),
            jax.ShapeDtypeStruct((part, out_weight.shape[1]), f32 if half else bf16),
        ),
        in_specs=[VMEM] * (3 + len(pools) + half),
        out_specs=(VMEM, VMEM),
        scratch_shapes=[pltpu.VMEM((part, width), bf16)],
        compiler_params=PARAMS,
        cost_estimate=attention_cost(aug.shape[0] // 2, keys + 512),
        name="attend_finish",
    )(aug, state, *pools, out_weight, *other)


def normalized(values_in, gain):
    values = values_in.astype(f32)
    scale = lax.rsqrt(jnp.mean(values * values, axis=-1, keepdims=True) + EPSILON)
    return (values * scale * gain.astype(f32)).astype(bf16)


def stage_kernel(*refs):
    count = len(refs) // 2
    for copy in fetch(zip(refs[:count], refs[count : 2 * count]), refs[-1]):
        copy.wait()


def stage(weights):
    return pl.pallas_call(
        stage_kernel,
        out_shape=tuple(pltpu.VMEM(w.shape, w.dtype) for w in weights),
        in_specs=[HBM] * len(weights),
        out_specs=(VMEM,) * len(weights),
        scratch_shapes=[pltpu.SemaphoreType.DMA((len(weights),))],
        compiler_params=pltpu.CompilerParams(vmem_limit_bytes=1024 * 1024),
        cost_estimate=pl.CostEstimate(
            flops=0, bytes_accessed=sum(2 * w.size for w in weights), transcendentals=0
        ),
        name="stage",
    )(*in_hbm(weights))


def mlp_kernel(rows_ref, gain_ref, gate_ref, up_ref, down_ref, out_ref):
    normed = normalized(rows_ref[...], gain_ref[...])
    gate = jnp.dot(normed, gate_ref[...], preferred_element_type=f32)
    upward = jnp.dot(normed, up_ref[...], preferred_element_type=f32)
    hidden = (jax.nn.silu(gate) * upward).astype(bf16)
    out_ref[...] = jnp.dot(hidden, down_ref[...], preferred_element_type=f32).astype(out_ref.dtype)


def feed_forward(rows, gain, gate_weight, up_weight, down_weight, dtype):
    count, depth = rows.shape
    width = gate_weight.shape[1]
    return pl.pallas_call(
        mlp_kernel,
        out_shape=jax.ShapeDtypeStruct((count, depth), dtype),
        in_specs=[VMEM] * 5,
        out_specs=VMEM,
        compiler_params=PARAMS,
        cost_estimate=pl.CostEstimate(
            flops=6 * count * depth * width, bytes_accessed=6 * depth * width, transcendentals=0
        ),
        name="feed_forward",
    )(rows, gain.reshape(1, depth), *in_vmem((gate_weight, up_weight, down_weight)))


def next_kernel(rows_ref, gain_ref, query_ref, keyval_hbm, *refs):
    refs, (keyval_ref, sem) = refs[:-2], refs[-2:]
    copy = pltpu.make_async_copy(keyval_hbm, keyval_ref, sem)
    copy.start()
    normed = normalized(rows_ref[...], gain_ref[...])
    query = jnp.dot(normed, query_ref[...], preferred_element_type=f32).astype(bf16)
    copy.wait()
    keyval = scores_of(keyval_ref[...], normed).astype(bf16)
    if len(refs) == 2:
        query_out, keyval_out = refs
        query_out[...] = query
        keyval_out[...] = keyval
        return
    query_in, keyval_in, query_out, keyval_out = refs
    part = query.shape[0]
    mine = pl.multiple_of(half_start(2 * part, 1), part)
    theirs = pl.multiple_of(half_start(2 * part, 0), part)
    query_out[pl.ds(mine, part), :] = query
    query_out[pl.ds(theirs, part), :] = query_in[...]

    @pl.when(mine == 0)
    def _():
        keyval_out[:, :part] = keyval
        keyval_out[:, part:] = keyval_in[...]

    @pl.when(mine != 0)
    def _():
        keyval_out[:, :part] = keyval_in[...]
        keyval_out[:, part:] = keyval


def next_projections(rows, gain, query_weight, keyval_weight, other):
    count, depth = rows.shape
    widths = (query_weight.shape[1], keyval_weight.shape[0])
    out_rows = 2 * count if other else count
    return pl.pallas_call(
        next_kernel,
        out_shape=(
            jax.ShapeDtypeStruct((out_rows, widths[0]), bf16),
            jax.ShapeDtypeStruct((widths[1], out_rows), bf16),
        ),
        in_specs=[VMEM] * 3 + [HBM] + [VMEM] * len(other),
        out_specs=(VMEM, VMEM),
        scratch_shapes=[pltpu.VMEM(keyval_weight.shape, bf16), pltpu.SemaphoreType.DMA],
        compiler_params=PARAMS,
        cost_estimate=pl.CostEstimate(
            flops=2 * count * depth * sum(widths),
            bytes_accessed=2 * depth * sum(widths),
            transcendentals=0,
        ),
        name="next_layer",
    )(rows, gain.reshape(1, depth), *in_vmem([query_weight]), *in_hbm([keyval_weight]), *other)


def trade(value, axis, bit):
    size = lax.axis_size(axis)
    return lax.ppermute(value, axis, [(i, i ^ bit) for i in range(size)])


def cross(value, even_bit, odd_bit):
    size = lax.axis_size("req")
    pairs = [(i, i ^ (odd_bit if i % 2 else even_bit)) for i in range(size)]
    return lax.ppermute(value, "req", pairs)


def wide(value):
    return value.astype(f32)


def per_device(
    new_query,
    new_keyval,
    residual_in,
    leaf_cache,
    leaf_length,
    new_counts,
    request_mid,
    mid_root,
    node_length,
    prefix_pool,
    page_node,
    page_rank,
    out_weight,
    norm_gain,
    gate_weight,
    up_weight,
    down_weight,
    next_gain,
    query_weight,
    keyval_weight,
):
    rows = new_query.shape[0]
    part = rows // 2
    kv_local = new_keyval.shape[1] // (2 * HD)
    pool = prepare(page_node, page_rank, node_length, mid_root, prefix_pool)
    local_args = (new_query, new_keyval, leaf_cache, leaf_length, new_counts, request_mid)
    if lax.axis_size("req") == 8:
        first = cross(pool, 2, 4)
        second = cross(pool, 4, 2)
        beside = trade(pool, "req", 1)
        aug, state = start_attention(*local_args, [pool, beside])
        first, second, aug, state = lax.optimization_barrier((first, second, aug, state))
        corner = cross(first, 4, 2)
        first_other = trade(first, "req", 1)
        second_other = trade(second, "req", 1)
        near = [first, second, first_other, second_other]
        state = extend_attention(aug, state, near, kv_local)
        corner, aug, state = lax.optimization_barrier((corner, aug, state))
        pools = [corner, trade(corner, "req", 1)]
    else:
        every = lax.all_gather(pool, "req", axis=0)
        holders = every.shape[0]
        aug, state = start_attention(*local_args, [pool])
        places = (lax.axis_index("req") + 1 + jnp.arange(holders - 1)) % holders
        step = 4
        for i in range(0, holders - 1, step):
            chunk = every[places[i : i + step]].reshape(-1, pool.shape[1])
            state = extend_attention(aug, state, [chunk], kv_local)
        pools = []

    theirs_att, theirs_proj = finish_attention(
        aug, state, pools, out_weight, 0, kv_local, rows, ()
    )
    attention, mine_proj = finish_attention(
        aug, state, pools, out_weight, 1, kv_local, rows, (theirs_att,)
    )

    mine = half_start(rows, 1)
    theirs = half_start(rows, 0)
    share = rows // lax.axis_size("tp")
    place = lax.axis_index("tp") * share
    res_mine = lax.dynamic_slice_in_dim(residual_in, mine, part, 0)
    if lax.axis_size("tp") == 4:
        got = trade(theirs_proj, "tp", 1)
        pair = (mine_proj + wide(got)).astype(bf16)
        pair, *mlp = lax.optimization_barrier((pair, gate_weight, up_weight, down_weight))
        got = trade(pair, "tp", 2)
        got, *mlp = lax.optimization_barrier((got, *stage(mlp)))
        mixed_mine = (wide(res_mine) + (wide(pair) + wide(got))).astype(bf16)
        mixed_theirs = trade(mixed_mine, "tp", 1)
        mlp_mine = feed_forward(mixed_mine, norm_gain, *mlp, bf16)
        got = trade(mlp_mine, "tp", 1)
        mlp_theirs = feed_forward(mixed_theirs, norm_gain, *mlp, f32)
        pair = (mlp_theirs + wide(got)).astype(bf16)
        pair, query_weight = lax.optimization_barrier((pair, query_weight))
        got = trade(pair, "tp", 2)
        got, query_weight = lax.optimization_barrier((got, *stage([query_weight])))
        layer_theirs = (wide(mixed_theirs) + (wide(pair) + wide(got))).astype(bf16)
        layer_mine = trade(layer_theirs, "tp", 1)
    else:
        res_theirs = lax.dynamic_slice_in_dim(residual_in, theirs, part, 0)
        order = jnp.where(mine == 0, 1, 0)

        def in_order(theirs_part, mine_part):
            both = jnp.stack([theirs_part, mine_part])
            return jnp.where(order == 1, both[::-1], both).reshape(rows, -1)

        total = lax.psum(in_order(wide(theirs_proj), mine_proj), "tp")
        mixed = (wide(in_order(res_theirs, res_mine)) + total).astype(bf16)
        mlp = feed_forward(mixed, norm_gain, gate_weight, up_weight, down_weight, f32)
        layer = (wide(mixed) + lax.psum(mlp, "tp")).astype(bf16)
        layer_mine = lax.dynamic_slice_in_dim(layer, mine, part, 0)
        layer_theirs = lax.dynamic_slice_in_dim(layer, theirs, part, 0)
    weights = [next_gain, query_weight, keyval_weight.T]
    other = next_projections(layer_theirs, *weights, ())
    next_query, next_keyval = next_projections(layer_mine, *weights, other)
    at = lax.rem(place, part)
    held = (place >= mine) & (place < mine + part)
    residual_out = jnp.where(
        held,
        lax.dynamic_slice_in_dim(layer_mine, at, share, 0),
        lax.dynamic_slice_in_dim(layer_theirs, at, share, 0),
    )
    return (attention, residual_out, next_query, next_keyval.T)


def solution(mesh):
    in_specs = (
        P("req", "tp"),
        P("req", "tp"),
        P("req", None),
        P("req", None, "tp"),
        P("req"),
        P("req", None),
        P("req"),
        P(),
        P(),
        P("req", None, "tp"),
        P("req"),
        P("req"),
        P("tp", None),
        P(),
        P(None, "tp"),
        P(None, "tp"),
        P("tp", None),
        P(),
        P(None, "tp"),
        P(None, "tp"),
    )
    out_specs = (P("req", "tp"), P(("req", "tp"), None), P("req", "tp"), P("req", "tp"))
    return jax.shard_map(
        per_device, mesh=mesh, in_specs=in_specs, out_specs=out_specs, check_vma=False
    )
```

```python
import functools
import math

import jax
import jax.numpy as jnp
from jax import lax
from jax.experimental import pallas as pl
from jax.experimental.pallas import tpu as pltpu
from jax.sharding import PartitionSpec as P

HD = 80
ROOTS = 2
MIDS = 6
LANES = 128
MASKED = -1e30
EPSILON = 1e-05
RATE = math.log2(math.e) / math.sqrt(HD)

PIECES = 2

bf16 = jnp.bfloat16
f32 = jnp.float32
i32 = jnp.int32
HBM = pl.BlockSpec(memory_space=pltpu.HBM)
VMEM = pl.BlockSpec(memory_space=pltpu.VMEM)
SMEM = pl.BlockSpec(memory_space=pltpu.SMEM)
PARAMS = pltpu.CompilerParams(vmem_limit_bytes=24 * 1024 * 1024)


def padded(width):
    return -(-width // LANES) * LANES


def key_start(c):
    return c * 2 * HD // LANES * LANES


def key_shift(c):
    return c * 2 * HD % LANES


def value_start(c):
    return (c * 2 * HD + HD) // LANES * LANES


def value_shift(c):
    return (c * 2 * HD + HD) % LANES


def key_window(ref, c):
    first = ref[:, key_start(c) : key_start(c) + LANES]
    last = ref[:, ref.shape[1] - LANES :]
    return jnp.concatenate([first, last], axis=1)


def value_window(ref, c):
    stop = min(value_start(c) + 2 * LANES, ref.shape[1])
    return ref[:, value_start(c) : stop]


def scores_of(query, keys):
    return lax.dot_general(query, keys, (((1,), (1,)), ((), ())), preferred_element_type=f32)


def fetch(pairs, sems):
    copies = [pltpu.make_async_copy(a, b, sems.at[i]) for i, (a, b) in enumerate(pairs)]
    for copy in copies:
        copy.start()
    return copies


def piece(width, k):
    step = width // PIECES
    return slice(k * step, (k + 1) * step)


def pieces_of(rows, width, dtype):
    return tuple(jax.ShapeDtypeStruct((rows, width // PIECES), dtype) for _ in range(PIECES))


def joined(refs):
    return jnp.concatenate([ref[...] for ref in refs], axis=1)


def in_hbm(values):
    return [pltpu.with_memory_space_constraint(value, pltpu.HBM) for value in values]


def in_vmem(values):
    return [pltpu.with_memory_space_constraint(value, pltpu.VMEM) for value in values]


def prep_kernel(
    node_hbm, rank_hbm, length_hbm, root_hbm, pool_ref, out_ref, node_ref, rank_ref, length_ref, root_ref, sems
):
    pairs = ((node_hbm, node_ref), (rank_hbm, rank_ref), (length_hbm, length_ref), (root_hbm, root_ref))
    for copy in fetch(pairs, sems):
        copy.wait()
    pages, size, width = pool_ref.shape
    free = out_ref.shape[1] - width
    lane = lax.broadcasted_iota(i32, (size, free), 1)
    slot = lax.broadcasted_iota(i32, (size, free), 0)
    root = jnp.full((size, free), -2, i32)
    for m in range(MIDS):
        root = jnp.where(lane == m, root_ref[m], root)
    hidden = jnp.where(lane < MIDS, MASKED, 0.0)
    for p in range(pages):
        node = node_ref[p]
        left = length_ref[jnp.maximum(node, 0)] - size * rank_ref[p]
        seen = ((root == node) | (lane + ROOTS == node)) & (slot < left)
        rows = slice(p * size, (p + 1) * size)
        out_ref[rows, :width] = pool_ref[p]
        out_ref[rows, width:] = jnp.where(seen, 0.0, hidden).astype(bf16)


def prepare(page_node, page_rank, node_length, mid_root, prefix_pool):
    pages, size, width = prefix_pool.shape
    tables = (page_node, page_rank, node_length, mid_root)
    return pl.pallas_call(
        prep_kernel,
        out_shape=jax.ShapeDtypeStruct((pages * size, padded(width + MIDS)), bf16),
        in_specs=[HBM] * 4 + [VMEM],
        out_specs=VMEM,
        scratch_shapes=[pltpu.SMEM(t.shape, i32) for t in tables] + [pltpu.SemaphoreType.DMA((4,))],
        compiler_params=PARAMS,
        name="pool_rows",
    )(*in_hbm(tables), prefix_pool)


def half_start(rows, half):
    parity = lax.rem(lax.axis_index("tp"), 2)
    return (parity if half else 1 - parity) * (rows // 2)


def fold(scores, values, state):
    top = functools.reduce(jnp.maximum, [jnp.max(s, axis=1, keepdims=True) for s in scores])
    if state is not None:
        top = jnp.maximum(top, state[0])
    total, weighted = None, None
    for s, v in zip(scores, values):
        raised = jnp.exp2((s - top) * RATE)
        part = jnp.sum(raised, axis=1, keepdims=True)
        mixed = jnp.dot(raised.astype(bf16), v, preferred_element_type=f32)
        total = part if total is None else total + part
        weighted = mixed if weighted is None else weighted + mixed
    if state is not None:
        factor = jnp.exp2((state[0] - top) * RATE)
        total = total + state[1] * factor
        weighted = weighted + state[2] * factor
    return top, total, weighted


def pack(top, total, weighted):
    lane = lax.broadcasted_iota(i32, weighted.shape, 1)
    return jnp.where(lane == 0, top, jnp.where(lane == 1, total, weighted))


def unpack(state):
    return state[:, 0:1], state[:, 1:2], state


def local_kernel(
    count_hbm, mid_hbm, leaf_len_hbm, query_ref, keyval_ref, leaf_ref, *refs, chunks
):
    pool_refs = refs[:chunks]
    aug_ref, state_ref, count_ref, mid_ref, leaf_len_ref, sems = refs[chunks:]
    pairs = ((count_hbm, count_ref), (mid_hbm, mid_ref), (leaf_len_hbm, leaf_len_ref))
    for copy in fetch(pairs, sems):
        copy.wait()
    rows = query_ref.shape[0]
    part = rows // 2
    width = keyval_ref.shape[1]
    requests, slots, _ = leaf_ref.shape
    kv_local = width // (2 * HD)
    group = query_ref.shape[1] // (kv_local * HD)
    lane = lax.broadcasted_iota(i32, (part, LANES), 1)
    zero = jnp.zeros((part, LANES), i32)
    leaf_all = leaf_ref[...].reshape(requests * slots, width)
    leaf_at = lax.broadcasted_iota(i32, (part, requests * slots), 1)
    for half in range(2):
        first = half_start(rows, half)
        row = lax.broadcasted_iota(i32, (part, LANES), 0) + first
        start, low, high, mid = zero, zero, zero, zero
        begin = jnp.int32(0)
        for r in range(requests):
            here = row >= begin
            start = jnp.where(here, begin, start)
            low = jnp.where(here, r * slots, low)
            high = jnp.where(here, r * slots + leaf_len_ref[r], high)
            mid = jnp.where(here, mid_ref[r], mid)
            begin = begin + count_ref[0, r]
        chosen = jnp.where(lane == width % LANES + mid, 1.0, 0.0).astype(bf16)
        leaf_ok = (leaf_at >= low[:, 0:1]) & (leaf_at < high[:, 0:1])
        new_ok = (lane >= start) & (lane <= row)
        tokens = query_ref[pl.ds(pl.multiple_of(first, part), part), :]
        for c in range(kv_local):
            base = (half * kv_local + c) * group * part
            block = slice(base, base + group * part)
            key0, val0 = key_start(c), value_start(c)
            shift = key_shift(c)
            for g in range(group):
                h = c * group + g
                at = slice(base + g * part, base + (g + 1) * part)
                aug_ref[at, :LANES] = jnp.zeros((part, LANES), bf16)
                aug_ref[at, shift : shift + HD] = tokens[:, h * HD : (h + 1) * HD]
                aug_ref[at, LANES:] = chosen
            query = aug_ref[block, :]
            narrow = query[:, :LANES]
            s_leaf = scores_of(narrow, leaf_all[:, key0 : key0 + LANES])
            s_leaf = jnp.where(leaf_ok[None], s_leaf.reshape(group, part, -1), MASKED)
            s_new = scores_of(narrow, keyval_ref[:, key0 : key0 + LANES])
            s_new = jnp.where(new_ok[None], s_new.reshape(group, part, -1), MASKED)
            scores = [s_leaf.reshape(group * part, -1), s_new.reshape(group * part, -1)]
            stop = min(val0 + 2 * LANES, width)
            fill = val0 + 2 * LANES - stop
            values = [leaf_all[:, val0:stop], keyval_ref[:, val0:stop]]
            if fill:
                values = [
                    jnp.concatenate([v, jnp.zeros((v.shape[0], fill), bf16)], axis=1) for v in values
                ]
            for pool_ref in pool_refs:
                scores.append(scores_of(query, key_window(pool_ref, c)))
                values.append(value_window(pool_ref, c))
            state_ref[block, :] = pack(*fold(scores, values, None))


def start_attention(new_query, new_keyval, leaf, leaf_length, counts, request_mid, pools):
    rows, query_width = new_query.shape
    heads = query_width // HD
    tables = (counts, request_mid, leaf_length)
    keys = leaf.shape[0] * leaf.shape[1] + rows + sum(item.shape[0] for item in pools)
    return pl.pallas_call(
        functools.partial(local_kernel, chunks=len(pools)),
        out_shape=(
            jax.ShapeDtypeStruct((heads * rows, 2 * LANES), bf16),
            jax.ShapeDtypeStruct((heads * rows, 2 * LANES), f32),
        ),
        in_specs=[HBM] * 3 + [VMEM] * (3 + len(pools)),
        out_specs=(VMEM, VMEM),
        scratch_shapes=[pltpu.SMEM(t.shape, i32) for t in tables] + [pltpu.SemaphoreType.DMA((3,))],
        compiler_params=PARAMS,
        cost_estimate=attention_cost(heads * rows, keys),
        name="attend_local",
    )(*in_hbm(tables), new_query, new_keyval, leaf, *pools)


def attention_cost(rows, keys):
    return pl.CostEstimate(
        flops=8 * LANES * rows * keys, bytes_accessed=8 * rows * 2 * LANES, transcendentals=rows * keys
    )


def extended(query, state, pool_refs, c):
    scores = [scores_of(query, key_window(ref, c)) for ref in pool_refs]
    values = [value_window(ref, c) for ref in pool_refs]
    return fold(scores, values, unpack(state))


def chunk_kernel(*refs, blocks):
    aug_ref, state_ref = refs[:2]
    pool_refs, out_ref = refs[2:-1], refs[-1]
    size = aug_ref.shape[0] // blocks
    for b in range(blocks):
        at = slice(b * size, (b + 1) * size)
        state = extended(aug_ref[at, :], state_ref[at, :], pool_refs, b % (blocks // 2))
        out_ref[at, :] = pack(*state)


def extend_attention(aug, state, pools, kv_local):
    keys = sum(item.shape[0] for item in pools)
    return pl.pallas_call(
        functools.partial(chunk_kernel, blocks=2 * kv_local),
        out_shape=jax.ShapeDtypeStruct(state.shape, f32),
        in_specs=[VMEM] * (2 + len(pools)),
        out_specs=VMEM,
        compiler_params=PARAMS,
        cost_estimate=attention_cost(aug.shape[0], keys),
        name="attend_pages",
    )(aug, state, *pools)


def finish_kernel(*refs, half, kv_local, chunks, width):
    aug_ref, state_ref = refs[:2]
    pool_refs = refs[2 : 2 + chunks]
    weight_ref = refs[2 + chunks]
    part = aug_ref.shape[0] // (2 * width // HD)
    rest = refs[3 + chunks :]
    att_ref, *proj_refs, mine_ref = rest[2 * half :]
    proj_refs, res_refs = proj_refs[:PIECES], proj_refs[PIECES:]
    group = width // (kv_local * HD)
    size = group * part
    for c in range(kv_local):
        at = slice((half * kv_local + c) * size, (half * kv_local + c + 1) * size)
        if chunks:
            state = extended(aug_ref[at, :], state_ref[at, :], pool_refs, c)
        else:
            state = unpack(state_ref[at, :])
        shift = value_shift(c)
        result = (state[2][:, shift : shift + HD] / state[1]).astype(bf16)
        for g in range(group):
            h = c * group + g
            mine_ref[:, h * HD : (h + 1) * HD] = result[g * part : (g + 1) * part]
    if half:
        mine = pl.multiple_of(half_start(2 * part, 1), part)
        theirs = pl.multiple_of(half_start(2 * part, 0), part)
        att_ref[pl.ds(mine, part), :] = mine_ref[...]
        att_ref[pl.ds(theirs, part), :] = rest[0][...]
        for k, res_ref in enumerate(res_refs):
            res_ref[...] = rest[1][pl.ds(mine, part), piece(rest[1].shape[1], k)]
    else:
        att_ref[...] = mine_ref[...]
    for k, proj_ref in enumerate(proj_refs):
        weight = weight_ref[:, piece(weight_ref.shape[1], k)]
        proj = jnp.dot(mine_ref[...], weight, preferred_element_type=f32)
        proj_ref[...] = proj.astype(proj_ref.dtype)


def finish_attention(aug, state, pools, out_weight, half, kv_local, rows, other):
    width = out_weight.shape[0]
    part = rows // 2
    keys = sum(item.shape[0] for item in pools)
    return pl.pallas_call(
        functools.partial(
            finish_kernel, half=half, kv_local=kv_local, chunks=len(pools), width=width
        ),
        out_shape=(
            jax.ShapeDtypeStruct((rows if half else part, width), bf16),
            *pieces_of(part, out_weight.shape[1], f32 if half else bf16),
            *(pieces_of(part, out_weight.shape[1], bf16) if half else ()),
        ),
        in_specs=[VMEM] * (3 + len(pools) + len(other)),
        out_specs=(VMEM,) * (1 + PIECES + half * PIECES),
        scratch_shapes=[pltpu.VMEM((part, width), bf16)],
        compiler_params=PARAMS,
        cost_estimate=attention_cost(aug.shape[0] // 2, keys + 512),
        name="attend_finish",
    )(aug, state, *pools, out_weight, *other)


def normalized(values_in, gain):
    values = values_in.astype(f32)
    scale = lax.rsqrt(jnp.mean(values * values, axis=-1, keepdims=True) + EPSILON)
    return (values * scale * gain.astype(f32)).astype(bf16)


def stage_kernel(*refs):
    count = len(refs) // 2
    for copy in fetch(zip(refs[:count], refs[count : 2 * count]), refs[-1]):
        copy.wait()


def stage(weights):
    return pl.pallas_call(
        stage_kernel,
        out_shape=tuple(pltpu.VMEM(w.shape, w.dtype) for w in weights),
        in_specs=[HBM] * len(weights),
        out_specs=(VMEM,) * len(weights),
        scratch_shapes=[pltpu.SemaphoreType.DMA((len(weights),))],
        compiler_params=pltpu.CompilerParams(vmem_limit_bytes=1024 * 1024),
        cost_estimate=pl.CostEstimate(
            flops=0, bytes_accessed=sum(2 * w.size for w in weights), transcendentals=0
        ),
        name="stage",
    )(*in_hbm(weights))


def mlp_kernel(*refs):
    row_refs, (gain_ref, gate_ref, up_ref, down_ref) = refs[:PIECES], refs[PIECES : PIECES + 4]
    normed = normalized(joined(row_refs), gain_ref[...])
    gate = jnp.dot(normed, gate_ref[...], preferred_element_type=f32)
    upward = jnp.dot(normed, up_ref[...], preferred_element_type=f32)
    hidden = (jax.nn.silu(gate) * upward).astype(bf16)
    for k, out_ref in enumerate(refs[PIECES + 4 :]):
        weight = down_ref[:, piece(down_ref.shape[1], k)]
        result = jnp.dot(hidden, weight, preferred_element_type=f32)
        out_ref[...] = result.astype(out_ref.dtype)


def feed_forward(rows, gain, gate_weight, up_weight, down_weight, dtype):
    count = rows[0].shape[0]
    depth, width = gate_weight.shape
    return pl.pallas_call(
        mlp_kernel,
        out_shape=pieces_of(count, depth, dtype),
        in_specs=[VMEM] * (PIECES + 4),
        out_specs=(VMEM,) * PIECES,
        compiler_params=PARAMS,
        cost_estimate=pl.CostEstimate(
            flops=6 * count * depth * width, bytes_accessed=6 * depth * width, transcendentals=0
        ),
        name="feed_forward",
    )(*rows, gain.reshape(1, depth), *in_vmem((gate_weight, up_weight, down_weight)))


def next_kernel(*refs, half):
    row_refs, refs = refs[:PIECES], refs[PIECES:]
    gain_ref, query_ref, keyval_ref = refs[:3]
    rows = joined(row_refs)
    normed = normalized(rows, gain_ref[...])
    query = jnp.dot(normed, query_ref[...], preferred_element_type=f32).astype(bf16)
    keyval = scores_of(keyval_ref[...], normed).astype(bf16)
    if not half:
        query_out, keyval_out = refs[3:]
        query_out[...] = query
        keyval_out[...] = keyval
        return
    query_in, keyval_in = refs[3:5]
    query_out, keyval_out, residual_out = refs[5 + PIECES :]
    part = query.shape[0]
    mine = pl.multiple_of(half_start(2 * part, 1), part)
    theirs = pl.multiple_of(half_start(2 * part, 0), part)
    query_out[pl.ds(mine, part), :] = query
    query_out[pl.ds(theirs, part), :] = query_in[...]

    @pl.when(mine == 0)
    def _():
        keyval_out[:, :part] = keyval
        keyval_out[:, part:] = keyval_in[...]

    @pl.when(mine != 0)
    def _():
        keyval_out[:, :part] = keyval_in[...]
        keyval_out[:, part:] = keyval

    share = residual_out.shape[0]
    place = lax.axis_index("tp") * share
    at = pl.multiple_of(lax.rem(place, part), share)
    held = (place >= mine) & (place < mine + part)
    for k in range(PIECES):
        ours = row_refs[k][pl.ds(at, share), :]
        others = refs[5 + k][pl.ds(at, share), :]
        residual_out[:, piece(rows.shape[1], k)] = jnp.where(held, ours, others)


def next_projections(rows, gain, query_weight, keyval_weight, other):
    count = rows[0].shape[0]
    depth = query_weight.shape[0]
    widths = (query_weight.shape[1], keyval_weight.shape[0])
    half = len(other) > 0
    out_rows = 2 * count if half else count
    shapes = [(out_rows, widths[0]), (widths[1], out_rows)]
    if half:
        shapes.append((out_rows // lax.axis_size("tp"), depth))
    return pl.pallas_call(
        functools.partial(next_kernel, half=half),
        out_shape=tuple(jax.ShapeDtypeStruct(shape, bf16) for shape in shapes),
        in_specs=[VMEM] * (PIECES + 3 + len(other)),
        out_specs=(VMEM,) * len(shapes),
        compiler_params=PARAMS,
        cost_estimate=pl.CostEstimate(
            flops=2 * count * depth * sum(widths),
            bytes_accessed=2 * depth * sum(widths),
            transcendentals=0,
        ),
        name="next_layer",
    )(*rows, gain.reshape(1, depth), *in_vmem([query_weight]), keyval_weight, *other)


def trade(value, axis, bit):
    size = lax.axis_size(axis)
    return lax.ppermute(value, axis, [(i, i ^ bit) for i in range(size)])


def cross(value, even_bit, odd_bit):
    size = lax.axis_size("req")
    pairs = [(i, i ^ (odd_bit if i % 2 else even_bit)) for i in range(size)]
    return lax.ppermute(value, "req", pairs)


def trades(values, bit):
    return [trade(value, "tp", bit) for value in values]


def each(join, *pieces):
    return [join(*items) for items in zip(*pieces)]


def add_pair(mine, got):
    return (mine + wide(got)).astype(bf16)


def add_rows(pair, rows, got):
    return (wide(rows) + (wide(pair) + wide(got))).astype(bf16)


def wide(value):
    return value.astype(f32)


def per_device(
    new_query,
    new_keyval,
    residual_in,
    leaf_cache,
    leaf_length,
    new_counts,
    request_mid,
    mid_root,
    node_length,
    prefix_pool,
    page_node,
    page_rank,
    out_weight,
    norm_gain,
    gate_weight,
    up_weight,
    down_weight,
    next_gain,
    query_weight,
    keyval_weight,
):
    rows = new_query.shape[0]
    part = rows // 2
    kv_local = new_keyval.shape[1] // (2 * HD)
    pool = prepare(page_node, page_rank, node_length, mid_root, prefix_pool)
    local_args = (new_query, new_keyval, leaf_cache, leaf_length, new_counts, request_mid)
    if lax.axis_size("req") == 8:
        first = cross(pool, 2, 4)
        second = cross(pool, 4, 2)
        beside = trade(pool, "req", 1)
        aug, state = start_attention(*local_args, [pool, beside])
        first, second, aug, state = lax.optimization_barrier((first, second, aug, state))
        corner = cross(first, 4, 2)
        first_other = trade(first, "req", 1)
        second_other = trade(second, "req", 1)
        near = [first, second, first_other, second_other]
        state = extend_attention(aug, state, near, kv_local)
        corner, aug, state = lax.optimization_barrier((corner, aug, state))
        pools = [corner, trade(corner, "req", 1)]
    else:
        every = lax.all_gather(pool, "req", axis=0)
        holders = every.shape[0]
        aug, state = start_attention(*local_args, [pool])
        places = (lax.axis_index("req") + 1 + jnp.arange(holders - 1)) % holders
        step = 4
        for i in range(0, holders - 1, step):
            chunk = every[places[i : i + step]].reshape(-1, pool.shape[1])
            state = extend_attention(aug, state, [chunk], kv_local)
        pools = []

    theirs_att, *theirs_proj = finish_attention(
        aug, state, pools, out_weight, 0, kv_local, rows, ()
    )
    attention, *mine_proj = finish_attention(
        aug, state, pools, out_weight, 1, kv_local, rows, (theirs_att, residual_in)
    )
    mine_proj, res_mine = mine_proj[:PIECES], mine_proj[PIECES:]

    mine = half_start(rows, 1)
    theirs = half_start(rows, 0)
    depth = residual_in.shape[1]
    if lax.axis_size("tp") == 4:
        got = trades(theirs_proj, 1)
        pair = each(add_pair, mine_proj, got)
        pair[0], *mlp = lax.optimization_barrier((pair[0], gate_weight, up_weight, down_weight))
        got = trades(pair, 2)
        got[-1], *mlp = lax.optimization_barrier((got[-1], *stage(mlp)))
        mixed_mine = each(add_rows, pair, res_mine, got)
        mixed_theirs = trades(mixed_mine, 1)
        got = trades(feed_forward(mixed_mine, norm_gain, *mlp, bf16), 1)
        mlp_theirs = feed_forward(mixed_theirs, norm_gain, *mlp, f32)
        pair = each(add_pair, mlp_theirs, got)
        pair[0], query_weight = lax.optimization_barrier((pair[0], query_weight))
        got = trades(pair, 2)
        got[-1], query_weight = lax.optimization_barrier((got[-1], stage([query_weight])[0]))
        layer_theirs = each(add_rows, pair, mixed_theirs, got)
        layer_mine = trades(layer_theirs, 1)
    else:
        res_mine = jnp.concatenate(res_mine, axis=1)
        res_theirs = lax.dynamic_slice_in_dim(residual_in, theirs, part, 0)

        def in_order(theirs_part, mine_part):
            both = jnp.stack([theirs_part, mine_part])
            return jnp.where(mine == 0, both[::-1], both).reshape(rows, -1)

        theirs_proj = jnp.concatenate([wide(item) for item in theirs_proj], axis=1)
        mine_proj = jnp.concatenate(mine_proj, axis=1)
        total = lax.psum(in_order(theirs_proj, mine_proj), "tp")
        mixed = (wide(in_order(res_theirs, res_mine)) + total).astype(bf16)
        mixed_pieces = [mixed[:, piece(depth, k)] for k in range(PIECES)]
        mlp = feed_forward(mixed_pieces, norm_gain, gate_weight, up_weight, down_weight, f32)
        mlp = lax.psum(jnp.concatenate(mlp, axis=1), "tp")
        layer = (wide(mixed) + mlp).astype(bf16)
        layer = [layer[:, piece(depth, k)] for k in range(PIECES)]
        layer_mine = [lax.dynamic_slice_in_dim(item, mine, part, 0) for item in layer]
        layer_theirs = [lax.dynamic_slice_in_dim(item, theirs, part, 0) for item in layer]
    weights = (next_gain, query_weight, keyval_weight.T)
    other = next_projections(layer_theirs, *weights, ())
    next_query, next_keyval, residual_out = next_projections(
        layer_mine, *weights, (*other, *layer_theirs)
    )
    return (attention, residual_out, next_query, next_keyval.T)


def solution(mesh):
    in_specs = (
        P("req", "tp"),
        P("req", "tp"),
        P("req", None),
        P("req", None, "tp"),
        P("req"),
        P("req", None),
        P("req"),
        P(),
        P(),
        P("req", None, "tp"),
        P("req"),
        P("req"),
        P("tp", None),
        P(),
        P(None, "tp"),
        P(None, "tp"),
        P("tp", None),
        P(),
        P(None, "tp"),
        P(None, "tp"),
    )
    out_specs = (P("req", "tp"), P(("req", "tp"), None), P("req", "tp"), P("req", "tp"))
    return jax.shard_map(
        per_device, mesh=mesh, in_specs=in_specs, out_specs=out_specs, check_vma=False
    )
```

```python
import functools
import math

import jax
import jax.numpy as jnp
from jax import lax
from jax.experimental import pallas as pl
from jax.experimental.pallas import tpu as pltpu
from jax.sharding import PartitionSpec as P

HD = 80
ROOTS = 2
MIDS = 6
LANES = 128
MASKED = -1e30
EPSILON = 1e-05
RATE = math.log2(math.e) / math.sqrt(HD)

PIECES = 2

bf16 = jnp.bfloat16
f32 = jnp.float32
i32 = jnp.int32
HBM = pl.BlockSpec(memory_space=pltpu.HBM)
VMEM = pl.BlockSpec(memory_space=pltpu.VMEM)
SMEM = pl.BlockSpec(memory_space=pltpu.SMEM)
PARAMS = pltpu.CompilerParams(vmem_limit_bytes=24 * 1024 * 1024)


def padded(width):
    return -(-width // LANES) * LANES


def key_start(c):
    return c * 2 * HD // LANES * LANES


def key_shift(c):
    return c * 2 * HD % LANES


def value_start(c):
    return (c * 2 * HD + HD) // LANES * LANES


def value_shift(c):
    return (c * 2 * HD + HD) % LANES


def key_window(ref, c):
    first = ref[:, key_start(c) : key_start(c) + LANES]
    last = ref[:, ref.shape[1] - LANES :]
    return jnp.concatenate([first, last], axis=1)


def value_window(ref, c):
    stop = min(value_start(c) + 2 * LANES, ref.shape[1])
    return ref[:, value_start(c) : stop]


def scores_of(query, keys):
    return lax.dot_general(query, keys, (((1,), (1,)), ((), ())), preferred_element_type=f32)


def fetch(pairs, sems):
    copies = [pltpu.make_async_copy(a, b, sems.at[i]) for i, (a, b) in enumerate(pairs)]
    for copy in copies:
        copy.start()
    return copies


def piece(width, k):
    step = width // PIECES
    return slice(k * step, (k + 1) * step)


def pieces_of(rows, width, dtype):
    return tuple(jax.ShapeDtypeStruct((rows, width // PIECES), dtype) for _ in range(PIECES))


def joined(refs):
    return jnp.concatenate([ref[...] for ref in refs], axis=1)


def in_hbm(values):
    return [pltpu.with_memory_space_constraint(value, pltpu.HBM) for value in values]


def in_vmem(values):
    return [pltpu.with_memory_space_constraint(value, pltpu.VMEM) for value in values]


def prep_kernel(
    node_hbm, rank_hbm, length_hbm, root_hbm, pool_ref, out_ref, node_ref, rank_ref, length_ref, root_ref, sems
):
    pairs = ((node_hbm, node_ref), (rank_hbm, rank_ref), (length_hbm, length_ref), (root_hbm, root_ref))
    for copy in fetch(pairs, sems):
        copy.wait()
    pages, size, width = pool_ref.shape
    free = out_ref.shape[1] - width
    lane = lax.broadcasted_iota(i32, (size, free), 1)
    slot = lax.broadcasted_iota(i32, (size, free), 0)
    root = jnp.full((size, free), -2, i32)
    for m in range(MIDS):
        root = jnp.where(lane == m, root_ref[m], root)
    hidden = jnp.where(lane < MIDS, MASKED, 0.0)
    for p in range(pages):
        node = node_ref[p]
        left = length_ref[jnp.maximum(node, 0)] - size * rank_ref[p]
        seen = ((root == node) | (lane + ROOTS == node)) & (slot < left)
        rows = slice(p * size, (p + 1) * size)
        out_ref[rows, :width] = pool_ref[p]
        out_ref[rows, width:] = jnp.where(seen, 0.0, hidden).astype(bf16)


def prepare(page_node, page_rank, node_length, mid_root, prefix_pool):
    pages, size, width = prefix_pool.shape
    tables = (page_node, page_rank, node_length, mid_root)
    return pl.pallas_call(
        prep_kernel,
        out_shape=jax.ShapeDtypeStruct((pages * size, padded(width + MIDS)), bf16),
        in_specs=[HBM] * 4 + [VMEM],
        out_specs=VMEM,
        scratch_shapes=[pltpu.SMEM(t.shape, i32) for t in tables] + [pltpu.SemaphoreType.DMA((4,))],
        compiler_params=PARAMS,
        name="pool_rows",
    )(*in_hbm(tables), prefix_pool)


def half_start(rows, half):
    parity = lax.rem(lax.axis_index("tp"), 2)
    return (parity if half else 1 - parity) * (rows // 2)


def fold(scores, values, state):
    top = functools.reduce(jnp.maximum, [jnp.max(s, axis=1, keepdims=True) for s in scores])
    if state is not None:
        top = jnp.maximum(top, state[0])
    total, weighted = None, None
    for s, v in zip(scores, values):
        raised = jnp.exp2((s - top) * RATE)
        part = jnp.sum(raised, axis=1, keepdims=True)
        mixed = jnp.dot(raised.astype(bf16), v, preferred_element_type=f32)
        total = part if total is None else total + part
        weighted = mixed if weighted is None else weighted + mixed
    if state is not None:
        factor = jnp.exp2((state[0] - top) * RATE)
        total = total + state[1] * factor
        weighted = weighted + state[2] * factor
    return top, total, weighted


def pack(top, total, weighted):
    lane = lax.broadcasted_iota(i32, weighted.shape, 1)
    return jnp.where(lane == 0, top, jnp.where(lane == 1, total, weighted))


def unpack(state):
    return state[:, 0:1], state[:, 1:2], state


def local_kernel(
    count_hbm, mid_hbm, leaf_len_hbm, query_ref, keyval_ref, leaf_ref, *refs, chunks
):
    pool_refs = refs[:chunks]
    aug_ref, state_ref, count_ref, mid_ref, leaf_len_ref, sems = refs[chunks:]
    pairs = ((count_hbm, count_ref), (mid_hbm, mid_ref), (leaf_len_hbm, leaf_len_ref))
    for copy in fetch(pairs, sems):
        copy.wait()
    rows = query_ref.shape[0]
    part = rows // 2
    width = keyval_ref.shape[1]
    requests, slots, _ = leaf_ref.shape
    kv_local = width // (2 * HD)
    group = query_ref.shape[1] // (kv_local * HD)
    lane = lax.broadcasted_iota(i32, (part, LANES), 1)
    zero = jnp.zeros((part, LANES), i32)
    leaf_all = leaf_ref[...].reshape(requests * slots, width)
    leaf_at = lax.broadcasted_iota(i32, (part, requests * slots), 1)
    for half in range(2):
        first = half_start(rows, half)
        row = lax.broadcasted_iota(i32, (part, LANES), 0) + first
        start, low, high, mid = zero, zero, zero, zero
        begin = jnp.int32(0)
        for r in range(requests):
            here = row >= begin
            start = jnp.where(here, begin, start)
            low = jnp.where(here, r * slots, low)
            high = jnp.where(here, r * slots + leaf_len_ref[r], high)
            mid = jnp.where(here, mid_ref[r], mid)
            begin = begin + count_ref[0, r]
        chosen = jnp.where(lane == width % LANES + mid, 1.0, 0.0).astype(bf16)
        leaf_ok = (leaf_at >= low[:, 0:1]) & (leaf_at < high[:, 0:1])
        new_ok = (lane >= start) & (lane <= row)
        tokens = query_ref[pl.ds(pl.multiple_of(first, part), part), :]
        for c in range(kv_local):
            base = (half * kv_local + c) * group * part
            block = slice(base, base + group * part)
            key0, val0 = key_start(c), value_start(c)
            shift = key_shift(c)
            for g in range(group):
                h = c * group + g
                at = slice(base + g * part, base + (g + 1) * part)
                aug_ref[at, :LANES] = jnp.zeros((part, LANES), bf16)
                aug_ref[at, shift : shift + HD] = tokens[:, h * HD : (h + 1) * HD]
                aug_ref[at, LANES:] = chosen
            query = aug_ref[block, :]
            narrow = query[:, :LANES]
            s_leaf = scores_of(narrow, leaf_all[:, key0 : key0 + LANES])
            s_leaf = jnp.where(leaf_ok[None], s_leaf.reshape(group, part, -1), MASKED)
            s_new = scores_of(narrow, keyval_ref[:, key0 : key0 + LANES])
            s_new = jnp.where(new_ok[None], s_new.reshape(group, part, -1), MASKED)
            scores = [s_leaf.reshape(group * part, -1), s_new.reshape(group * part, -1)]
            stop = min(val0 + 2 * LANES, width)
            fill = val0 + 2 * LANES - stop
            values = [leaf_all[:, val0:stop], keyval_ref[:, val0:stop]]
            if fill:
                values = [
                    jnp.concatenate([v, jnp.zeros((v.shape[0], fill), bf16)], axis=1) for v in values
                ]
            for pool_ref in pool_refs:
                scores.append(scores_of(query, key_window(pool_ref, c)))
                values.append(value_window(pool_ref, c))
            state_ref[block, :] = pack(*fold(scores, values, None))


def start_attention(new_query, new_keyval, leaf, leaf_length, counts, request_mid, pools):
    rows, query_width = new_query.shape
    heads = query_width // HD
    tables = (counts, request_mid, leaf_length)
    keys = leaf.shape[0] * leaf.shape[1] + rows + sum(item.shape[0] for item in pools)
    return pl.pallas_call(
        functools.partial(local_kernel, chunks=len(pools)),
        out_shape=(
            jax.ShapeDtypeStruct((heads * rows, 2 * LANES), bf16),
            jax.ShapeDtypeStruct((heads * rows, 2 * LANES), f32),
        ),
        in_specs=[HBM] * 3 + [VMEM] * (3 + len(pools)),
        out_specs=(VMEM, VMEM),
        scratch_shapes=[pltpu.SMEM(t.shape, i32) for t in tables] + [pltpu.SemaphoreType.DMA((3,))],
        compiler_params=PARAMS,
        cost_estimate=attention_cost(heads * rows, keys),
        name="attend_local",
    )(*in_hbm(tables), new_query, new_keyval, leaf, *pools)


def attention_cost(rows, keys):
    return pl.CostEstimate(
        flops=8 * LANES * rows * keys, bytes_accessed=8 * rows * 2 * LANES, transcendentals=rows * keys
    )


def extended(query, state, pool_refs, c):
    scores = [scores_of(query, key_window(ref, c)) for ref in pool_refs]
    values = [value_window(ref, c) for ref in pool_refs]
    return fold(scores, values, unpack(state))


def chunk_kernel(*refs, blocks):
    aug_ref, state_ref = refs[:2]
    pool_refs, out_ref = refs[2:-1], refs[-1]
    size = aug_ref.shape[0] // blocks
    for b in range(blocks):
        at = slice(b * size, (b + 1) * size)
        state = extended(aug_ref[at, :], state_ref[at, :], pool_refs, b % (blocks // 2))
        out_ref[at, :] = pack(*state)


def extend_attention(aug, state, pools, kv_local):
    keys = sum(item.shape[0] for item in pools)
    return pl.pallas_call(
        functools.partial(chunk_kernel, blocks=2 * kv_local),
        out_shape=jax.ShapeDtypeStruct(state.shape, f32),
        in_specs=[VMEM] * (2 + len(pools)),
        out_specs=VMEM,
        compiler_params=PARAMS,
        cost_estimate=attention_cost(aug.shape[0], keys),
        name="attend_pages",
    )(aug, state, *pools)


def finish_kernel(*refs, half, kv_local, chunks, width):
    aug_ref, state_ref = refs[:2]
    pool_refs = refs[2 : 2 + chunks]
    weight_ref = refs[2 + chunks]
    part = aug_ref.shape[0] // (2 * width // HD)
    rest = refs[3 + chunks :]
    att_ref, *proj_refs, mine_ref = rest[2 * half :]
    proj_refs, res_refs = proj_refs[:PIECES], proj_refs[PIECES:]
    group = width // (kv_local * HD)
    size = group * part
    for c in range(kv_local):
        at = slice((half * kv_local + c) * size, (half * kv_local + c + 1) * size)
        if chunks:
            state = extended(aug_ref[at, :], state_ref[at, :], pool_refs, c)
        else:
            state = unpack(state_ref[at, :])
        shift = value_shift(c)
        result = (state[2][:, shift : shift + HD] / state[1]).astype(bf16)
        for g in range(group):
            h = c * group + g
            mine_ref[:, h * HD : (h + 1) * HD] = result[g * part : (g + 1) * part]
    if half:
        mine = pl.multiple_of(half_start(2 * part, 1), part)
        theirs = pl.multiple_of(half_start(2 * part, 0), part)
        att_ref[pl.ds(mine, part), :] = mine_ref[...]
        att_ref[pl.ds(theirs, part), :] = rest[0][...]
        for k, res_ref in enumerate(res_refs):
            res_ref[...] = rest[1][pl.ds(mine, part), piece(rest[1].shape[1], k)]
    else:
        att_ref[...] = mine_ref[...]
    for k, proj_ref in enumerate(proj_refs):
        weight = weight_ref[:, piece(weight_ref.shape[1], k)]
        proj = jnp.dot(mine_ref[...], weight, preferred_element_type=f32)
        proj_ref[...] = proj.astype(proj_ref.dtype)


def finish_attention(aug, state, pools, out_weight, half, kv_local, rows, other):
    width = out_weight.shape[0]
    part = rows // 2
    keys = sum(item.shape[0] for item in pools)
    return pl.pallas_call(
        functools.partial(
            finish_kernel, half=half, kv_local=kv_local, chunks=len(pools), width=width
        ),
        out_shape=(
            jax.ShapeDtypeStruct((rows if half else part, width), bf16),
            *pieces_of(part, out_weight.shape[1], f32 if half else bf16),
            *(pieces_of(part, out_weight.shape[1], bf16) if half else ()),
        ),
        in_specs=[VMEM] * (3 + len(pools) + len(other)),
        out_specs=(VMEM,) * (1 + PIECES + half * PIECES),
        scratch_shapes=[pltpu.VMEM((part, width), bf16)],
        compiler_params=PARAMS,
        cost_estimate=attention_cost(aug.shape[0] // 2, keys + 512),
        name="attend_finish",
    )(aug, state, *pools, out_weight, *other)


def normalized(values_in, gain):
    values = values_in.astype(f32)
    scale = lax.rsqrt(jnp.mean(values * values, axis=-1, keepdims=True) + EPSILON)
    return (values * scale * gain.astype(f32)).astype(bf16)


def stage_kernel(*refs):
    count = len(refs) // 2
    for copy in fetch(zip(refs[:count], refs[count : 2 * count]), refs[-1]):
        copy.wait()


def stage(weights):
    return pl.pallas_call(
        stage_kernel,
        out_shape=tuple(pltpu.VMEM(w.shape, w.dtype) for w in weights),
        in_specs=[HBM] * len(weights),
        out_specs=(VMEM,) * len(weights),
        scratch_shapes=[pltpu.SemaphoreType.DMA((len(weights),))],
        compiler_params=pltpu.CompilerParams(vmem_limit_bytes=1024 * 1024),
        cost_estimate=pl.CostEstimate(
            flops=0, bytes_accessed=sum(2 * w.size for w in weights), transcendentals=0
        ),
        name="stage",
    )(*in_hbm(weights))


def mlp_kernel(*refs):
    row_refs, (gain_ref, gate_ref, up_ref, down_ref) = refs[:PIECES], refs[PIECES : PIECES + 4]
    normed = normalized(joined(row_refs), gain_ref[...])
    gate = jnp.dot(normed, gate_ref[...], preferred_element_type=f32)
    upward = jnp.dot(normed, up_ref[...], preferred_element_type=f32)
    hidden = (jax.nn.silu(gate) * upward).astype(bf16)
    for k, out_ref in enumerate(refs[PIECES + 4 :]):
        weight = down_ref[:, piece(down_ref.shape[1], k)]
        result = jnp.dot(hidden, weight, preferred_element_type=f32)
        out_ref[...] = result.astype(out_ref.dtype)


def feed_forward(rows, gain, gate_weight, up_weight, down_weight, dtype):
    count = rows[0].shape[0]
    depth, width = gate_weight.shape
    return pl.pallas_call(
        mlp_kernel,
        out_shape=pieces_of(count, depth, dtype),
        in_specs=[VMEM] * (PIECES + 4),
        out_specs=(VMEM,) * PIECES,
        compiler_params=PARAMS,
        cost_estimate=pl.CostEstimate(
            flops=6 * count * depth * width, bytes_accessed=6 * depth * width, transcendentals=0
        ),
        name="feed_forward",
    )(*rows, gain.reshape(1, depth), *in_vmem((gate_weight, up_weight, down_weight)))


def next_kernel(*refs, half):
    row_refs, refs = refs[:PIECES], refs[PIECES:]
    gain_ref, query_ref, keyval_ref = refs[:3]
    rows = joined(row_refs)
    normed = normalized(rows, gain_ref[...])
    query = jnp.dot(normed, query_ref[...], preferred_element_type=f32).astype(bf16)
    keyval = scores_of(keyval_ref[...], normed).astype(bf16)
    if not half:
        query_out, keyval_out = refs[3:]
        query_out[...] = query
        keyval_out[...] = keyval
        return
    query_in, keyval_in = refs[3:5]
    query_out, keyval_out, residual_out = refs[5 + PIECES :]
    part = query.shape[0]
    mine = pl.multiple_of(half_start(2 * part, 1), part)
    theirs = pl.multiple_of(half_start(2 * part, 0), part)
    query_out[pl.ds(mine, part), :] = query
    query_out[pl.ds(theirs, part), :] = query_in[...]

    @pl.when(mine == 0)
    def _():
        keyval_out[:, :part] = keyval
        keyval_out[:, part:] = keyval_in[...]

    @pl.when(mine != 0)
    def _():
        keyval_out[:, :part] = keyval_in[...]
        keyval_out[:, part:] = keyval

    share = residual_out.shape[0]
    place = lax.axis_index("tp") * share
    at = pl.multiple_of(lax.rem(place, part), share)
    held = (place >= mine) & (place < mine + part)
    for k in range(PIECES):
        ours = row_refs[k][pl.ds(at, share), :]
        others = refs[5 + k][pl.ds(at, share), :]
        residual_out[:, piece(rows.shape[1], k)] = jnp.where(held, ours, others)


def next_projections(rows, gain, query_weight, keyval_weight, other):
    count = rows[0].shape[0]
    depth = query_weight.shape[0]
    widths = (query_weight.shape[1], keyval_weight.shape[0])
    half = len(other) > 0
    out_rows = 2 * count if half else count
    shapes = [(out_rows, widths[0]), (widths[1], out_rows)]
    if half:
        shapes.append((out_rows // lax.axis_size("tp"), depth))
    return pl.pallas_call(
        functools.partial(next_kernel, half=half),
        out_shape=tuple(jax.ShapeDtypeStruct(shape, bf16) for shape in shapes),
        in_specs=[VMEM] * (PIECES + 3 + len(other)),
        out_specs=(VMEM,) * len(shapes),
        compiler_params=PARAMS,
        cost_estimate=pl.CostEstimate(
            flops=2 * count * depth * sum(widths),
            bytes_accessed=2 * depth * sum(widths),
            transcendentals=0,
        ),
        name="next_layer",
    )(*rows, gain.reshape(1, depth), *in_vmem([query_weight]), keyval_weight, *other)


def trade(value, axis, bit):
    size = lax.axis_size(axis)
    return lax.ppermute(value, axis, [(i, i ^ bit) for i in range(size)])


def cross(value, even_bit, odd_bit):
    size = lax.axis_size("req")
    pairs = [(i, i ^ (odd_bit if i % 2 else even_bit)) for i in range(size)]
    return lax.ppermute(value, "req", pairs)


def trades(values, bit):
    return [trade(value, "tp", bit) for value in values]


def each(join, *pieces):
    return [join(*items) for items in zip(*pieces)]


def add_pair(mine, got):
    return (mine + wide(got)).astype(bf16)


def add_rows(pair, rows, got):
    return (wide(rows) + (wide(pair) + wide(got))).astype(bf16)


def wide(value):
    return value.astype(f32)


def per_device(
    new_query,
    new_keyval,
    residual_in,
    leaf_cache,
    leaf_length,
    new_counts,
    request_mid,
    mid_root,
    node_length,
    prefix_pool,
    page_node,
    page_rank,
    out_weight,
    norm_gain,
    gate_weight,
    up_weight,
    down_weight,
    next_gain,
    query_weight,
    keyval_weight,
):
    rows = new_query.shape[0]
    part = rows // 2
    kv_local = new_keyval.shape[1] // (2 * HD)
    pool = prepare(page_node, page_rank, node_length, mid_root, prefix_pool)
    local_args = (new_query, new_keyval, leaf_cache, leaf_length, new_counts, request_mid)
    if lax.axis_size("req") == 8:
        first = cross(pool, 2, 4)
        second = cross(pool, 4, 2)
        beside = trade(pool, "req", 1)
        aug, state = start_attention(*local_args, [pool, beside])
        first, aug, state = lax.optimization_barrier((first, aug, state))
        corner = cross(first, 4, 2)
        first, second = lax.optimization_barrier((first, second))
        near = [first, second, trade(first, "req", 1), trade(second, "req", 1)]
        state = extend_attention(aug, state, near, kv_local)
        state, down_weight = lax.optimization_barrier((state, down_weight))
        corner, state, down_weight = lax.optimization_barrier(
            (corner, state, *stage([down_weight]))
        )
        corner_other = trade(corner, "req", 1)
        state = extend_attention(aug, state, [corner], kv_local)
        pools = [corner_other]
    else:
        every = lax.all_gather(pool, "req", axis=0)
        holders = every.shape[0]
        aug, state = start_attention(*local_args, [pool])
        places = (lax.axis_index("req") + 1 + jnp.arange(holders - 1)) % holders
        step = 4
        for i in range(0, holders - 1, step):
            chunk = every[places[i : i + step]].reshape(-1, pool.shape[1])
            state = extend_attention(aug, state, [chunk], kv_local)
        pools = []

    theirs_att, *theirs_proj = finish_attention(
        aug, state, pools, out_weight, 0, kv_local, rows, ()
    )
    attention, *mine_proj = finish_attention(
        aug, state, pools, out_weight, 1, kv_local, rows, (theirs_att, residual_in)
    )
    mine_proj, res_mine = mine_proj[:PIECES], mine_proj[PIECES:]

    mine = half_start(rows, 1)
    theirs = half_start(rows, 0)
    depth = residual_in.shape[1]
    if lax.axis_size("tp") == 4:
        got = trades(theirs_proj, 1)
        last = add_pair(mine_proj[-1], got[-1])
        last, gate_weight, up_weight = lax.optimization_barrier((last, gate_weight, up_weight))
        staged = stage([gate_weight, up_weight])
        got[:-1], gate_weight, up_weight = lax.optimization_barrier((got[:-1], *staged))
        mlp = (gate_weight, up_weight, down_weight)
        pair = [*each(add_pair, mine_proj[:-1], got[:-1]), last]
        got = trades(pair, 2)
        mixed_mine = each(add_rows, pair, res_mine, got)
        mixed_theirs = trades(mixed_mine, 1)
        got = trades(feed_forward(mixed_mine, norm_gain, *mlp, bf16), 1)
        mlp_theirs = feed_forward(mixed_theirs, norm_gain, *mlp, f32)
        last = add_pair(mlp_theirs[-1], got[-1])
        last, query_weight = lax.optimization_barrier((last, query_weight))
        got[:-1], query_weight = lax.optimization_barrier((got[:-1], *stage([query_weight])))
        pair = [*each(add_pair, mlp_theirs[:-1], got[:-1]), last]
        got = trades(pair, 2)
        layer_theirs = each(add_rows, pair, mixed_theirs, got)
        layer_mine = trades(layer_theirs, 1)
    else:
        res_mine = jnp.concatenate(res_mine, axis=1)
        res_theirs = lax.dynamic_slice_in_dim(residual_in, theirs, part, 0)

        def in_order(theirs_part, mine_part):
            both = jnp.stack([theirs_part, mine_part])
            return jnp.where(mine == 0, both[::-1], both).reshape(rows, -1)

        theirs_proj = jnp.concatenate([wide(item) for item in theirs_proj], axis=1)
        mine_proj = jnp.concatenate(mine_proj, axis=1)
        total = lax.psum(in_order(theirs_proj, mine_proj), "tp")
        mixed = (wide(in_order(res_theirs, res_mine)) + total).astype(bf16)
        mixed_pieces = [mixed[:, piece(depth, k)] for k in range(PIECES)]
        mlp = feed_forward(mixed_pieces, norm_gain, gate_weight, up_weight, down_weight, f32)
        mlp = lax.psum(jnp.concatenate(mlp, axis=1), "tp")
        layer = (wide(mixed) + mlp).astype(bf16)
        layer = [layer[:, piece(depth, k)] for k in range(PIECES)]
        layer_mine = [lax.dynamic_slice_in_dim(item, mine, part, 0) for item in layer]
        layer_theirs = [lax.dynamic_slice_in_dim(item, theirs, part, 0) for item in layer]
    weights = (next_gain, query_weight, keyval_weight.T)
    other = next_projections(layer_theirs, *weights, ())
    next_query, next_keyval, residual_out = next_projections(
        layer_mine, *weights, (*other, *layer_theirs)
    )
    return (attention, residual_out, next_query, next_keyval.T)


def solution(mesh):
    in_specs = (
        P("req", "tp"),
        P("req", "tp"),
        P("req", None),
        P("req", None, "tp"),
        P("req"),
        P("req", None),
        P("req"),
        P(),
        P(),
        P("req", None, "tp"),
        P("req"),
        P("req"),
        P("tp", None),
        P(),
        P(None, "tp"),
        P(None, "tp"),
        P("tp", None),
        P(),
        P(None, "tp"),
        P(None, "tp"),
    )
    out_specs = (P("req", "tp"), P(("req", "tp"), None), P("req", "tp"), P("req", "tp"))
    return jax.shard_map(
        per_device, mesh=mesh, in_specs=in_specs, out_specs=out_specs, check_vma=False
    )
```

```python
import functools
import math

import jax
import jax.numpy as jnp
from jax import lax
from jax.experimental import pallas as pl
from jax.experimental.pallas import tpu as pltpu
from jax.sharding import PartitionSpec as P

HD = 80
ROOTS = 2
MIDS = 6
LANES = 128
MASKED = -1e30
EPSILON = 1e-05
RATE = math.log2(math.e) / math.sqrt(HD)

PIECES = 2

bf16 = jnp.bfloat16
f32 = jnp.float32
i32 = jnp.int32
HBM = pl.BlockSpec(memory_space=pltpu.HBM)
VMEM = pl.BlockSpec(memory_space=pltpu.VMEM)
SMEM = pl.BlockSpec(memory_space=pltpu.SMEM)
PARAMS = pltpu.CompilerParams(vmem_limit_bytes=24 * 1024 * 1024)


def padded(width):
    return -(-width // LANES) * LANES


def key_start(c):
    return c * 2 * HD // LANES * LANES


def key_shift(c):
    return c * 2 * HD % LANES


def value_start(c):
    return (c * 2 * HD + HD) // LANES * LANES


def value_shift(c):
    return (c * 2 * HD + HD) % LANES


def key_window(ref, c):
    first = ref[:, key_start(c) : key_start(c) + LANES]
    last = ref[:, ref.shape[1] - LANES :]
    return jnp.concatenate([first, last], axis=1)


def value_window(ref, c):
    stop = min(value_start(c) + 2 * LANES, ref.shape[1])
    return ref[:, value_start(c) : stop]


def scores_of(query, keys):
    return lax.dot_general(query, keys, (((1,), (1,)), ((), ())), preferred_element_type=f32)


def fetch(pairs, sems):
    copies = [pltpu.make_async_copy(a, b, sems.at[i]) for i, (a, b) in enumerate(pairs)]
    for copy in copies:
        copy.start()
    return copies


def piece(width, k):
    step = width // PIECES
    return slice(k * step, (k + 1) * step)


def pieces_of(rows, width, dtype):
    return tuple(jax.ShapeDtypeStruct((rows, width // PIECES), dtype) for _ in range(PIECES))


def joined(refs):
    return jnp.concatenate([ref[...] for ref in refs], axis=1)


def in_hbm(values):
    return [pltpu.with_memory_space_constraint(value, pltpu.HBM) for value in values]


def in_vmem(values):
    return [pltpu.with_memory_space_constraint(value, pltpu.VMEM) for value in values]


def prep_kernel(
    node_hbm, rank_hbm, length_hbm, root_hbm, pool_hbm, out_ref,
    node_ref, rank_ref, length_ref, root_ref, pool_ref, sems,
):
    pairs = (
        (pool_hbm, pool_ref),
        (node_hbm, node_ref),
        (rank_hbm, rank_ref),
        (length_hbm, length_ref),
        (root_hbm, root_ref),
    )
    pool_copy, *copies = fetch(pairs, sems)
    for copy in copies:
        copy.wait()
    pages, size, width = pool_ref.shape
    free = out_ref.shape[1] - width
    lane = lax.broadcasted_iota(i32, (size, free), 1)
    slot = lax.broadcasted_iota(i32, (size, free), 0)
    root = jnp.full((size, free), -2, i32)
    for m in range(MIDS):
        root = jnp.where(lane == m, root_ref[m], root)
    hidden = jnp.where(lane < MIDS, MASKED, 0.0)
    for p in range(pages):
        node = node_ref[p]
        left = length_ref[jnp.maximum(node, 0)] - size * rank_ref[p]
        seen = ((root == node) | (lane + ROOTS == node)) & (slot < left)
        rows = slice(p * size, (p + 1) * size)
        out_ref[rows, width:] = jnp.where(seen, 0.0, hidden).astype(bf16)
    pool_copy.wait()
    out_ref[:, :width] = pool_ref[...].reshape(pages * size, width)


def prepare(page_node, page_rank, node_length, mid_root, prefix_pool):
    pages, size, width = prefix_pool.shape
    tables = (page_node, page_rank, node_length, mid_root)
    return pl.pallas_call(
        prep_kernel,
        out_shape=jax.ShapeDtypeStruct((pages * size, padded(width + MIDS)), bf16),
        in_specs=[HBM] * 5,
        out_specs=VMEM,
        scratch_shapes=[pltpu.SMEM(t.shape, i32) for t in tables]
        + [pltpu.VMEM(prefix_pool.shape, bf16), pltpu.SemaphoreType.DMA((5,))],
        compiler_params=PARAMS,
        name="pool_rows",
    )(*in_hbm((*tables, prefix_pool)))


def half_start(rows, half):
    parity = lax.rem(lax.axis_index("tp"), 2)
    return (parity if half else 1 - parity) * (rows // 2)


def fold(scores, values, state):
    top = functools.reduce(jnp.maximum, [jnp.max(s, axis=1, keepdims=True) for s in scores])
    if state is not None:
        top = jnp.maximum(top, state[0])
    total, weighted = None, None
    for s, v in zip(scores, values):
        raised = jnp.exp2((s - top) * RATE)
        part = jnp.sum(raised, axis=1, keepdims=True)
        mixed = jnp.dot(raised.astype(bf16), v, preferred_element_type=f32)
        total = part if total is None else total + part
        weighted = mixed if weighted is None else weighted + mixed
    if state is not None:
        factor = jnp.exp2((state[0] - top) * RATE)
        total = total + state[1] * factor
        weighted = weighted + state[2] * factor
    return top, total, weighted


def pack(top, total, weighted):
    lane = lax.broadcasted_iota(i32, weighted.shape, 1)
    return jnp.where(lane == 0, top, jnp.where(lane == 1, total, weighted))


def unpack(state):
    return state[:, 0:1], state[:, 1:2], state


def local_kernel(
    count_hbm, mid_hbm, leaf_len_hbm, query_ref, keyval_ref, leaf_ref, *refs, chunks
):
    pool_refs = refs[:chunks]
    aug_ref, state_ref, count_ref, mid_ref, leaf_len_ref, sems = refs[chunks:]
    pairs = ((count_hbm, count_ref), (mid_hbm, mid_ref), (leaf_len_hbm, leaf_len_ref))
    for copy in fetch(pairs, sems):
        copy.wait()
    rows = query_ref.shape[0]
    part = rows // 2
    width = keyval_ref.shape[1]
    requests, slots, _ = leaf_ref.shape
    kv_local = width // (2 * HD)
    group = query_ref.shape[1] // (kv_local * HD)
    lane = lax.broadcasted_iota(i32, (part, LANES), 1)
    zero = jnp.zeros((part, LANES), i32)
    leaf_all = leaf_ref[...].reshape(requests * slots, width)
    leaf_at = lax.broadcasted_iota(i32, (part, requests * slots), 1)
    for half in range(2):
        first = half_start(rows, half)
        row = lax.broadcasted_iota(i32, (part, LANES), 0) + first
        start, low, high, mid = zero, zero, zero, zero
        begin = jnp.int32(0)
        for r in range(requests):
            here = row >= begin
            start = jnp.where(here, begin, start)
            low = jnp.where(here, r * slots, low)
            high = jnp.where(here, r * slots + leaf_len_ref[r], high)
            mid = jnp.where(here, mid_ref[r], mid)
            begin = begin + count_ref[0, r]
        chosen = jnp.where(lane == width % LANES + mid, 1.0, 0.0).astype(bf16)
        leaf_ok = (leaf_at >= low[:, 0:1]) & (leaf_at < high[:, 0:1])
        new_ok = (lane >= start) & (lane <= row)
        tokens = query_ref[pl.ds(pl.multiple_of(first, part), part), :]
        for c in range(kv_local):
            base = (half * kv_local + c) * group * part
            block = slice(base, base + group * part)
            key0, val0 = key_start(c), value_start(c)
            shift = key_shift(c)
            for g in range(group):
                h = c * group + g
                at = slice(base + g * part, base + (g + 1) * part)
                aug_ref[at, :LANES] = jnp.zeros((part, LANES), bf16)
                aug_ref[at, shift : shift + HD] = tokens[:, h * HD : (h + 1) * HD]
                aug_ref[at, LANES:] = chosen
            query = aug_ref[block, :]
            narrow = query[:, :LANES]
            s_leaf = scores_of(narrow, leaf_all[:, key0 : key0 + LANES])
            s_leaf = jnp.where(leaf_ok[None], s_leaf.reshape(group, part, -1), MASKED)
            s_new = scores_of(narrow, keyval_ref[:, key0 : key0 + LANES])
            s_new = jnp.where(new_ok[None], s_new.reshape(group, part, -1), MASKED)
            scores = [s_leaf.reshape(group * part, -1), s_new.reshape(group * part, -1)]
            stop = min(val0 + 2 * LANES, width)
            fill = val0 + 2 * LANES - stop
            values = [leaf_all[:, val0:stop], keyval_ref[:, val0:stop]]
            if fill:
                values = [
                    jnp.concatenate([v, jnp.zeros((v.shape[0], fill), bf16)], axis=1) for v in values
                ]
            for pool_ref in pool_refs:
                scores.append(scores_of(query, key_window(pool_ref, c)))
                values.append(value_window(pool_ref, c))
            state_ref[block, :] = pack(*fold(scores, values, None))


def start_attention(new_query, new_keyval, leaf, leaf_length, counts, request_mid, pools):
    rows, query_width = new_query.shape
    heads = query_width // HD
    tables = (counts, request_mid, leaf_length)
    keys = leaf.shape[0] * leaf.shape[1] + rows + sum(item.shape[0] for item in pools)
    return pl.pallas_call(
        functools.partial(local_kernel, chunks=len(pools)),
        out_shape=(
            jax.ShapeDtypeStruct((heads * rows, 2 * LANES), bf16),
            jax.ShapeDtypeStruct((heads * rows, 2 * LANES), f32),
        ),
        in_specs=[HBM] * 3 + [VMEM] * (3 + len(pools)),
        out_specs=(VMEM, VMEM),
        scratch_shapes=[pltpu.SMEM(t.shape, i32) for t in tables] + [pltpu.SemaphoreType.DMA((3,))],
        compiler_params=PARAMS,
        cost_estimate=attention_cost(heads * rows, keys),
        name="attend_local",
    )(*in_hbm(tables), new_query, new_keyval, leaf, *pools)


def attention_cost(rows, keys):
    return pl.CostEstimate(
        flops=8 * LANES * rows * keys, bytes_accessed=8 * rows * 2 * LANES, transcendentals=rows * keys
    )


def extended(query, state, pool_refs, c):
    scores = [scores_of(query, key_window(ref, c)) for ref in pool_refs]
    values = [value_window(ref, c) for ref in pool_refs]
    return fold(scores, values, unpack(state))


def chunk_kernel(*refs, blocks):
    aug_ref, state_ref = refs[:2]
    pool_refs, out_ref = refs[2:-1], refs[-1]
    size = aug_ref.shape[0] // blocks
    for b in range(blocks):
        at = slice(b * size, (b + 1) * size)
        state = extended(aug_ref[at, :], state_ref[at, :], pool_refs, b % (blocks // 2))
        out_ref[at, :] = pack(*state)


def extend_attention(aug, state, pools, kv_local):
    keys = sum(item.shape[0] for item in pools)
    return pl.pallas_call(
        functools.partial(chunk_kernel, blocks=2 * kv_local),
        out_shape=jax.ShapeDtypeStruct(state.shape, f32),
        in_specs=[VMEM] * (2 + len(pools)),
        out_specs=VMEM,
        compiler_params=PARAMS,
        cost_estimate=attention_cost(aug.shape[0], keys),
        name="attend_pages",
    )(aug, state, *pools)


def project(out_refs, rows, weight_ref, places):
    for out_ref, k in zip(out_refs, places):
        weight = weight_ref[:, piece(weight_ref.shape[1], k)]
        result = jnp.dot(rows, weight, preferred_element_type=f32)
        out_ref[...] = result.astype(out_ref.dtype)


def finish_kernel(*refs, half, kv_local, chunks, width):
    aug_ref, state_ref = refs[:2]
    pool_refs = refs[2 : 2 + chunks]
    weight_ref = refs[2 + chunks]
    part = aug_ref.shape[0] // (2 * width // HD)
    rest = refs[3 + chunks :]
    att_ref, *proj_refs, mine_ref = rest[2 * half :]
    if half:
        send_refs, proj_refs = proj_refs[: PIECES - 1], proj_refs[PIECES - 1 :]
        proj_refs, res_refs = proj_refs[:PIECES], proj_refs[PIECES:]
        project(send_refs, rest[0][...], weight_ref, range(1, PIECES))
    group = width // (kv_local * HD)
    size = group * part
    for c in range(kv_local):
        at = slice((half * kv_local + c) * size, (half * kv_local + c + 1) * size)
        if chunks:
            state = extended(aug_ref[at, :], state_ref[at, :], pool_refs, c)
        else:
            state = unpack(state_ref[at, :])
        shift = value_shift(c)
        result = (state[2][:, shift : shift + HD] / state[1]).astype(bf16)
        for g in range(group):
            h = c * group + g
            mine_ref[:, h * HD : (h + 1) * HD] = result[g * part : (g + 1) * part]
    if half:
        mine = pl.multiple_of(half_start(2 * part, 1), part)
        theirs = pl.multiple_of(half_start(2 * part, 0), part)
        att_ref[pl.ds(mine, part), :] = mine_ref[...]
        att_ref[pl.ds(theirs, part), :] = rest[0][...]
        for k, res_ref in enumerate(res_refs):
            res_ref[...] = rest[1][pl.ds(mine, part), piece(rest[1].shape[1], k)]
    else:
        att_ref[...] = mine_ref[...]
    project(proj_refs, mine_ref[...], weight_ref, range(PIECES if half else 1))


def finish_attention(aug, state, pools, out_weight, half, kv_local, rows, other):
    width = out_weight.shape[0]
    part = rows // 2
    keys = sum(item.shape[0] for item in pools)
    depth = out_weight.shape[1]
    sent = pieces_of(part, depth, bf16)
    if half:
        shapes = (*sent[:-1], *pieces_of(part, depth, f32), *pieces_of(part, depth, bf16))
    else:
        shapes = sent[-1:]
    return pl.pallas_call(
        functools.partial(
            finish_kernel, half=half, kv_local=kv_local, chunks=len(pools), width=width
        ),
        out_shape=(jax.ShapeDtypeStruct((rows if half else part, width), bf16), *shapes),
        in_specs=[VMEM] * (3 + len(pools) + len(other)),
        out_specs=(VMEM,) * (1 + len(shapes)),
        scratch_shapes=[pltpu.VMEM((part, width), bf16)],
        compiler_params=PARAMS,
        cost_estimate=attention_cost(aug.shape[0] // 2, keys + 512),
        name="attend_finish",
    )(aug, state, *pools, out_weight, *other)


def normalized(values_in, gain):
    values = values_in.astype(f32)
    scale = lax.rsqrt(jnp.mean(values * values, axis=-1, keepdims=True) + EPSILON)
    return (values * scale * gain.astype(f32)).astype(bf16)


def stage_kernel(*refs):
    count = len(refs) // 2
    for copy in fetch(zip(refs[:count], refs[count : 2 * count]), refs[-1]):
        copy.wait()


def stage(weights):
    return pl.pallas_call(
        stage_kernel,
        out_shape=tuple(pltpu.VMEM(w.shape, w.dtype) for w in weights),
        in_specs=[HBM] * len(weights),
        out_specs=(VMEM,) * len(weights),
        scratch_shapes=[pltpu.SemaphoreType.DMA((len(weights),))],
        compiler_params=pltpu.CompilerParams(vmem_limit_bytes=1024 * 1024),
        cost_estimate=pl.CostEstimate(
            flops=0, bytes_accessed=sum(2 * w.size for w in weights), transcendentals=0
        ),
        name="stage",
    )(*in_hbm(weights))


def mlp_kernel(*refs, second):
    row_refs, (gain_ref, gate_ref, up_ref, down_ref) = refs[:PIECES], refs[PIECES : PIECES + 4]
    refs = refs[PIECES + 4 :]
    if second:
        project(refs[1:PIECES], refs[0][...], down_ref, range(PIECES - 1))
    normed = normalized(joined(row_refs), gain_ref[...])
    gate = jnp.dot(normed, gate_ref[...], preferred_element_type=f32)
    upward = jnp.dot(normed, up_ref[...], preferred_element_type=f32)
    hidden = (jax.nn.silu(gate) * upward).astype(bf16)
    if second:
        project(refs[PIECES:], hidden, down_ref, range(PIECES))
    else:
        refs[0][...] = hidden
        project(refs[1:], hidden, down_ref, [PIECES - 1])


def feed_forward(rows, gain, gate_weight, up_weight, down_weight, other=()):
    count = rows[0].shape[0]
    depth, width = gate_weight.shape
    sent = pieces_of(count, depth, bf16)
    if other:
        shapes = (*sent[:-1], *pieces_of(count, depth, f32))
    else:
        shapes = (jax.ShapeDtypeStruct((count, width), bf16), sent[-1])
    return pl.pallas_call(
        functools.partial(mlp_kernel, second=len(other) > 0),
        out_shape=shapes,
        in_specs=[VMEM] * (PIECES + 4 + len(other)),
        out_specs=(VMEM,) * len(shapes),
        compiler_params=PARAMS,
        cost_estimate=pl.CostEstimate(
            flops=6 * count * depth * width, bytes_accessed=6 * depth * width, transcendentals=0
        ),
        name="feed_forward",
    )(*rows, gain.reshape(1, depth), *in_vmem((gate_weight, up_weight, down_weight)), *other)


def next_kernel(*refs, half):
    row_refs, refs = refs[:PIECES], refs[PIECES:]
    gain_ref, query_ref, keyval_ref = refs[:3]
    rows = joined(row_refs)
    normed = normalized(rows, gain_ref[...])
    query = jnp.dot(normed, query_ref[...], preferred_element_type=f32).astype(bf16)
    keyval = scores_of(keyval_ref[...], normed).astype(bf16)
    if not half:
        query_out, keyval_out = refs[3:]
        query_out[...] = query
        keyval_out[...] = keyval
        return
    query_in, keyval_in = refs[3:5]
    query_out, keyval_out, residual_out = refs[5 + PIECES :]
    part = query.shape[0]
    mine = pl.multiple_of(half_start(2 * part, 1), part)
    theirs = pl.multiple_of(half_start(2 * part, 0), part)
    query_out[pl.ds(mine, part), :] = query
    query_out[pl.ds(theirs, part), :] = query_in[...]

    @pl.when(mine == 0)
    def _():
        keyval_out[:, :part] = keyval
        keyval_out[:, part:] = keyval_in[...]

    @pl.when(mine != 0)
    def _():
        keyval_out[:, :part] = keyval_in[...]
        keyval_out[:, part:] = keyval

    share = residual_out.shape[0]
    place = lax.axis_index("tp") * share
    at = pl.multiple_of(lax.rem(place, part), share)
    held = (place >= mine) & (place < mine + part)
    for k in range(PIECES):
        ours = row_refs[k][pl.ds(at, share), :]
        others = refs[5 + k][pl.ds(at, share), :]
        residual_out[:, piece(rows.shape[1], k)] = jnp.where(held, ours, others)


def next_projections(rows, gain, query_weight, keyval_weight, other):
    count = rows[0].shape[0]
    depth = query_weight.shape[0]
    widths = (query_weight.shape[1], keyval_weight.shape[0])
    half = len(other) > 0
    out_rows = 2 * count if half else count
    shapes = [(out_rows, widths[0]), (widths[1], out_rows)]
    if half:
        shapes.append((out_rows // lax.axis_size("tp"), depth))
    return pl.pallas_call(
        functools.partial(next_kernel, half=half),
        out_shape=tuple(jax.ShapeDtypeStruct(shape, bf16) for shape in shapes),
        in_specs=[VMEM] * (PIECES + 3 + len(other)),
        out_specs=(VMEM,) * len(shapes),
        compiler_params=PARAMS,
        cost_estimate=pl.CostEstimate(
            flops=2 * count * depth * sum(widths),
            bytes_accessed=2 * depth * sum(widths),
            transcendentals=0,
        ),
        name="next_layer",
    )(*rows, gain.reshape(1, depth), *in_vmem([query_weight]), keyval_weight, *other)


def trade(value, axis, bit):
    size = lax.axis_size(axis)
    return lax.ppermute(value, axis, [(i, i ^ bit) for i in range(size)])


def cross(value, even_bit, odd_bit):
    size = lax.axis_size("req")
    pairs = [(i, i ^ (odd_bit if i % 2 else even_bit)) for i in range(size)]
    return lax.ppermute(value, "req", pairs)


def trades(values, bit):
    return [trade(value, "tp", bit) for value in values]


def each(join, *pieces):
    return [join(*items) for items in zip(*pieces)]


def add_pair(mine, got):
    return (mine + wide(got)).astype(bf16)


def pairs_in_turn(mine, got, weights):
    last = add_pair(mine[-1], got[-1])
    _, rest, weights = lax.optimization_barrier((last, got[:-1], weights))
    return [*each(add_pair, mine[:-1], rest), last], weights


def add_rows(pair, rows, got):
    return (wide(rows) + (wide(pair) + wide(got))).astype(bf16)


def wide(value):
    return value.astype(f32)


def per_device(
    new_query,
    new_keyval,
    residual_in,
    leaf_cache,
    leaf_length,
    new_counts,
    request_mid,
    mid_root,
    node_length,
    prefix_pool,
    page_node,
    page_rank,
    out_weight,
    norm_gain,
    gate_weight,
    up_weight,
    down_weight,
    next_gain,
    query_weight,
    keyval_weight,
):
    rows = new_query.shape[0]
    part = rows // 2
    kv_local = new_keyval.shape[1] // (2 * HD)
    pool = prepare(page_node, page_rank, node_length, mid_root, prefix_pool)
    local_args = (new_query, new_keyval, leaf_cache, leaf_length, new_counts, request_mid)
    if lax.axis_size("req") == 8:
        first = cross(pool, 2, 4)
        second = cross(pool, 4, 2)
        beside = trade(pool, "req", 1)
        aug, state = start_attention(*local_args, [pool, beside])
        first, aug, state = lax.optimization_barrier((first, aug, state))
        corner = cross(first, 4, 2)
        first, second = lax.optimization_barrier((first, second))
        near = [first, second, trade(first, "req", 1), trade(second, "req", 1)]
        state = extend_attention(aug, state, near, kv_local)
        state, down_weight = lax.optimization_barrier((state, down_weight))
        corner, state, down_weight = lax.optimization_barrier(
            (corner, state, *stage([down_weight]))
        )
        corner_other = trade(corner, "req", 1)
        state = extend_attention(aug, state, [corner], kv_local)
        pools = [corner_other]
    else:
        every = lax.all_gather(pool, "req", axis=0)
        holders = every.shape[0]
        aug, state = start_attention(*local_args, [pool])
        places = (lax.axis_index("req") + 1 + jnp.arange(holders - 1)) % holders
        step = 4
        for i in range(0, holders - 1, step):
            chunk = every[places[i : i + step]].reshape(-1, pool.shape[1])
            state = extend_attention(aug, state, [chunk], kv_local)
        pools = []

    theirs_att, *theirs_proj = finish_attention(
        aug, state, pools, out_weight, 0, kv_local, rows, ()
    )
    attention, *mine_proj = finish_attention(
        aug, state, pools, out_weight, 1, kv_local, rows, (theirs_att, residual_in)
    )
    theirs_proj = theirs_proj + mine_proj[: PIECES - 1]
    mine_proj, res_mine = mine_proj[PIECES - 1 : -PIECES], mine_proj[-PIECES:]

    mine = half_start(rows, 1)
    theirs = half_start(rows, 0)
    depth = residual_in.shape[1]
    if lax.axis_size("tp") == 4:
        got = trades(theirs_proj, 1)
        pair, (gate_weight, up_weight) = pairs_in_turn(
            mine_proj[::-1], got[::-1], (gate_weight, up_weight)
        )
        pair = pair[::-1]
        got = trades(pair, 2)
        got[-1], *staged = lax.optimization_barrier((got[-1], *stage([gate_weight, up_weight])))
        mlp = (*staged, down_weight)
        mixed_mine = each(add_rows, pair, res_mine, got)
        mixed_theirs = trades(mixed_mine, 1)
        hidden, last = feed_forward(mixed_mine, norm_gain, *mlp)
        last = trade(last, "tp", 1)
        result = feed_forward(mixed_theirs, norm_gain, *mlp, [hidden])
        got = [*trades(result[: PIECES - 1], 1), last]
        mlp_theirs = result[PIECES - 1 :]
        pair, (query_weight,) = pairs_in_turn(mlp_theirs, got, (query_weight,))
        got = trades(pair, 2)
        got[-1], query_weight = lax.optimization_barrier((got[-1], *stage([query_weight])))
        layer_theirs = each(add_rows, pair, mixed_theirs, got)
        layer_mine = trades(layer_theirs, 1)
    else:
        res_mine = jnp.concatenate(res_mine, axis=1)
        res_theirs = lax.dynamic_slice_in_dim(residual_in, theirs, part, 0)

        def in_order(theirs_part, mine_part):
            both = jnp.stack([theirs_part, mine_part])
            return jnp.where(mine == 0, both[::-1], both).reshape(rows, -1)

        theirs_proj = jnp.concatenate([wide(item) for item in theirs_proj], axis=1)
        mine_proj = jnp.concatenate(mine_proj, axis=1)
        total = lax.psum(in_order(theirs_proj, mine_proj), "tp")
        mixed = (wide(in_order(res_theirs, res_mine)) + total).astype(bf16)
        mixed_halves = [
            [mixed[h * part : (h + 1) * part, piece(depth, k)] for k in range(PIECES)]
            for h in range(2)
        ]
        mlp_weights = (gate_weight, up_weight, down_weight)
        hidden, last = feed_forward(mixed_halves[0], norm_gain, *mlp_weights)
        result = feed_forward(mixed_halves[1], norm_gain, *mlp_weights, [hidden])
        halves = [[*result[: PIECES - 1], last], result[PIECES - 1 :]]
        mlp = [jnp.concatenate([wide(item) for item in half], axis=1) for half in halves]
        mlp = lax.psum(jnp.concatenate(mlp, axis=0), "tp")
        layer = (wide(mixed) + mlp).astype(bf16)
        layer = [layer[:, piece(depth, k)] for k in range(PIECES)]
        layer_mine = [lax.dynamic_slice_in_dim(item, mine, part, 0) for item in layer]
        layer_theirs = [lax.dynamic_slice_in_dim(item, theirs, part, 0) for item in layer]
    weights = (next_gain, query_weight, keyval_weight.T)
    other = next_projections(layer_theirs, *weights, ())
    next_query, next_keyval, residual_out = next_projections(
        layer_mine, *weights, (*other, *layer_theirs)
    )
    return (attention, residual_out, next_query, next_keyval.T)


def solution(mesh):
    in_specs = (
        P("req", "tp"),
        P("req", "tp"),
        P("req", None),
        P("req", None, "tp"),
        P("req"),
        P("req", None),
        P("req"),
        P(),
        P(),
        P("req", None, "tp"),
        P("req"),
        P("req"),
        P("tp", None),
        P(),
        P(None, "tp"),
        P(None, "tp"),
        P("tp", None),
        P(),
        P(None, "tp"),
        P(None, "tp"),
    )
    out_specs = (P("req", "tp"), P(("req", "tp"), None), P("req", "tp"), P("req", "tp"))
    return jax.shard_map(
        per_device, mesh=mesh, in_specs=in_specs, out_specs=out_specs, check_vma=False
    )
```

```python
import functools
import math

import jax
import jax.numpy as jnp
from jax import lax
from jax.experimental import pallas as pl
from jax.experimental.pallas import tpu as pltpu
from jax.sharding import PartitionSpec as P

HD = 80
ROOTS = 2
MIDS = 6
LANES = 128
MASKED = -1e30
EPSILON = 1e-05
RATE = math.log2(math.e) / math.sqrt(HD)

PIECES = 2

bf16 = jnp.bfloat16
f32 = jnp.float32
i32 = jnp.int32
HBM = pl.BlockSpec(memory_space=pltpu.HBM)
VMEM = pl.BlockSpec(memory_space=pltpu.VMEM)
SMEM = pl.BlockSpec(memory_space=pltpu.SMEM)
PARAMS = pltpu.CompilerParams(vmem_limit_bytes=24 * 1024 * 1024)


def padded(width):
    return -(-width // LANES) * LANES


def key_start(c):
    return c * 2 * HD // LANES * LANES


def key_shift(c):
    return c * 2 * HD % LANES


def value_start(c):
    return (c * 2 * HD + HD) // LANES * LANES


def value_shift(c):
    return (c * 2 * HD + HD) % LANES


def key_window(ref, c):
    first = ref[:, key_start(c) : key_start(c) + LANES]
    last = ref[:, ref.shape[1] - LANES :]
    return jnp.concatenate([first, last], axis=1)


def value_window(ref, c):
    stop = min(value_start(c) + 2 * LANES, ref.shape[1])
    return ref[:, value_start(c) : stop]


def scores_of(query, keys):
    return lax.dot_general(query, keys, (((1,), (1,)), ((), ())), preferred_element_type=f32)


def fetch(pairs, sems):
    copies = [pltpu.make_async_copy(a, b, sems.at[i]) for i, (a, b) in enumerate(pairs)]
    for copy in copies:
        copy.start()
    return copies


def piece(width, k):
    step = width // PIECES
    return slice(k * step, (k + 1) * step)


def pieces_of(rows, width, dtype):
    return tuple(jax.ShapeDtypeStruct((rows, width // PIECES), dtype) for _ in range(PIECES))


def joined(refs):
    return jnp.concatenate([ref[...] for ref in refs], axis=1)


def in_hbm(values):
    return [pltpu.with_memory_space_constraint(value, pltpu.HBM) for value in values]


def in_vmem(values):
    return [pltpu.with_memory_space_constraint(value, pltpu.VMEM) for value in values]


def prep_kernel(
    node_hbm, rank_hbm, length_hbm, root_hbm, pool_hbm, out_ref,
    node_ref, rank_ref, length_ref, root_ref, pool_ref, sems,
):
    pairs = (
        (pool_hbm, pool_ref),
        (node_hbm, node_ref),
        (rank_hbm, rank_ref),
        (length_hbm, length_ref),
        (root_hbm, root_ref),
    )
    pool_copy, *copies = fetch(pairs, sems)
    for copy in copies:
        copy.wait()
    pages, size, width = pool_ref.shape
    free = out_ref.shape[1] - width
    lane = lax.broadcasted_iota(i32, (size, free), 1)
    slot = lax.broadcasted_iota(i32, (size, free), 0)
    root = jnp.full((size, free), -2, i32)
    for m in range(MIDS):
        root = jnp.where(lane == m, root_ref[m], root)
    hidden = jnp.where(lane < MIDS, MASKED, 0.0)
    for p in range(pages):
        node = node_ref[p]
        left = length_ref[jnp.maximum(node, 0)] - size * rank_ref[p]
        seen = ((root == node) | (lane + ROOTS == node)) & (slot < left)
        rows = slice(p * size, (p + 1) * size)
        out_ref[rows, width:] = jnp.where(seen, 0.0, hidden).astype(bf16)
    pool_copy.wait()
    out_ref[:, :width] = pool_ref[...].reshape(pages * size, width)


def prepare(page_node, page_rank, node_length, mid_root, prefix_pool):
    pages, size, width = prefix_pool.shape
    tables = (page_node, page_rank, node_length, mid_root)
    return pl.pallas_call(
        prep_kernel,
        out_shape=jax.ShapeDtypeStruct((pages * size, padded(width + MIDS)), bf16),
        in_specs=[HBM] * 5,
        out_specs=VMEM,
        scratch_shapes=[pltpu.SMEM(t.shape, i32) for t in tables]
        + [pltpu.VMEM(prefix_pool.shape, bf16), pltpu.SemaphoreType.DMA((5,))],
        compiler_params=PARAMS,
        name="pool_rows",
    )(*in_hbm((*tables, prefix_pool)))


def half_start(rows, half):
    parity = lax.rem(lax.axis_index("tp"), 2)
    return (parity if half else 1 - parity) * (rows // 2)


def fold(scores, values, state):
    top = functools.reduce(jnp.maximum, [jnp.max(s, axis=1, keepdims=True) for s in scores])
    if state is not None:
        top = jnp.maximum(top, state[0])
    total, weighted = None, None
    for s, v in zip(scores, values):
        raised = jnp.exp2((s - top) * RATE)
        part = jnp.sum(raised, axis=1, keepdims=True)
        mixed = jnp.dot(raised.astype(bf16), v, preferred_element_type=f32)
        total = part if total is None else total + part
        weighted = mixed if weighted is None else weighted + mixed
    if state is not None:
        factor = jnp.exp2((state[0] - top) * RATE)
        total = total + state[1] * factor
        weighted = weighted + state[2] * factor
    return top, total, weighted


def pack(top, total, weighted):
    lane = lax.broadcasted_iota(i32, weighted.shape, 1)
    return jnp.where(lane == 0, top, jnp.where(lane == 1, total, weighted))


def unpack(state):
    return state[:, 0:1], state[:, 1:2], state


def local_kernel(
    count_hbm, mid_hbm, leaf_len_hbm, query_ref, keyval_ref, leaf_ref, *refs, chunks
):
    pool_refs = refs[:chunks]
    aug_ref, state_ref, count_ref, mid_ref, leaf_len_ref, sems = refs[chunks:]
    pairs = ((count_hbm, count_ref), (mid_hbm, mid_ref), (leaf_len_hbm, leaf_len_ref))
    for copy in fetch(pairs, sems):
        copy.wait()
    rows = query_ref.shape[0]
    part = rows // 2
    width = keyval_ref.shape[1]
    requests, slots, _ = leaf_ref.shape
    kv_local = width // (2 * HD)
    group = query_ref.shape[1] // (kv_local * HD)
    lane = lax.broadcasted_iota(i32, (part, LANES), 1)
    zero = jnp.zeros((part, LANES), i32)
    leaf_all = leaf_ref[...].reshape(requests * slots, width)
    leaf_at = lax.broadcasted_iota(i32, (part, requests * slots), 1)
    for half in range(2):
        first = half_start(rows, half)
        row = lax.broadcasted_iota(i32, (part, LANES), 0) + first
        start, low, high, mid = zero, zero, zero, zero
        begin = jnp.int32(0)
        for r in range(requests):
            here = row >= begin
            start = jnp.where(here, begin, start)
            low = jnp.where(here, r * slots, low)
            high = jnp.where(here, r * slots + leaf_len_ref[r], high)
            mid = jnp.where(here, mid_ref[r], mid)
            begin = begin + count_ref[0, r]
        chosen = jnp.where(lane == width % LANES + mid, 1.0, 0.0).astype(bf16)
        leaf_ok = (leaf_at >= low[:, 0:1]) & (leaf_at < high[:, 0:1])
        new_ok = (lane >= start) & (lane <= row)
        tokens = query_ref[pl.ds(pl.multiple_of(first, part), part), :]
        for c in range(kv_local):
            base = (half * kv_local + c) * group * part
            block = slice(base, base + group * part)
            key0, val0 = key_start(c), value_start(c)
            shift = key_shift(c)
            for g in range(group):
                h = c * group + g
                at = slice(base + g * part, base + (g + 1) * part)
                aug_ref[at, :LANES] = jnp.zeros((part, LANES), bf16)
                aug_ref[at, shift : shift + HD] = tokens[:, h * HD : (h + 1) * HD]
                aug_ref[at, LANES:] = chosen
            query = aug_ref[block, :]
            narrow = query[:, :LANES]
            s_leaf = scores_of(narrow, leaf_all[:, key0 : key0 + LANES])
            s_leaf = jnp.where(leaf_ok[None], s_leaf.reshape(group, part, -1), MASKED)
            s_new = scores_of(narrow, keyval_ref[:, key0 : key0 + LANES])
            s_new = jnp.where(new_ok[None], s_new.reshape(group, part, -1), MASKED)
            scores = [s_leaf.reshape(group * part, -1), s_new.reshape(group * part, -1)]
            stop = min(val0 + 2 * LANES, width)
            fill = val0 + 2 * LANES - stop
            values = [leaf_all[:, val0:stop], keyval_ref[:, val0:stop]]
            if fill:
                values = [
                    jnp.concatenate([v, jnp.zeros((v.shape[0], fill), bf16)], axis=1) for v in values
                ]
            for pool_ref in pool_refs:
                scores.append(scores_of(query, key_window(pool_ref, c)))
                values.append(value_window(pool_ref, c))
            state_ref[block, :] = pack(*fold(scores, values, None))


def start_attention(new_query, new_keyval, leaf, leaf_length, counts, request_mid, pools):
    rows, query_width = new_query.shape
    heads = query_width // HD
    tables = (counts, request_mid, leaf_length)
    keys = leaf.shape[0] * leaf.shape[1] + rows + sum(item.shape[0] for item in pools)
    return pl.pallas_call(
        functools.partial(local_kernel, chunks=len(pools)),
        out_shape=(
            jax.ShapeDtypeStruct((heads * rows, 2 * LANES), bf16),
            jax.ShapeDtypeStruct((heads * rows, 2 * LANES), f32),
        ),
        in_specs=[HBM] * 3 + [VMEM] * (3 + len(pools)),
        out_specs=(VMEM, VMEM),
        scratch_shapes=[pltpu.SMEM(t.shape, i32) for t in tables] + [pltpu.SemaphoreType.DMA((3,))],
        compiler_params=PARAMS,
        cost_estimate=attention_cost(heads * rows, keys),
        name="attend_local",
    )(*in_hbm(tables), new_query, new_keyval, leaf, *pools)


def attention_cost(rows, keys):
    return pl.CostEstimate(
        flops=8 * LANES * rows * keys, bytes_accessed=8 * rows * 2 * LANES, transcendentals=rows * keys
    )


def extended(query, state, pool_refs, c):
    scores = [scores_of(query, key_window(ref, c)) for ref in pool_refs]
    values = [value_window(ref, c) for ref in pool_refs]
    return fold(scores, values, unpack(state))


def chunk_kernel(*refs, blocks):
    aug_ref, state_ref = refs[:2]
    pool_refs, out_ref = refs[2:-1], refs[-1]
    size = aug_ref.shape[0] // blocks
    for b in range(blocks):
        at = slice(b * size, (b + 1) * size)
        state = extended(aug_ref[at, :], state_ref[at, :], pool_refs, b % (blocks // 2))
        out_ref[at, :] = pack(*state)


def extend_attention(aug, state, pools, kv_local):
    keys = sum(item.shape[0] for item in pools)
    return pl.pallas_call(
        functools.partial(chunk_kernel, blocks=2 * kv_local),
        out_shape=jax.ShapeDtypeStruct(state.shape, f32),
        in_specs=[VMEM] * (2 + len(pools)),
        out_specs=VMEM,
        compiler_params=PARAMS,
        cost_estimate=attention_cost(aug.shape[0], keys),
        name="attend_pages",
    )(aug, state, *pools)


def project(out_refs, rows, weight_ref, places):
    for out_ref, k in zip(out_refs, places):
        weight = weight_ref[:, piece(weight_ref.shape[1], k)]
        result = jnp.dot(rows, weight, preferred_element_type=f32)
        out_ref[...] = result.astype(out_ref.dtype)


def finish_kernel(*refs, half, kv_local, chunks, width):
    aug_ref, state_ref = refs[:2]
    pool_refs = refs[2 : 2 + chunks]
    weight_ref = refs[2 + chunks]
    part = aug_ref.shape[0] // (2 * width // HD)
    rest = refs[3 + chunks :]
    att_ref, *proj_refs, mine_ref = rest[2 * half :]
    if half:
        send_refs, proj_refs = proj_refs[: PIECES - 1], proj_refs[PIECES - 1 :]
        proj_refs, res_refs = proj_refs[:PIECES], proj_refs[PIECES:]
        project(send_refs, rest[0][...], weight_ref, range(1, PIECES))
    group = width // (kv_local * HD)
    size = group * part
    for c in range(kv_local):
        at = slice((half * kv_local + c) * size, (half * kv_local + c + 1) * size)
        if chunks:
            state = extended(aug_ref[at, :], state_ref[at, :], pool_refs, c)
        else:
            state = unpack(state_ref[at, :])
        shift = value_shift(c)
        result = (state[2][:, shift : shift + HD] / state[1]).astype(bf16)
        for g in range(group):
            h = c * group + g
            mine_ref[:, h * HD : (h + 1) * HD] = result[g * part : (g + 1) * part]
    if half:
        mine = pl.multiple_of(half_start(2 * part, 1), part)
        theirs = pl.multiple_of(half_start(2 * part, 0), part)
        att_ref[pl.ds(mine, part), :] = mine_ref[...]
        att_ref[pl.ds(theirs, part), :] = rest[0][...]
        for k, res_ref in enumerate(res_refs):
            res_ref[...] = rest[1][pl.ds(mine, part), piece(rest[1].shape[1], k)]
    else:
        att_ref[...] = mine_ref[...]
    project(proj_refs, mine_ref[...], weight_ref, range(PIECES if half else 1))


def finish_attention(aug, state, pools, out_weight, half, kv_local, rows, other):
    width = out_weight.shape[0]
    part = rows // 2
    keys = sum(item.shape[0] for item in pools)
    depth = out_weight.shape[1]
    sent = pieces_of(part, depth, bf16)
    if half:
        shapes = (*sent[:-1], *pieces_of(part, depth, f32), *pieces_of(part, depth, bf16))
    else:
        shapes = sent[-1:]
    return pl.pallas_call(
        functools.partial(
            finish_kernel, half=half, kv_local=kv_local, chunks=len(pools), width=width
        ),
        out_shape=(jax.ShapeDtypeStruct((rows if half else part, width), bf16), *shapes),
        in_specs=[VMEM] * (3 + len(pools) + len(other)),
        out_specs=(VMEM,) * (1 + len(shapes)),
        scratch_shapes=[pltpu.VMEM((part, width), bf16)],
        compiler_params=PARAMS,
        cost_estimate=attention_cost(aug.shape[0] // 2, keys + 512),
        name="attend_finish",
    )(aug, state, *pools, out_weight, *other)


def normalized(values_in, gain):
    values = values_in.astype(f32)
    scale = lax.rsqrt(jnp.mean(values * values, axis=-1, keepdims=True) + EPSILON)
    return (values * scale * gain.astype(f32)).astype(bf16)


def stage_kernel(*refs):
    count = len(refs) // 2
    for copy in fetch(zip(refs[:count], refs[count : 2 * count]), refs[-1]):
        copy.wait()


def stage(weights):
    return pl.pallas_call(
        stage_kernel,
        out_shape=tuple(pltpu.VMEM(w.shape, w.dtype) for w in weights),
        in_specs=[HBM] * len(weights),
        out_specs=(VMEM,) * len(weights),
        scratch_shapes=[pltpu.SemaphoreType.DMA((len(weights),))],
        compiler_params=pltpu.CompilerParams(vmem_limit_bytes=1024 * 1024),
        cost_estimate=pl.CostEstimate(
            flops=0, bytes_accessed=sum(2 * w.size for w in weights), transcendentals=0
        ),
        name="stage",
    )(*in_hbm(weights))


def mlp_kernel(*refs, second):
    row_refs, (gain_ref, gate_ref, up_ref, down_ref) = refs[:PIECES], refs[PIECES : PIECES + 4]
    refs = refs[PIECES + 4 :]
    if second:
        project(refs[1:PIECES], refs[0][...], down_ref, range(PIECES - 1))
    normed = normalized(joined(row_refs), gain_ref[...])
    gate = jnp.dot(normed, gate_ref[...], preferred_element_type=f32)
    upward = jnp.dot(normed, up_ref[...], preferred_element_type=f32)
    hidden = (jax.nn.silu(gate) * upward).astype(bf16)
    if second:
        project(refs[PIECES:], hidden, down_ref, range(PIECES))
    else:
        refs[0][...] = hidden
        project(refs[1:], hidden, down_ref, [PIECES - 1])


def feed_forward(rows, gain, gate_weight, up_weight, down_weight, other=()):
    count = rows[0].shape[0]
    depth, width = gate_weight.shape
    sent = pieces_of(count, depth, bf16)
    if other:
        shapes = (*sent[:-1], *pieces_of(count, depth, f32))
    else:
        shapes = (jax.ShapeDtypeStruct((count, width), bf16), sent[-1])
    return pl.pallas_call(
        functools.partial(mlp_kernel, second=len(other) > 0),
        out_shape=shapes,
        in_specs=[VMEM] * (PIECES + 4 + len(other)),
        out_specs=(VMEM,) * len(shapes),
        compiler_params=PARAMS,
        cost_estimate=pl.CostEstimate(
            flops=6 * count * depth * width, bytes_accessed=6 * depth * width, transcendentals=0
        ),
        name="feed_forward",
    )(*rows, gain.reshape(1, depth), *in_vmem((gate_weight, up_weight, down_weight)), *other)


def next_kernel(*refs, half):
    row_refs, refs = refs[:PIECES], refs[PIECES:]
    gain_ref, query_ref, keyval_ref = refs[:3]
    rows = joined(row_refs)
    normed = normalized(rows, gain_ref[...])
    query = jnp.dot(normed, query_ref[...], preferred_element_type=f32).astype(bf16)
    keyval = scores_of(keyval_ref[...], normed).astype(bf16)
    if not half:
        query_out, keyval_out = refs[3:]
        query_out[...] = query
        keyval_out[...] = keyval
        return
    query_in, keyval_in = refs[3:5]
    query_out, keyval_out, residual_out = refs[5 + PIECES :]
    part = query.shape[0]
    mine = pl.multiple_of(half_start(2 * part, 1), part)
    theirs = pl.multiple_of(half_start(2 * part, 0), part)
    query_out[pl.ds(mine, part), :] = query
    query_out[pl.ds(theirs, part), :] = query_in[...]

    @pl.when(mine == 0)
    def _():
        keyval_out[:, :part] = keyval
        keyval_out[:, part:] = keyval_in[...]

    @pl.when(mine != 0)
    def _():
        keyval_out[:, :part] = keyval_in[...]
        keyval_out[:, part:] = keyval

    share = residual_out.shape[0]
    place = lax.axis_index("tp") * share
    at = pl.multiple_of(lax.rem(place, part), share)
    held = (place >= mine) & (place < mine + part)
    for k in range(PIECES):
        ours = row_refs[k][pl.ds(at, share), :]
        others = refs[5 + k][pl.ds(at, share), :]
        residual_out[:, piece(rows.shape[1], k)] = jnp.where(held, ours, others)


def next_projections(rows, gain, query_weight, keyval_weight, other):
    count = rows[0].shape[0]
    depth = query_weight.shape[0]
    widths = (query_weight.shape[1], keyval_weight.shape[0])
    half = len(other) > 0
    out_rows = 2 * count if half else count
    shapes = [(out_rows, widths[0]), (widths[1], out_rows)]
    if half:
        shapes.append((out_rows // lax.axis_size("tp"), depth))
    return pl.pallas_call(
        functools.partial(next_kernel, half=half),
        out_shape=tuple(jax.ShapeDtypeStruct(shape, bf16) for shape in shapes),
        in_specs=[VMEM] * (PIECES + 3 + len(other)),
        out_specs=(VMEM,) * len(shapes),
        compiler_params=PARAMS,
        cost_estimate=pl.CostEstimate(
            flops=2 * count * depth * sum(widths),
            bytes_accessed=2 * depth * sum(widths),
            transcendentals=0,
        ),
        name="next_layer",
    )(*rows, gain.reshape(1, depth), *in_vmem([query_weight]), keyval_weight, *other)


def trade(value, axis, bit):
    size = lax.axis_size(axis)
    return lax.ppermute(value, axis, [(i, i ^ bit) for i in range(size)])


def cross(value, even_bit, odd_bit):
    size = lax.axis_size("req")
    pairs = [(i, i ^ (odd_bit if i % 2 else even_bit)) for i in range(size)]
    return lax.ppermute(value, "req", pairs)


def trades(values, bit):
    return [trade(value, "tp", bit) for value in values]


def each(join, *pieces):
    return [join(*items) for items in zip(*pieces)]


def add_pair(mine, got):
    return (mine + wide(got)).astype(bf16)


def add_rows(pair, rows, got):
    return (wide(rows) + (wide(pair) + wide(got))).astype(bf16)


def wide(value):
    return value.astype(f32)


def per_device(
    new_query,
    new_keyval,
    residual_in,
    leaf_cache,
    leaf_length,
    new_counts,
    request_mid,
    mid_root,
    node_length,
    prefix_pool,
    page_node,
    page_rank,
    out_weight,
    norm_gain,
    gate_weight,
    up_weight,
    down_weight,
    next_gain,
    query_weight,
    keyval_weight,
):
    rows = new_query.shape[0]
    part = rows // 2
    kv_local = new_keyval.shape[1] // (2 * HD)
    pool = prepare(page_node, page_rank, node_length, mid_root, prefix_pool)
    local_args = (new_query, new_keyval, leaf_cache, leaf_length, new_counts, request_mid)
    if lax.axis_size("req") == 8:
        first = cross(pool, 2, 4)
        second = cross(pool, 4, 2)
        beside = trade(pool, "req", 1)
        aug, state = start_attention(*local_args, [pool, beside])
        first, aug, state = lax.optimization_barrier((first, aug, state))
        corner = cross(first, 4, 2)
        first, second = lax.optimization_barrier((first, second))
        near = [first, second, trade(first, "req", 1), trade(second, "req", 1)]
        state = extend_attention(aug, state, near, kv_local)
        corner_other = trade(corner, "req", 1)
        state = extend_attention(aug, state, [corner], kv_local)
        pools = [corner_other]
    else:
        every = lax.all_gather(pool, "req", axis=0)
        holders = every.shape[0]
        aug, state = start_attention(*local_args, [pool])
        places = (lax.axis_index("req") + 1 + jnp.arange(holders - 1)) % holders
        step = 4
        for i in range(0, holders - 1, step):
            chunk = every[places[i : i + step]].reshape(-1, pool.shape[1])
            state = extend_attention(aug, state, [chunk], kv_local)
        pools = []

    theirs_att, *theirs_proj = finish_attention(
        aug, state, pools, out_weight, 0, kv_local, rows, ()
    )
    attention, *mine_proj = finish_attention(
        aug, state, pools, out_weight, 1, kv_local, rows, (theirs_att, residual_in)
    )
    theirs_proj = theirs_proj + mine_proj[: PIECES - 1]
    mine_proj, res_mine = mine_proj[PIECES - 1 : -PIECES], mine_proj[-PIECES:]

    mine = half_start(rows, 1)
    theirs = half_start(rows, 0)
    depth = residual_in.shape[1]
    if lax.axis_size("tp") == 4:
        got = trades(theirs_proj, 1)
        lead = add_pair(mine_proj[0], got[0])
        _, *mlp = lax.optimization_barrier((lead, gate_weight, up_weight, down_weight))
        got[1:], *mlp = lax.optimization_barrier((got[1:], *stage(mlp)))
        pair = [lead, *each(add_pair, mine_proj[1:], got[1:])]
        got = trades(pair, 2)
        mixed_mine = each(add_rows, pair, res_mine, got)
        mixed_theirs = trades(mixed_mine, 1)
        hidden, last = feed_forward(mixed_mine, norm_gain, *mlp)
        last = trade(last, "tp", 1)
        result = feed_forward(mixed_theirs, norm_gain, *mlp, [hidden])
        got = [*trades(result[: PIECES - 1], 1), last]
        mlp_theirs = result[PIECES - 1 :]
        lead = add_pair(mlp_theirs[-1], got[-1])
        _, query_weight = lax.optimization_barrier((lead, query_weight))
        got[:-1], query_weight = lax.optimization_barrier((got[:-1], *stage([query_weight])))
        pair = [*each(add_pair, mlp_theirs[:-1], got[:-1]), lead]
        got = trades(pair, 2)
        layer_theirs = each(add_rows, pair, mixed_theirs, got)
        layer_mine = trades(layer_theirs, 1)
    else:
        res_mine = jnp.concatenate(res_mine, axis=1)
        res_theirs = lax.dynamic_slice_in_dim(residual_in, theirs, part, 0)

        def in_order(theirs_part, mine_part):
            both = jnp.stack([theirs_part, mine_part])
            return jnp.where(mine == 0, both[::-1], both).reshape(rows, -1)

        theirs_proj = jnp.concatenate([wide(item) for item in theirs_proj], axis=1)
        mine_proj = jnp.concatenate(mine_proj, axis=1)
        total = lax.psum(in_order(theirs_proj, mine_proj), "tp")
        mixed = (wide(in_order(res_theirs, res_mine)) + total).astype(bf16)
        mixed_halves = [
            [mixed[h * part : (h + 1) * part, piece(depth, k)] for k in range(PIECES)]
            for h in range(2)
        ]
        mlp_weights = (gate_weight, up_weight, down_weight)
        hidden, last = feed_forward(mixed_halves[0], norm_gain, *mlp_weights)
        result = feed_forward(mixed_halves[1], norm_gain, *mlp_weights, [hidden])
        halves = [[*result[: PIECES - 1], last], result[PIECES - 1 :]]
        mlp = [jnp.concatenate([wide(item) for item in half], axis=1) for half in halves]
        mlp = lax.psum(jnp.concatenate(mlp, axis=0), "tp")
        layer = (wide(mixed) + mlp).astype(bf16)
        layer = [layer[:, piece(depth, k)] for k in range(PIECES)]
        layer_mine = [lax.dynamic_slice_in_dim(item, mine, part, 0) for item in layer]
        layer_theirs = [lax.dynamic_slice_in_dim(item, theirs, part, 0) for item in layer]
    weights = (next_gain, query_weight, keyval_weight.T)
    other = next_projections(layer_theirs, *weights, ())
    next_query, next_keyval, residual_out = next_projections(
        layer_mine, *weights, (*other, *layer_theirs)
    )
    return (attention, residual_out, next_query, next_keyval.T)


def solution(mesh):
    in_specs = (
        P("req", "tp"),
        P("req", "tp"),
        P("req", None),
        P("req", None, "tp"),
        P("req"),
        P("req", None),
        P("req"),
        P(),
        P(),
        P("req", None, "tp"),
        P("req"),
        P("req"),
        P("tp", None),
        P(),
        P(None, "tp"),
        P(None, "tp"),
        P("tp", None),
        P(),
        P(None, "tp"),
        P(None, "tp"),
    )
    out_specs = (P("req", "tp"), P(("req", "tp"), None), P("req", "tp"), P("req", "tp"))
    return jax.shard_map(
        per_device, mesh=mesh, in_specs=in_specs, out_specs=out_specs, check_vma=False
    )
```

```python
import functools
import math

import jax
import jax.numpy as jnp
from jax import lax
from jax.experimental import pallas as pl
from jax.experimental.pallas import tpu as pltpu
from jax.sharding import PartitionSpec as P

HD = 80
ROOTS = 2
MIDS = 6
LANES = 128
MASKED = -1e30
EPSILON = 1e-05
RATE = math.log2(math.e) / math.sqrt(HD)

PIECES = 2

bf16 = jnp.bfloat16
f32 = jnp.float32
i32 = jnp.int32
HBM = pl.BlockSpec(memory_space=pltpu.HBM)
VMEM = pl.BlockSpec(memory_space=pltpu.VMEM)
SMEM = pl.BlockSpec(memory_space=pltpu.SMEM)
PARAMS = pltpu.CompilerParams(vmem_limit_bytes=24 * 1024 * 1024)


def padded(width):
    return -(-width // LANES) * LANES


def key_start(c):
    return c * 2 * HD // LANES * LANES


def key_shift(c):
    return c * 2 * HD % LANES


def value_start(c):
    return (c * 2 * HD + HD) // LANES * LANES


def value_shift(c):
    return (c * 2 * HD + HD) % LANES


def key_window(ref, c):
    first = ref[:, key_start(c) : key_start(c) + LANES]
    last = ref[:, ref.shape[1] - LANES :]
    return jnp.concatenate([first, last], axis=1)


def value_window(ref, c):
    stop = min(value_start(c) + 2 * LANES, ref.shape[1])
    return ref[:, value_start(c) : stop]


def scores_of(query, keys):
    return lax.dot_general(query, keys, (((1,), (1,)), ((), ())), preferred_element_type=f32)


def fetch(pairs, sems):
    copies = [pltpu.make_async_copy(a, b, sems.at[i]) for i, (a, b) in enumerate(pairs)]
    for copy in copies:
        copy.start()
    return copies


def piece(width, k):
    step = width // PIECES
    return slice(k * step, (k + 1) * step)


def pieces_of(rows, width, dtype):
    return tuple(jax.ShapeDtypeStruct((rows, width // PIECES), dtype) for _ in range(PIECES))


def joined(refs):
    return jnp.concatenate([ref[...] for ref in refs], axis=1)


def in_hbm(values):
    return [pltpu.with_memory_space_constraint(value, pltpu.HBM) for value in values]


def in_vmem(values):
    return [pltpu.with_memory_space_constraint(value, pltpu.VMEM) for value in values]


def prep_kernel(
    node_hbm, rank_hbm, length_hbm, root_hbm, pool_hbm, out_ref,
    node_ref, rank_ref, length_ref, root_ref, pool_ref, sems,
):
    pairs = (
        (pool_hbm, pool_ref),
        (node_hbm, node_ref),
        (rank_hbm, rank_ref),
        (length_hbm, length_ref),
        (root_hbm, root_ref),
    )
    pool_copy, *copies = fetch(pairs, sems)
    for copy in copies:
        copy.wait()
    pages, size, width = pool_ref.shape
    free = out_ref.shape[1] - width
    lane = lax.broadcasted_iota(i32, (size, free), 1)
    slot = lax.broadcasted_iota(i32, (size, free), 0)
    root = jnp.full((size, free), -2, i32)
    for m in range(MIDS):
        root = jnp.where(lane == m, root_ref[m], root)
    hidden = jnp.where(lane < MIDS, MASKED, 0.0)
    for p in range(pages):
        node = node_ref[p]
        left = length_ref[jnp.maximum(node, 0)] - size * rank_ref[p]
        seen = ((root == node) | (lane + ROOTS == node)) & (slot < left)
        rows = slice(p * size, (p + 1) * size)
        out_ref[rows, width:] = jnp.where(seen, 0.0, hidden).astype(bf16)
    pool_copy.wait()
    out_ref[:, :width] = pool_ref[...].reshape(pages * size, width)


def prepare(page_node, page_rank, node_length, mid_root, prefix_pool):
    pages, size, width = prefix_pool.shape
    tables = (page_node, page_rank, node_length, mid_root)
    return pl.pallas_call(
        prep_kernel,
        out_shape=jax.ShapeDtypeStruct((pages * size, padded(width + MIDS)), bf16),
        in_specs=[HBM] * 5,
        out_specs=VMEM,
        scratch_shapes=[pltpu.SMEM(t.shape, i32) for t in tables]
        + [pltpu.VMEM(prefix_pool.shape, bf16), pltpu.SemaphoreType.DMA((5,))],
        compiler_params=PARAMS,
        name="pool_rows",
    )(*in_hbm((*tables, prefix_pool)))


def half_start(rows, half):
    parity = lax.rem(lax.axis_index("tp"), 2)
    return (parity if half else 1 - parity) * (rows // 2)


def fold(scores, values, state):
    top = functools.reduce(jnp.maximum, [jnp.max(s, axis=1, keepdims=True) for s in scores])
    if state is not None:
        top = jnp.maximum(top, state[0])
    total, weighted = None, None
    for s, v in zip(scores, values):
        raised = jnp.exp2((s - top) * RATE)
        part = jnp.sum(raised, axis=1, keepdims=True)
        mixed = jnp.dot(raised.astype(bf16), v, preferred_element_type=f32)
        total = part if total is None else total + part
        weighted = mixed if weighted is None else weighted + mixed
    if state is not None:
        factor = jnp.exp2((state[0] - top) * RATE)
        total = total + state[1] * factor
        weighted = weighted + state[2] * factor
    return top, total, weighted


def pack(top, total, weighted):
    lane = lax.broadcasted_iota(i32, weighted.shape, 1)
    return jnp.where(lane == 0, top, jnp.where(lane == 1, total, weighted))


def unpack(state):
    return state[:, 0:1], state[:, 1:2], state


def local_kernel(
    count_hbm, mid_hbm, leaf_len_hbm, query_ref, keyval_ref, leaf_ref, *refs, chunks
):
    pool_refs = refs[:chunks]
    aug_ref, state_ref, count_ref, mid_ref, leaf_len_ref, sems = refs[chunks:]
    pairs = ((count_hbm, count_ref), (mid_hbm, mid_ref), (leaf_len_hbm, leaf_len_ref))
    for copy in fetch(pairs, sems):
        copy.wait()
    rows = query_ref.shape[0]
    part = rows // 2
    width = keyval_ref.shape[1]
    requests, slots, _ = leaf_ref.shape
    kv_local = width // (2 * HD)
    group = query_ref.shape[1] // (kv_local * HD)
    lane = lax.broadcasted_iota(i32, (part, LANES), 1)
    zero = jnp.zeros((part, LANES), i32)
    leaf_all = leaf_ref[...].reshape(requests * slots, width)
    leaf_at = lax.broadcasted_iota(i32, (part, requests * slots), 1)
    for half in range(2):
        first = half_start(rows, half)
        row = lax.broadcasted_iota(i32, (part, LANES), 0) + first
        start, low, high, mid = zero, zero, zero, zero
        begin = jnp.int32(0)
        for r in range(requests):
            here = row >= begin
            start = jnp.where(here, begin, start)
            low = jnp.where(here, r * slots, low)
            high = jnp.where(here, r * slots + leaf_len_ref[r], high)
            mid = jnp.where(here, mid_ref[r], mid)
            begin = begin + count_ref[0, r]
        chosen = jnp.where(lane == width % LANES + mid, 1.0, 0.0).astype(bf16)
        leaf_ok = (leaf_at >= low[:, 0:1]) & (leaf_at < high[:, 0:1])
        new_ok = (lane >= start) & (lane <= row)
        tokens = query_ref[pl.ds(pl.multiple_of(first, part), part), :]
        for c in range(kv_local):
            base = (half * kv_local + c) * group * part
            block = slice(base, base + group * part)
            key0, val0 = key_start(c), value_start(c)
            shift = key_shift(c)
            for g in range(group):
                h = c * group + g
                at = slice(base + g * part, base + (g + 1) * part)
                aug_ref[at, :LANES] = jnp.zeros((part, LANES), bf16)
                aug_ref[at, shift : shift + HD] = tokens[:, h * HD : (h + 1) * HD]
                aug_ref[at, LANES:] = chosen
            query = aug_ref[block, :]
            narrow = query[:, :LANES]
            s_leaf = scores_of(narrow, leaf_all[:, key0 : key0 + LANES])
            s_leaf = jnp.where(leaf_ok[None], s_leaf.reshape(group, part, -1), MASKED)
            s_new = scores_of(narrow, keyval_ref[:, key0 : key0 + LANES])
            s_new = jnp.where(new_ok[None], s_new.reshape(group, part, -1), MASKED)
            scores = [s_leaf.reshape(group * part, -1), s_new.reshape(group * part, -1)]
            stop = min(val0 + 2 * LANES, width)
            fill = val0 + 2 * LANES - stop
            values = [leaf_all[:, val0:stop], keyval_ref[:, val0:stop]]
            if fill:
                values = [
                    jnp.concatenate([v, jnp.zeros((v.shape[0], fill), bf16)], axis=1) for v in values
                ]
            for pool_ref in pool_refs:
                scores.append(scores_of(query, key_window(pool_ref, c)))
                values.append(value_window(pool_ref, c))
            state_ref[block, :] = pack(*fold(scores, values, None))


def start_attention(new_query, new_keyval, leaf, leaf_length, counts, request_mid, pools):
    rows, query_width = new_query.shape
    heads = query_width // HD
    tables = (counts, request_mid, leaf_length)
    keys = leaf.shape[0] * leaf.shape[1] + rows + sum(item.shape[0] for item in pools)
    return pl.pallas_call(
        functools.partial(local_kernel, chunks=len(pools)),
        out_shape=(
            jax.ShapeDtypeStruct((heads * rows, 2 * LANES), bf16),
            jax.ShapeDtypeStruct((heads * rows, 2 * LANES), f32),
        ),
        in_specs=[HBM] * 3 + [VMEM] * (3 + len(pools)),
        out_specs=(VMEM, VMEM),
        scratch_shapes=[pltpu.SMEM(t.shape, i32) for t in tables] + [pltpu.SemaphoreType.DMA((3,))],
        compiler_params=PARAMS,
        cost_estimate=attention_cost(heads * rows, keys),
        name="attend_local",
    )(*in_hbm(tables), new_query, new_keyval, leaf, *pools)


def attention_cost(rows, keys):
    return pl.CostEstimate(
        flops=8 * LANES * rows * keys, bytes_accessed=8 * rows * 2 * LANES, transcendentals=rows * keys
    )


def extended(query, state, pool_refs, c):
    scores = [scores_of(query, key_window(ref, c)) for ref in pool_refs]
    values = [value_window(ref, c) for ref in pool_refs]
    return fold(scores, values, unpack(state))


def chunk_kernel(*refs, blocks):
    aug_ref, state_ref = refs[:2]
    pool_refs, out_ref = refs[2:-1], refs[-1]
    size = aug_ref.shape[0] // blocks
    for b in range(blocks):
        at = slice(b * size, (b + 1) * size)
        state = extended(aug_ref[at, :], state_ref[at, :], pool_refs, b % (blocks // 2))
        out_ref[at, :] = pack(*state)


def extend_attention(aug, state, pools, kv_local):
    keys = sum(item.shape[0] for item in pools)
    return pl.pallas_call(
        functools.partial(chunk_kernel, blocks=2 * kv_local),
        out_shape=jax.ShapeDtypeStruct(state.shape, f32),
        in_specs=[VMEM] * (2 + len(pools)),
        out_specs=VMEM,
        compiler_params=PARAMS,
        cost_estimate=attention_cost(aug.shape[0], keys),
        name="attend_pages",
    )(aug, state, *pools)


def project(out_refs, rows, weight_ref, places):
    for out_ref, k in zip(out_refs, places):
        weight = weight_ref[:, piece(weight_ref.shape[1], k)]
        result = jnp.dot(rows, weight, preferred_element_type=f32)
        out_ref[...] = result.astype(out_ref.dtype)


def finish_kernel(*refs, half, kv_local, chunks, width):
    aug_ref, state_ref = refs[:2]
    pool_refs = refs[2 : 2 + chunks]
    weight_ref = refs[2 + chunks]
    part = aug_ref.shape[0] // (2 * width // HD)
    rest = refs[3 + chunks :]
    att_ref, *proj_refs, mine_ref = rest[2 * half :]
    if half:
        send_refs, proj_refs = proj_refs[: PIECES - 1], proj_refs[PIECES - 1 :]
        proj_refs, res_refs = proj_refs[:PIECES], proj_refs[PIECES:]
        project(send_refs, rest[0][...], weight_ref, range(1, PIECES))
    group = width // (kv_local * HD)
    size = group * part
    for c in range(kv_local):
        at = slice((half * kv_local + c) * size, (half * kv_local + c + 1) * size)
        if chunks:
            state = extended(aug_ref[at, :], state_ref[at, :], pool_refs, c)
        else:
            state = unpack(state_ref[at, :])
        shift = value_shift(c)
        result = (state[2][:, shift : shift + HD] / state[1]).astype(bf16)
        for g in range(group):
            h = c * group + g
            mine_ref[:, h * HD : (h + 1) * HD] = result[g * part : (g + 1) * part]
    if half:
        mine = pl.multiple_of(half_start(2 * part, 1), part)
        theirs = pl.multiple_of(half_start(2 * part, 0), part)
        att_ref[pl.ds(mine, part), :] = mine_ref[...]
        att_ref[pl.ds(theirs, part), :] = rest[0][...]
        for k, res_ref in enumerate(res_refs):
            res_ref[...] = rest[1][pl.ds(mine, part), piece(rest[1].shape[1], k)]
    else:
        att_ref[...] = mine_ref[...]
    project(proj_refs, mine_ref[...], weight_ref, range(PIECES if half else 1))


def finish_attention(aug, state, pools, out_weight, half, kv_local, rows, other):
    width = out_weight.shape[0]
    part = rows // 2
    keys = sum(item.shape[0] for item in pools)
    depth = out_weight.shape[1]
    sent = pieces_of(part, depth, bf16)
    if half:
        shapes = (*sent[:-1], *pieces_of(part, depth, f32), *pieces_of(part, depth, bf16))
    else:
        shapes = sent[-1:]
    return pl.pallas_call(
        functools.partial(
            finish_kernel, half=half, kv_local=kv_local, chunks=len(pools), width=width
        ),
        out_shape=(jax.ShapeDtypeStruct((rows if half else part, width), bf16), *shapes),
        in_specs=[VMEM] * (3 + len(pools) + len(other)),
        out_specs=(VMEM,) * (1 + len(shapes)),
        scratch_shapes=[pltpu.VMEM((part, width), bf16)],
        compiler_params=PARAMS,
        cost_estimate=attention_cost(aug.shape[0] // 2, keys + 512),
        name="attend_finish",
    )(aug, state, *pools, out_weight, *other)


def normalized(values_in, gain):
    values = values_in.astype(f32)
    scale = lax.rsqrt(jnp.mean(values * values, axis=-1, keepdims=True) + EPSILON)
    return (values * scale * gain.astype(f32)).astype(bf16)


def stage_kernel(*refs):
    count = len(refs) // 2
    for copy in fetch(zip(refs[:count], refs[count : 2 * count]), refs[-1]):
        copy.wait()


def stage(weights):
    return pl.pallas_call(
        stage_kernel,
        out_shape=tuple(pltpu.VMEM(w.shape, w.dtype) for w in weights),
        in_specs=[HBM] * len(weights),
        out_specs=(VMEM,) * len(weights),
        scratch_shapes=[pltpu.SemaphoreType.DMA((len(weights),))],
        compiler_params=pltpu.CompilerParams(vmem_limit_bytes=1024 * 1024),
        cost_estimate=pl.CostEstimate(
            flops=0, bytes_accessed=sum(2 * w.size for w in weights), transcendentals=0
        ),
        name="stage",
    )(*in_hbm(weights))


def gained(rows, gain_ref, k):
    return (wide(rows) * wide(gain_ref[:, piece(gain_ref.shape[1], k)])).astype(bf16)


def inverse_rms(row_refs):
    squares = [jnp.sum(wide(ref[...]) ** 2, axis=-1, keepdims=True) for ref in row_refs]
    depth = sum(ref.shape[1] for ref in row_refs)
    return lax.rsqrt(sum(squares) / depth + EPSILON)


def times(rows, weight_ref, k):
    weight = weight_ref[piece(weight_ref.shape[0], k), :]
    return jnp.dot(rows, weight, preferred_element_type=f32)


def early_kernel(rows_ref, gain_ref, *refs):
    rows = gained(rows_ref[...], gain_ref, 0)
    count = len(refs) // 2
    for weight_ref, out_ref in zip(refs[:count], refs[count:]):
        out_ref[...] = times(rows, weight_ref, 0)


def early_products(rows, gain, weights):
    count = rows.shape[0]
    shapes = [jax.ShapeDtypeStruct((count, w.shape[1]), f32) for w in weights]
    return pl.pallas_call(
        early_kernel,
        out_shape=tuple(shapes),
        in_specs=[VMEM] * (2 + len(weights)),
        out_specs=(VMEM,) * len(weights),
        compiler_params=PARAMS,
        cost_estimate=pl.CostEstimate(
            flops=sum(w.size for w in weights) * count,
            bytes_accessed=sum(w.size for w in weights),
            transcendentals=0,
        ),
        name="early_piece",
    )(rows, gain.reshape(1, -1), *in_vmem(weights))


def mlp_kernel(*refs, second, early):
    row_refs, (gain_ref, gate_ref, up_ref, down_ref) = refs[:PIECES], refs[PIECES : PIECES + 4]
    refs = refs[PIECES + 4 :]
    sums = [0.0, 0.0]
    if early:
        sums, refs = [ref[...] for ref in refs[:2]], refs[2:]
    if second:
        project(refs[1:PIECES], refs[0][...], down_ref, range(PIECES - 1))
    scale = inverse_rms(row_refs)
    for k in range(early, PIECES):
        rows = gained(row_refs[k][...], gain_ref, k)
        sums = [item + times(rows, ref, k) for item, ref in zip(sums, (gate_ref, up_ref))]
    gate, upward = sums
    hidden = (jax.nn.silu(gate * scale) * (upward * scale)).astype(bf16)
    if second:
        project(refs[PIECES:], hidden, down_ref, range(PIECES))
    else:
        refs[0][...] = hidden
        project(refs[1:], hidden, down_ref, [PIECES - 1])


def feed_forward(rows, early, gain, gate_weight, up_weight, down_weight, other=()):
    count = rows[0].shape[0]
    depth, width = gate_weight.shape
    sent = pieces_of(count, depth, bf16)
    if other:
        shapes = (*sent[:-1], *pieces_of(count, depth, f32))
    else:
        shapes = (jax.ShapeDtypeStruct((count, width), bf16), sent[-1])
    return pl.pallas_call(
        functools.partial(mlp_kernel, second=len(other) > 0, early=min(len(early), 1)),
        out_shape=shapes,
        in_specs=[VMEM] * (PIECES + 4 + len(early) + len(other)),
        out_specs=(VMEM,) * len(shapes),
        compiler_params=PARAMS,
        cost_estimate=pl.CostEstimate(
            flops=6 * count * depth * width, bytes_accessed=6 * depth * width, transcendentals=0
        ),
        name="feed_forward",
    )(
        *rows,
        gain.reshape(1, depth),
        *in_vmem((gate_weight, up_weight, down_weight)),
        *early,
        *other,
    )


def next_kernel(*refs, half):
    row_refs, refs = refs[:PIECES], refs[PIECES:]
    gain_ref, query_ref, keyval_ref = refs[:3]
    rows = joined(row_refs)
    normed = normalized(rows, gain_ref[...])
    query = jnp.dot(normed, query_ref[...], preferred_element_type=f32).astype(bf16)
    keyval = scores_of(keyval_ref[...], normed).astype(bf16)
    if not half:
        query_out, keyval_out = refs[3:]
        query_out[...] = query
        keyval_out[...] = keyval
        return
    query_in, keyval_in = refs[3:5]
    query_out, keyval_out, residual_out = refs[5 + PIECES :]
    part = query.shape[0]
    mine = pl.multiple_of(half_start(2 * part, 1), part)
    theirs = pl.multiple_of(half_start(2 * part, 0), part)
    query_out[pl.ds(mine, part), :] = query
    query_out[pl.ds(theirs, part), :] = query_in[...]

    @pl.when(mine == 0)
    def _():
        keyval_out[:, :part] = keyval
        keyval_out[:, part:] = keyval_in[...]

    @pl.when(mine != 0)
    def _():
        keyval_out[:, :part] = keyval_in[...]
        keyval_out[:, part:] = keyval

    share = residual_out.shape[0]
    place = lax.axis_index("tp") * share
    at = pl.multiple_of(lax.rem(place, part), share)
    held = (place >= mine) & (place < mine + part)
    for k in range(PIECES):
        ours = row_refs[k][pl.ds(at, share), :]
        others = refs[5 + k][pl.ds(at, share), :]
        residual_out[:, piece(rows.shape[1], k)] = jnp.where(held, ours, others)


def next_projections(rows, gain, query_weight, keyval_weight, other):
    count = rows[0].shape[0]
    depth = query_weight.shape[0]
    widths = (query_weight.shape[1], keyval_weight.shape[0])
    half = len(other) > 0
    out_rows = 2 * count if half else count
    shapes = [(out_rows, widths[0]), (widths[1], out_rows)]
    if half:
        shapes.append((out_rows // lax.axis_size("tp"), depth))
    return pl.pallas_call(
        functools.partial(next_kernel, half=half),
        out_shape=tuple(jax.ShapeDtypeStruct(shape, bf16) for shape in shapes),
        in_specs=[VMEM] * (PIECES + 3 + len(other)),
        out_specs=(VMEM,) * len(shapes),
        compiler_params=PARAMS,
        cost_estimate=pl.CostEstimate(
            flops=2 * count * depth * sum(widths),
            bytes_accessed=2 * depth * sum(widths),
            transcendentals=0,
        ),
        name="next_layer",
    )(*rows, gain.reshape(1, depth), *in_vmem([query_weight]), keyval_weight, *other)


def trade(value, axis, bit):
    size = lax.axis_size(axis)
    return lax.ppermute(value, axis, [(i, i ^ bit) for i in range(size)])


def cross(value, even_bit, odd_bit):
    size = lax.axis_size("req")
    pairs = [(i, i ^ (odd_bit if i % 2 else even_bit)) for i in range(size)]
    return lax.ppermute(value, "req", pairs)


def trades(values, bit):
    return [trade(value, "tp", bit) for value in values]


def each(join, *pieces):
    return [join(*items) for items in zip(*pieces)]


def add_pair(mine, got):
    return (mine + wide(got)).astype(bf16)


def pairs_in_turn(mine, got, weights):
    last = add_pair(mine[-1], got[-1])
    _, rest, weights = lax.optimization_barrier((last, got[:-1], weights))
    return [*each(add_pair, mine[:-1], rest), last], weights


def add_rows(pair, rows, got):
    return (wide(rows) + (wide(pair) + wide(got))).astype(bf16)


def wide(value):
    return value.astype(f32)


def per_device(
    new_query,
    new_keyval,
    residual_in,
    leaf_cache,
    leaf_length,
    new_counts,
    request_mid,
    mid_root,
    node_length,
    prefix_pool,
    page_node,
    page_rank,
    out_weight,
    norm_gain,
    gate_weight,
    up_weight,
    down_weight,
    next_gain,
    query_weight,
    keyval_weight,
):
    rows = new_query.shape[0]
    part = rows // 2
    kv_local = new_keyval.shape[1] // (2 * HD)
    pool = prepare(page_node, page_rank, node_length, mid_root, prefix_pool)
    local_args = (new_query, new_keyval, leaf_cache, leaf_length, new_counts, request_mid)
    if lax.axis_size("req") == 8:
        first = cross(pool, 2, 4)
        second = cross(pool, 4, 2)
        beside = trade(pool, "req", 1)
        aug, state = start_attention(*local_args, [pool, beside])
        first, aug, state = lax.optimization_barrier((first, aug, state))
        corner = cross(first, 4, 2)
        first, second = lax.optimization_barrier((first, second))
        near = [first, second, trade(first, "req", 1), trade(second, "req", 1)]
        state = extend_attention(aug, state, near, kv_local)
        state, down_weight = lax.optimization_barrier((state, down_weight))
        corner, state, down_weight = lax.optimization_barrier(
            (corner, state, *stage([down_weight]))
        )
        corner_other = trade(corner, "req", 1)
        state = extend_attention(aug, state, [corner], kv_local)
        pools = [corner_other]
    else:
        every = lax.all_gather(pool, "req", axis=0)
        holders = every.shape[0]
        aug, state = start_attention(*local_args, [pool])
        places = (lax.axis_index("req") + 1 + jnp.arange(holders - 1)) % holders
        step = 4
        for i in range(0, holders - 1, step):
            chunk = every[places[i : i + step]].reshape(-1, pool.shape[1])
            state = extend_attention(aug, state, [chunk], kv_local)
        pools = []

    theirs_att, *theirs_proj = finish_attention(
        aug, state, pools, out_weight, 0, kv_local, rows, ()
    )
    attention, *mine_proj = finish_attention(
        aug, state, pools, out_weight, 1, kv_local, rows, (theirs_att, residual_in)
    )
    theirs_proj = theirs_proj + mine_proj[: PIECES - 1]
    mine_proj, res_mine = mine_proj[PIECES - 1 : -PIECES], mine_proj[-PIECES:]

    mine = half_start(rows, 1)
    theirs = half_start(rows, 0)
    depth = residual_in.shape[1]
    if lax.axis_size("tp") == 4:
        got = trades(theirs_proj, 1)
        pair, (gate_weight, up_weight) = pairs_in_turn(
            mine_proj[::-1], got[::-1], (gate_weight, up_weight)
        )
        pair = pair[::-1]
        got = trades(pair, 2)
        got[-1], *staged = lax.optimization_barrier((got[-1], *stage([gate_weight, up_weight])))
        mlp = (*staged, down_weight)
        mixed_mine = each(add_rows, pair, res_mine, got)
        mixed_theirs = trades(mixed_mine, 1)
        hidden, last = feed_forward(mixed_mine, (), norm_gain, *mlp)
        last = trade(last, "tp", 1)
        early = early_products(mixed_theirs[0], norm_gain, mlp[:2])
        _, mixed_theirs[1:] = lax.optimization_barrier((early, mixed_theirs[1:]))
        result = feed_forward(mixed_theirs, early, norm_gain, *mlp, [hidden])
        got = [*trades(result[: PIECES - 1], 1), last]
        mlp_theirs = result[PIECES - 1 :]
        pair, (query_weight,) = pairs_in_turn(mlp_theirs, got, (query_weight,))
        got = trades(pair, 2)
        got[-1], query_weight = lax.optimization_barrier((got[-1], *stage([query_weight])))
        layer_theirs = each(add_rows, pair, mixed_theirs, got)
        layer_mine = trades(layer_theirs, 1)
    else:
        res_mine = jnp.concatenate(res_mine, axis=1)
        res_theirs = lax.dynamic_slice_in_dim(residual_in, theirs, part, 0)

        def in_order(theirs_part, mine_part):
            both = jnp.stack([theirs_part, mine_part])
            return jnp.where(mine == 0, both[::-1], both).reshape(rows, -1)

        theirs_proj = jnp.concatenate([wide(item) for item in theirs_proj], axis=1)
        mine_proj = jnp.concatenate(mine_proj, axis=1)
        total = lax.psum(in_order(theirs_proj, mine_proj), "tp")
        mixed = (wide(in_order(res_theirs, res_mine)) + total).astype(bf16)
        mixed_halves = [
            [mixed[h * part : (h + 1) * part, piece(depth, k)] for k in range(PIECES)]
            for h in range(2)
        ]
        mlp_weights = (gate_weight, up_weight, down_weight)
        hidden, last = feed_forward(mixed_halves[0], (), norm_gain, *mlp_weights)
        result = feed_forward(mixed_halves[1], (), norm_gain, *mlp_weights, [hidden])
        halves = [[*result[: PIECES - 1], last], result[PIECES - 1 :]]
        mlp = [jnp.concatenate([wide(item) for item in half], axis=1) for half in halves]
        mlp = lax.psum(jnp.concatenate(mlp, axis=0), "tp")
        layer = (wide(mixed) + mlp).astype(bf16)
        layer = [layer[:, piece(depth, k)] for k in range(PIECES)]
        layer_mine = [lax.dynamic_slice_in_dim(item, mine, part, 0) for item in layer]
        layer_theirs = [lax.dynamic_slice_in_dim(item, theirs, part, 0) for item in layer]
    weights = (next_gain, query_weight, keyval_weight.T)
    other = next_projections(layer_theirs, *weights, ())
    next_query, next_keyval, residual_out = next_projections(
        layer_mine, *weights, (*other, *layer_theirs)
    )
    return (attention, residual_out, next_query, next_keyval.T)


def solution(mesh):
    in_specs = (
        P("req", "tp"),
        P("req", "tp"),
        P("req", None),
        P("req", None, "tp"),
        P("req"),
        P("req", None),
        P("req"),
        P(),
        P(),
        P("req", None, "tp"),
        P("req"),
        P("req"),
        P("tp", None),
        P(),
        P(None, "tp"),
        P(None, "tp"),
        P("tp", None),
        P(),
        P(None, "tp"),
        P(None, "tp"),
    )
    out_specs = (P("req", "tp"), P(("req", "tp"), None), P("req", "tp"), P("req", "tp"))
    return jax.shard_map(
        per_device, mesh=mesh, in_specs=in_specs, out_specs=out_specs, check_vma=False
    )
```

```python
import functools
import math

import jax
import jax.numpy as jnp
from jax import lax
from jax.experimental import pallas as pl
from jax.experimental.pallas import tpu as pltpu
from jax.sharding import PartitionSpec as P

HD = 80
ROOTS = 2
MIDS = 6
LANES = 128
MASKED = -1e30
EPSILON = 1e-05
RATE = math.log2(math.e) / math.sqrt(HD)

PIECES = 2

bf16 = jnp.bfloat16
f32 = jnp.float32
i32 = jnp.int32
HBM = pl.BlockSpec(memory_space=pltpu.HBM)
VMEM = pl.BlockSpec(memory_space=pltpu.VMEM)
SMEM = pl.BlockSpec(memory_space=pltpu.SMEM)
PARAMS = pltpu.CompilerParams(vmem_limit_bytes=24 * 1024 * 1024)


def padded(width):
    return -(-width // LANES) * LANES


def key_start(c):
    return c * 2 * HD // LANES * LANES


def key_shift(c):
    return c * 2 * HD % LANES


def value_start(c):
    return (c * 2 * HD + HD) // LANES * LANES


def value_shift(c):
    return (c * 2 * HD + HD) % LANES


def key_window(ref, c):
    first = ref[:, key_start(c) : key_start(c) + LANES]
    last = ref[:, ref.shape[1] - LANES :]
    return jnp.concatenate([first, last], axis=1)


def value_window(ref, c):
    stop = min(value_start(c) + 2 * LANES, ref.shape[1])
    return ref[:, value_start(c) : stop]


def scores_of(query, keys):
    return lax.dot_general(query, keys, (((1,), (1,)), ((), ())), preferred_element_type=f32)


def fetch(pairs, sems):
    copies = [pltpu.make_async_copy(a, b, sems.at[i]) for i, (a, b) in enumerate(pairs)]
    for copy in copies:
        copy.start()
    return copies


def piece(width, k):
    step = width // PIECES
    return slice(k * step, (k + 1) * step)


def pieces_of(rows, width, dtype):
    return tuple(jax.ShapeDtypeStruct((rows, width // PIECES), dtype) for _ in range(PIECES))


def joined(refs):
    return jnp.concatenate([ref[...] for ref in refs], axis=1)


def in_hbm(values):
    return [pltpu.with_memory_space_constraint(value, pltpu.HBM) for value in values]


def in_vmem(values):
    return [pltpu.with_memory_space_constraint(value, pltpu.VMEM) for value in values]


def prep_kernel(
    node_hbm, rank_hbm, length_hbm, root_hbm, pool_hbm, out_ref,
    node_ref, rank_ref, length_ref, root_ref, pool_ref, sems,
):
    pairs = (
        (pool_hbm, pool_ref),
        (node_hbm, node_ref),
        (rank_hbm, rank_ref),
        (length_hbm, length_ref),
        (root_hbm, root_ref),
    )
    pool_copy, *copies = fetch(pairs, sems)
    for copy in copies:
        copy.wait()
    pages, size, width = pool_ref.shape
    free = out_ref.shape[1] - width
    lane = lax.broadcasted_iota(i32, (size, free), 1)
    slot = lax.broadcasted_iota(i32, (size, free), 0)
    root = jnp.full((size, free), -2, i32)
    for m in range(MIDS):
        root = jnp.where(lane == m, root_ref[m], root)
    hidden = jnp.where(lane < MIDS, MASKED, 0.0)
    for p in range(pages):
        node = node_ref[p]
        left = length_ref[jnp.maximum(node, 0)] - size * rank_ref[p]
        seen = ((root == node) | (lane + ROOTS == node)) & (slot < left)
        rows = slice(p * size, (p + 1) * size)
        out_ref[rows, width:] = jnp.where(seen, 0.0, hidden).astype(bf16)
    pool_copy.wait()
    out_ref[:, :width] = pool_ref[...].reshape(pages * size, width)


def prepare(page_node, page_rank, node_length, mid_root, prefix_pool):
    pages, size, width = prefix_pool.shape
    tables = (page_node, page_rank, node_length, mid_root)
    return pl.pallas_call(
        prep_kernel,
        out_shape=jax.ShapeDtypeStruct((pages * size, padded(width + MIDS)), bf16),
        in_specs=[HBM] * 5,
        out_specs=VMEM,
        scratch_shapes=[pltpu.SMEM(t.shape, i32) for t in tables]
        + [pltpu.VMEM(prefix_pool.shape, bf16), pltpu.SemaphoreType.DMA((5,))],
        compiler_params=PARAMS,
        name="pool_rows",
    )(*in_hbm((*tables, prefix_pool)))


def half_start(rows, half):
    parity = lax.rem(lax.axis_index("tp"), 2)
    return (parity if half else 1 - parity) * (rows // 2)


def fold(scores, values, state):
    top = functools.reduce(jnp.maximum, [jnp.max(s, axis=1, keepdims=True) for s in scores])
    if state is not None:
        top = jnp.maximum(top, state[0])
    total, weighted = None, None
    for s, v in zip(scores, values):
        raised = jnp.exp2((s - top) * RATE)
        part = jnp.sum(raised, axis=1, keepdims=True)
        mixed = jnp.dot(raised.astype(bf16), v, preferred_element_type=f32)
        total = part if total is None else total + part
        weighted = mixed if weighted is None else weighted + mixed
    if state is not None:
        factor = jnp.exp2((state[0] - top) * RATE)
        total = total + state[1] * factor
        weighted = weighted + state[2] * factor
    return top, total, weighted


def pack(top, total, weighted):
    lane = lax.broadcasted_iota(i32, weighted.shape, 1)
    return jnp.where(lane == 0, top, jnp.where(lane == 1, total, weighted))


def unpack(state):
    return state[:, 0:1], state[:, 1:2], state


def local_kernel(
    count_hbm, mid_hbm, leaf_len_hbm, query_ref, keyval_ref, leaf_ref, *refs, chunks
):
    pool_refs = refs[:chunks]
    aug_ref, state_ref, count_ref, mid_ref, leaf_len_ref, sems = refs[chunks:]
    pairs = ((count_hbm, count_ref), (mid_hbm, mid_ref), (leaf_len_hbm, leaf_len_ref))
    for copy in fetch(pairs, sems):
        copy.wait()
    rows = query_ref.shape[0]
    part = rows // 2
    width = keyval_ref.shape[1]
    requests, slots, _ = leaf_ref.shape
    kv_local = width // (2 * HD)
    group = query_ref.shape[1] // (kv_local * HD)
    lane = lax.broadcasted_iota(i32, (part, LANES), 1)
    zero = jnp.zeros((part, LANES), i32)
    leaf_all = leaf_ref[...].reshape(requests * slots, width)
    leaf_at = lax.broadcasted_iota(i32, (part, requests * slots), 1)
    for half in range(2):
        first = half_start(rows, half)
        row = lax.broadcasted_iota(i32, (part, LANES), 0) + first
        start, low, high, mid = zero, zero, zero, zero
        begin = jnp.int32(0)
        for r in range(requests):
            here = row >= begin
            start = jnp.where(here, begin, start)
            low = jnp.where(here, r * slots, low)
            high = jnp.where(here, r * slots + leaf_len_ref[r], high)
            mid = jnp.where(here, mid_ref[r], mid)
            begin = begin + count_ref[0, r]
        chosen = jnp.where(lane == width % LANES + mid, 1.0, 0.0).astype(bf16)
        leaf_ok = (leaf_at >= low[:, 0:1]) & (leaf_at < high[:, 0:1])
        new_ok = (lane >= start) & (lane <= row)
        tokens = query_ref[pl.ds(pl.multiple_of(first, part), part), :]
        for c in range(kv_local):
            base = (half * kv_local + c) * group * part
            block = slice(base, base + group * part)
            key0, val0 = key_start(c), value_start(c)
            shift = key_shift(c)
            for g in range(group):
                h = c * group + g
                at = slice(base + g * part, base + (g + 1) * part)
                aug_ref[at, :LANES] = jnp.zeros((part, LANES), bf16)
                aug_ref[at, shift : shift + HD] = tokens[:, h * HD : (h + 1) * HD]
                aug_ref[at, LANES:] = chosen
            query = aug_ref[block, :]
            narrow = query[:, :LANES]
            s_leaf = scores_of(narrow, leaf_all[:, key0 : key0 + LANES])
            s_leaf = jnp.where(leaf_ok[None], s_leaf.reshape(group, part, -1), MASKED)
            s_new = scores_of(narrow, keyval_ref[:, key0 : key0 + LANES])
            s_new = jnp.where(new_ok[None], s_new.reshape(group, part, -1), MASKED)
            scores = [s_leaf.reshape(group * part, -1), s_new.reshape(group * part, -1)]
            stop = min(val0 + 2 * LANES, width)
            fill = val0 + 2 * LANES - stop
            values = [leaf_all[:, val0:stop], keyval_ref[:, val0:stop]]
            if fill:
                values = [
                    jnp.concatenate([v, jnp.zeros((v.shape[0], fill), bf16)], axis=1) for v in values
                ]
            for pool_ref in pool_refs:
                scores.append(scores_of(query, key_window(pool_ref, c)))
                values.append(value_window(pool_ref, c))
            state_ref[block, :] = pack(*fold(scores, values, None))


def start_attention(new_query, new_keyval, leaf, leaf_length, counts, request_mid, pools):
    rows, query_width = new_query.shape
    heads = query_width // HD
    tables = (counts, request_mid, leaf_length)
    keys = leaf.shape[0] * leaf.shape[1] + rows + sum(item.shape[0] for item in pools)
    return pl.pallas_call(
        functools.partial(local_kernel, chunks=len(pools)),
        out_shape=(
            jax.ShapeDtypeStruct((heads * rows, 2 * LANES), bf16),
            jax.ShapeDtypeStruct((heads * rows, 2 * LANES), f32),
        ),
        in_specs=[HBM] * 3 + [VMEM] * (3 + len(pools)),
        out_specs=(VMEM, VMEM),
        scratch_shapes=[pltpu.SMEM(t.shape, i32) for t in tables] + [pltpu.SemaphoreType.DMA((3,))],
        compiler_params=PARAMS,
        cost_estimate=attention_cost(heads * rows, keys),
        name="attend_local",
    )(*in_hbm(tables), new_query, new_keyval, leaf, *pools)


def attention_cost(rows, keys):
    return pl.CostEstimate(
        flops=8 * LANES * rows * keys, bytes_accessed=8 * rows * 2 * LANES, transcendentals=rows * keys
    )


def extended(query, state, pool_refs, c):
    scores = [scores_of(query, key_window(ref, c)) for ref in pool_refs]
    values = [value_window(ref, c) for ref in pool_refs]
    return fold(scores, values, unpack(state))


def chunk_kernel(*refs, blocks):
    aug_ref, state_ref = refs[:2]
    pool_refs, out_ref = refs[2:-1], refs[-1]
    size = aug_ref.shape[0] // blocks
    for b in range(blocks):
        at = slice(b * size, (b + 1) * size)
        state = extended(aug_ref[at, :], state_ref[at, :], pool_refs, b % (blocks // 2))
        out_ref[at, :] = pack(*state)


def extend_attention(aug, state, pools, kv_local):
    keys = sum(item.shape[0] for item in pools)
    return pl.pallas_call(
        functools.partial(chunk_kernel, blocks=2 * kv_local),
        out_shape=jax.ShapeDtypeStruct(state.shape, f32),
        in_specs=[VMEM] * (2 + len(pools)),
        out_specs=VMEM,
        compiler_params=PARAMS,
        cost_estimate=attention_cost(aug.shape[0], keys),
        name="attend_pages",
    )(aug, state, *pools)


def project(out_refs, rows, weight_ref, places):
    for out_ref, k in zip(out_refs, places):
        weight = weight_ref[:, piece(weight_ref.shape[1], k)]
        result = jnp.dot(rows, weight, preferred_element_type=f32)
        out_ref[...] = result.astype(out_ref.dtype)


def finish_kernel(*refs, half, kv_local, chunks, width):
    aug_ref, state_ref = refs[:2]
    pool_refs = refs[2 : 2 + chunks]
    weight_ref = refs[2 + chunks]
    part = aug_ref.shape[0] // (2 * width // HD)
    rest = refs[3 + chunks :]
    att_ref, *proj_refs, mine_ref = rest[2 * half :]
    if half:
        send_refs, proj_refs = proj_refs[: PIECES - 1], proj_refs[PIECES - 1 :]
        proj_refs, res_refs = proj_refs[:PIECES], proj_refs[PIECES:]
        project(send_refs, rest[0][...], weight_ref, range(1, PIECES))
    group = width // (kv_local * HD)
    size = group * part
    for c in range(kv_local):
        at = slice((half * kv_local + c) * size, (half * kv_local + c + 1) * size)
        if chunks:
            state = extended(aug_ref[at, :], state_ref[at, :], pool_refs, c)
        else:
            state = unpack(state_ref[at, :])
        shift = value_shift(c)
        result = (state[2][:, shift : shift + HD] / state[1]).astype(bf16)
        for g in range(group):
            h = c * group + g
            mine_ref[:, h * HD : (h + 1) * HD] = result[g * part : (g + 1) * part]
    if half:
        mine = pl.multiple_of(half_start(2 * part, 1), part)
        theirs = pl.multiple_of(half_start(2 * part, 0), part)
        att_ref[pl.ds(mine, part), :] = mine_ref[...]
        att_ref[pl.ds(theirs, part), :] = rest[0][...]
        for k, res_ref in enumerate(res_refs):
            res_ref[...] = rest[1][pl.ds(mine, part), piece(rest[1].shape[1], k)]
    else:
        att_ref[...] = mine_ref[...]
    project(proj_refs, mine_ref[...], weight_ref, range(PIECES if half else 1))


def finish_attention(aug, state, pools, out_weight, half, kv_local, rows, other):
    width = out_weight.shape[0]
    part = rows // 2
    keys = sum(item.shape[0] for item in pools)
    depth = out_weight.shape[1]
    sent = pieces_of(part, depth, bf16)
    if half:
        shapes = (*sent[:-1], *pieces_of(part, depth, f32), *pieces_of(part, depth, bf16))
    else:
        shapes = sent[-1:]
    return pl.pallas_call(
        functools.partial(
            finish_kernel, half=half, kv_local=kv_local, chunks=len(pools), width=width
        ),
        out_shape=(jax.ShapeDtypeStruct((rows if half else part, width), bf16), *shapes),
        in_specs=[VMEM] * (3 + len(pools) + len(other)),
        out_specs=(VMEM,) * (1 + len(shapes)),
        scratch_shapes=[pltpu.VMEM((part, width), bf16)],
        compiler_params=PARAMS,
        cost_estimate=attention_cost(aug.shape[0] // 2, keys + 512),
        name="attend_finish",
    )(aug, state, *pools, out_weight, *other)


def normalized(values_in, gain):
    values = values_in.astype(f32)
    scale = lax.rsqrt(jnp.mean(values * values, axis=-1, keepdims=True) + EPSILON)
    return (values * scale * gain.astype(f32)).astype(bf16)


def stage_kernel(*refs):
    count = len(refs) // 2
    for copy in fetch(zip(refs[:count], refs[count : 2 * count]), refs[-1]):
        copy.wait()


def stage(weights):
    return pl.pallas_call(
        stage_kernel,
        out_shape=tuple(pltpu.VMEM(w.shape, w.dtype) for w in weights),
        in_specs=[HBM] * len(weights),
        out_specs=(VMEM,) * len(weights),
        scratch_shapes=[pltpu.SemaphoreType.DMA((len(weights),))],
        compiler_params=pltpu.CompilerParams(vmem_limit_bytes=1024 * 1024),
        cost_estimate=pl.CostEstimate(
            flops=0, bytes_accessed=sum(2 * w.size for w in weights), transcendentals=0
        ),
        name="stage",
    )(*in_hbm(weights))


def gained(rows, gain_ref, k):
    return (wide(rows) * wide(gain_ref[:, piece(gain_ref.shape[1], k)])).astype(bf16)


def inverse_rms(row_refs):
    squares = [jnp.sum(wide(ref[...]) ** 2, axis=-1, keepdims=True) for ref in row_refs]
    depth = sum(ref.shape[1] for ref in row_refs)
    return lax.rsqrt(sum(squares) / depth + EPSILON)


def times(rows, weight_ref, k, flipped=False):
    if flipped:
        return scores_of(weight_ref[:, piece(weight_ref.shape[1], k)], rows)
    weight = weight_ref[piece(weight_ref.shape[0], k), :]
    return jnp.dot(rows, weight, preferred_element_type=f32)


def early_kernel(rows_ref, gain_ref, *refs, k, flips):
    rows = gained(rows_ref[...], gain_ref, k)
    count = len(flips)
    for weight_ref, out_ref, flipped in zip(refs[:count], refs[count:], flips):
        out_ref[...] = times(rows, weight_ref, k, flipped)


def early_products(rows, gain, weights, k=0, flips=(False, False)):
    count = rows.shape[0]
    shapes = [
        jax.ShapeDtypeStruct((w.shape[0], count) if flipped else (count, w.shape[1]), f32)
        for w, flipped in zip(weights, flips)
    ]
    return pl.pallas_call(
        functools.partial(early_kernel, k=k, flips=flips),
        out_shape=tuple(shapes),
        in_specs=[VMEM] * (2 + len(weights)),
        out_specs=(VMEM,) * len(weights),
        compiler_params=PARAMS,
        name="early_piece",
    )(rows, gain.reshape(1, -1), *weights)


def mlp_kernel(*refs, second, early):
    row_refs, (gain_ref, gate_ref, up_ref, down_ref) = refs[:PIECES], refs[PIECES : PIECES + 4]
    refs = refs[PIECES + 4 :]
    sums = [0.0, 0.0]
    if early:
        sums, refs = [ref[...] for ref in refs[:2]], refs[2:]
    if second:
        project(refs[1:PIECES], refs[0][...], down_ref, range(PIECES - 1))
    scale = inverse_rms(row_refs)
    for k in range(early, PIECES):
        rows = gained(row_refs[k][...], gain_ref, k)
        sums = [item + times(rows, ref, k) for item, ref in zip(sums, (gate_ref, up_ref))]
    gate, upward = sums
    hidden = (jax.nn.silu(gate * scale) * (upward * scale)).astype(bf16)
    if second:
        project(refs[PIECES:], hidden, down_ref, range(PIECES))
    else:
        refs[0][...] = hidden
        project(refs[1:], hidden, down_ref, [PIECES - 1])


def feed_forward(rows, early, gain, gate_weight, up_weight, down_weight, other=()):
    count = rows[0].shape[0]
    depth, width = gate_weight.shape
    sent = pieces_of(count, depth, bf16)
    if other:
        shapes = (*sent[:-1], *pieces_of(count, depth, f32))
    else:
        shapes = (jax.ShapeDtypeStruct((count, width), bf16), sent[-1])
    return pl.pallas_call(
        functools.partial(mlp_kernel, second=len(other) > 0, early=min(len(early), 1)),
        out_shape=shapes,
        in_specs=[VMEM] * (PIECES + 4 + len(early) + len(other)),
        out_specs=(VMEM,) * len(shapes),
        compiler_params=PARAMS,
        cost_estimate=pl.CostEstimate(
            flops=6 * count * depth * width, bytes_accessed=6 * depth * width, transcendentals=0
        ),
        name="feed_forward",
    )(
        *rows,
        gain.reshape(1, depth),
        *in_vmem((gate_weight, up_weight, down_weight)),
        *early,
        *other,
    )


def next_kernel(*refs, half):
    row_refs, refs = refs[:PIECES], refs[PIECES:]
    gain_ref, query_ref, keyval_ref = refs[:3]
    if half:
        query, keyval = refs[3][...], refs[4][...]
        refs = (*refs[:3], *refs[5:])
        for k in range(PIECES - 1):
            rows = gained(row_refs[k][...], gain_ref, k)
            query = query + times(rows, query_ref, k)
            keyval = keyval + times(rows, keyval_ref, k, True)
        scale = inverse_rms(row_refs)
        across = jnp.broadcast_to(scale, (scale.shape[0], LANES)).T[0:1, :]
        query, keyval = (query * scale).astype(bf16), (keyval * across).astype(bf16)
    else:
        normed = normalized(joined(row_refs), gain_ref[...])
        query = jnp.dot(normed, query_ref[...], preferred_element_type=f32).astype(bf16)
        keyval = scores_of(keyval_ref[...], normed).astype(bf16)
        query_out, keyval_out = refs[3:]
        query_out[...] = query
        keyval_out[...] = keyval
        return
    query_in, keyval_in = refs[3:5]
    query_out, keyval_out, residual_out = refs[5 + PIECES :]
    part = query.shape[0]
    mine = pl.multiple_of(half_start(2 * part, 1), part)
    theirs = pl.multiple_of(half_start(2 * part, 0), part)
    query_out[pl.ds(mine, part), :] = query
    query_out[pl.ds(theirs, part), :] = query_in[...]

    @pl.when(mine == 0)
    def _():
        keyval_out[:, :part] = keyval
        keyval_out[:, part:] = keyval_in[...]

    @pl.when(mine != 0)
    def _():
        keyval_out[:, :part] = keyval_in[...]
        keyval_out[:, part:] = keyval

    share = residual_out.shape[0]
    place = lax.axis_index("tp") * share
    at = pl.multiple_of(lax.rem(place, part), share)
    held = (place >= mine) & (place < mine + part)
    for k in range(PIECES):
        ours = row_refs[k][pl.ds(at, share), :]
        others = refs[5 + k][pl.ds(at, share), :]
        residual_out[:, piece(residual_out.shape[1], k)] = jnp.where(held, ours, others)


def next_projections(rows, gain, query_weight, keyval_weight, other):
    count = rows[0].shape[0]
    depth = query_weight.shape[0]
    widths = (query_weight.shape[1], keyval_weight.shape[0])
    half = len(other) > 0
    out_rows = 2 * count if half else count
    shapes = [(out_rows, widths[0]), (widths[1], out_rows)]
    if half:
        shapes.append((out_rows // lax.axis_size("tp"), depth))
    return pl.pallas_call(
        functools.partial(next_kernel, half=half),
        out_shape=tuple(jax.ShapeDtypeStruct(shape, bf16) for shape in shapes),
        in_specs=[VMEM] * (PIECES + 3 + len(other)),
        out_specs=(VMEM,) * len(shapes),
        compiler_params=PARAMS,
        cost_estimate=pl.CostEstimate(
            flops=2 * count * depth * sum(widths),
            bytes_accessed=2 * depth * sum(widths),
            transcendentals=0,
        ),
        name="next_layer",
    )(*rows, gain.reshape(1, depth), *in_vmem([query_weight]), keyval_weight, *other)


def trade(value, axis, bit):
    size = lax.axis_size(axis)
    return lax.ppermute(value, axis, [(i, i ^ bit) for i in range(size)])


def cross(value, even_bit, odd_bit):
    size = lax.axis_size("req")
    pairs = [(i, i ^ (odd_bit if i % 2 else even_bit)) for i in range(size)]
    return lax.ppermute(value, "req", pairs)


def trades(values, bit):
    return [trade(value, "tp", bit) for value in values]


def each(join, *pieces):
    return [join(*items) for items in zip(*pieces)]


def add_pair(mine, got):
    return (mine + wide(got)).astype(bf16)


def pairs_in_turn(mine, got, weights):
    last = add_pair(mine[-1], got[-1])
    _, rest, weights = lax.optimization_barrier((last, got[:-1], weights))
    return [*each(add_pair, mine[:-1], rest), last], weights


def add_rows(pair, rows, got):
    return (wide(rows) + (wide(pair) + wide(got))).astype(bf16)


def wide(value):
    return value.astype(f32)


def per_device(
    new_query,
    new_keyval,
    residual_in,
    leaf_cache,
    leaf_length,
    new_counts,
    request_mid,
    mid_root,
    node_length,
    prefix_pool,
    page_node,
    page_rank,
    out_weight,
    norm_gain,
    gate_weight,
    up_weight,
    down_weight,
    next_gain,
    query_weight,
    keyval_weight,
):
    rows = new_query.shape[0]
    part = rows // 2
    kv_local = new_keyval.shape[1] // (2 * HD)
    pool = prepare(page_node, page_rank, node_length, mid_root, prefix_pool)
    local_args = (new_query, new_keyval, leaf_cache, leaf_length, new_counts, request_mid)
    if lax.axis_size("req") == 8:
        first = cross(pool, 2, 4)
        second = cross(pool, 4, 2)
        beside = trade(pool, "req", 1)
        aug, state = start_attention(*local_args, [pool, beside])
        first, aug, state = lax.optimization_barrier((first, aug, state))
        corner = cross(first, 4, 2)
        first, second = lax.optimization_barrier((first, second))
        near = [first, second, trade(first, "req", 1), trade(second, "req", 1)]
        state = extend_attention(aug, state, near, kv_local)
        state, down_weight = lax.optimization_barrier((state, down_weight))
        corner, state, down_weight = lax.optimization_barrier(
            (corner, state, *stage([down_weight]))
        )
        corner_other = trade(corner, "req", 1)
        state = extend_attention(aug, state, [corner], kv_local)
        pools = [corner_other]
    else:
        every = lax.all_gather(pool, "req", axis=0)
        holders = every.shape[0]
        aug, state = start_attention(*local_args, [pool])
        places = (lax.axis_index("req") + 1 + jnp.arange(holders - 1)) % holders
        step = 4
        for i in range(0, holders - 1, step):
            chunk = every[places[i : i + step]].reshape(-1, pool.shape[1])
            state = extend_attention(aug, state, [chunk], kv_local)
        pools = []

    theirs_att, *theirs_proj = finish_attention(
        aug, state, pools, out_weight, 0, kv_local, rows, ()
    )
    attention, *mine_proj = finish_attention(
        aug, state, pools, out_weight, 1, kv_local, rows, (theirs_att, residual_in)
    )
    theirs_proj = theirs_proj + mine_proj[: PIECES - 1]
    mine_proj, res_mine = mine_proj[PIECES - 1 : -PIECES], mine_proj[-PIECES:]

    mine = half_start(rows, 1)
    theirs = half_start(rows, 0)
    depth = residual_in.shape[1]
    if lax.axis_size("tp") == 4:
        got = trades(theirs_proj, 1)
        pair, (gate_weight, up_weight) = pairs_in_turn(
            mine_proj[::-1], got[::-1], (gate_weight, up_weight)
        )
        pair = pair[::-1]
        got = trades(pair, 2)
        got[-1], *staged = lax.optimization_barrier((got[-1], *stage([gate_weight, up_weight])))
        mlp = (*staged, down_weight)
        mixed_mine = each(add_rows, pair, res_mine, got)
        mixed_theirs = trades(mixed_mine, 1)
        hidden, last = feed_forward(mixed_mine, (), norm_gain, *mlp)
        last = trade(last, "tp", 1)
        early = early_products(mixed_theirs[0], norm_gain, mlp[:2])
        _, mixed_theirs[1:] = lax.optimization_barrier((early, mixed_theirs[1:]))
        result = feed_forward(mixed_theirs, early, norm_gain, *mlp, [hidden])
        got = [*trades(result[: PIECES - 1], 1), last]
        mlp_theirs = result[PIECES - 1 :]
        pair, (query_weight,) = pairs_in_turn(mlp_theirs, got, (query_weight,))
        got = trades(pair, 2)
        got[-1], query_weight = lax.optimization_barrier((got[-1], *stage([query_weight])))
        layer_theirs = each(add_rows, pair, mixed_theirs, got)
        layer_mine = trades(layer_theirs, 1)
    else:
        res_mine = jnp.concatenate(res_mine, axis=1)
        res_theirs = lax.dynamic_slice_in_dim(residual_in, theirs, part, 0)

        def in_order(theirs_part, mine_part):
            both = jnp.stack([theirs_part, mine_part])
            return jnp.where(mine == 0, both[::-1], both).reshape(rows, -1)

        theirs_proj = jnp.concatenate([wide(item) for item in theirs_proj], axis=1)
        mine_proj = jnp.concatenate(mine_proj, axis=1)
        total = lax.psum(in_order(theirs_proj, mine_proj), "tp")
        mixed = (wide(in_order(res_theirs, res_mine)) + total).astype(bf16)
        mixed_halves = [
            [mixed[h * part : (h + 1) * part, piece(depth, k)] for k in range(PIECES)]
            for h in range(2)
        ]
        mlp_weights = (gate_weight, up_weight, down_weight)
        hidden, last = feed_forward(mixed_halves[0], (), norm_gain, *mlp_weights)
        result = feed_forward(mixed_halves[1], (), norm_gain, *mlp_weights, [hidden])
        halves = [[*result[: PIECES - 1], last], result[PIECES - 1 :]]
        mlp = [jnp.concatenate([wide(item) for item in half], axis=1) for half in halves]
        mlp = lax.psum(jnp.concatenate(mlp, axis=0), "tp")
        layer = (wide(mixed) + mlp).astype(bf16)
        layer = [layer[:, piece(depth, k)] for k in range(PIECES)]
        layer_mine = [lax.dynamic_slice_in_dim(item, mine, part, 0) for item in layer]
        layer_theirs = [lax.dynamic_slice_in_dim(item, theirs, part, 0) for item in layer]
    weights = (next_gain, query_weight, keyval_weight.T)
    other = next_projections(layer_theirs, *weights, ())
    _, arrived = lax.optimization_barrier((other, layer_mine[-1]))
    early = early_products(arrived, next_gain, weights[1:], PIECES - 1, (False, True))
    next_query, next_keyval, residual_out = next_projections(
        layer_mine, *weights, (*early, *other, *layer_theirs)
    )
    return (attention, residual_out, next_query, next_keyval.T)


def solution(mesh):
    in_specs = (
        P("req", "tp"),
        P("req", "tp"),
        P("req", None),
        P("req", None, "tp"),
        P("req"),
        P("req", None),
        P("req"),
        P(),
        P(),
        P("req", None, "tp"),
        P("req"),
        P("req"),
        P("tp", None),
        P(),
        P(None, "tp"),
        P(None, "tp"),
        P("tp", None),
        P(),
        P(None, "tp"),
        P(None, "tp"),
    )
    out_specs = (P("req", "tp"), P(("req", "tp"), None), P("req", "tp"), P("req", "tp"))
    return jax.shard_map(
        per_device, mesh=mesh, in_specs=in_specs, out_specs=out_specs, check_vma=False
    )
```

```python
import functools
import math

import jax
import jax.numpy as jnp
from jax import lax
from jax.experimental import pallas as pl
from jax.experimental.pallas import tpu as pltpu
from jax.sharding import PartitionSpec as P

HD = 80
ROOTS = 2
MIDS = 6
LANES = 128
MASKED = -1e30
EPSILON = 1e-05
RATE = math.log2(math.e) / math.sqrt(HD)

PIECES = 2

bf16 = jnp.bfloat16
f32 = jnp.float32
i32 = jnp.int32
HBM = pl.BlockSpec(memory_space=pltpu.HBM)
VMEM = pl.BlockSpec(memory_space=pltpu.VMEM)
SMEM = pl.BlockSpec(memory_space=pltpu.SMEM)
PARAMS = pltpu.CompilerParams(vmem_limit_bytes=24 * 1024 * 1024)


def padded(width):
    return -(-width // LANES) * LANES


def key_start(c):
    return c * 2 * HD // LANES * LANES


def key_shift(c):
    return c * 2 * HD % LANES


def value_start(c):
    return (c * 2 * HD + HD) // LANES * LANES


def value_shift(c):
    return (c * 2 * HD + HD) % LANES


def key_window(ref, c):
    first = ref[:, key_start(c) : key_start(c) + LANES]
    last = ref[:, ref.shape[1] - LANES :]
    return jnp.concatenate([first, last], axis=1)


def value_window(ref, c):
    stop = min(value_start(c) + 2 * LANES, ref.shape[1])
    return ref[:, value_start(c) : stop]


def scores_of(query, keys):
    return lax.dot_general(query, keys, (((1,), (1,)), ((), ())), preferred_element_type=f32)


def fetch(pairs, sems):
    copies = [pltpu.make_async_copy(a, b, sems.at[i]) for i, (a, b) in enumerate(pairs)]
    for copy in copies:
        copy.start()
    return copies


def piece(width, k):
    cut = width * 9 // 20
    return slice(cut, width) if k else slice(0, cut)


def pieces_of(rows, width, dtype):
    places = [piece(width, k) for k in range(PIECES)]
    return tuple(jax.ShapeDtypeStruct((rows, p.stop - p.start), dtype) for p in places)


def joined(refs):
    return jnp.concatenate([ref[...] for ref in refs], axis=1)


def in_hbm(values):
    return [pltpu.with_memory_space_constraint(value, pltpu.HBM) for value in values]


def in_vmem(values):
    return [pltpu.with_memory_space_constraint(value, pltpu.VMEM) for value in values]


def prep_kernel(
    node_hbm, rank_hbm, length_hbm, root_hbm, pool_hbm, out_ref,
    node_ref, rank_ref, length_ref, root_ref, pool_ref, sems,
):
    pairs = (
        (pool_hbm, pool_ref),
        (node_hbm, node_ref),
        (rank_hbm, rank_ref),
        (length_hbm, length_ref),
        (root_hbm, root_ref),
    )
    pool_copy, *copies = fetch(pairs, sems)
    for copy in copies:
        copy.wait()
    pages, size, width = pool_ref.shape
    free = out_ref.shape[1] - width
    lane = lax.broadcasted_iota(i32, (size, free), 1)
    slot = lax.broadcasted_iota(i32, (size, free), 0)
    root = jnp.full((size, free), -2, i32)
    for m in range(MIDS):
        root = jnp.where(lane == m, root_ref[m], root)
    hidden = jnp.where(lane < MIDS, MASKED, 0.0)
    for p in range(pages):
        node = node_ref[p]
        left = length_ref[jnp.maximum(node, 0)] - size * rank_ref[p]
        seen = ((root == node) | (lane + ROOTS == node)) & (slot < left)
        rows = slice(p * size, (p + 1) * size)
        out_ref[rows, width:] = jnp.where(seen, 0.0, hidden).astype(bf16)
    pool_copy.wait()
    out_ref[:, :width] = pool_ref[...].reshape(pages * size, width)


def prepare(page_node, page_rank, node_length, mid_root, prefix_pool):
    pages, size, width = prefix_pool.shape
    tables = (page_node, page_rank, node_length, mid_root)
    return pl.pallas_call(
        prep_kernel,
        out_shape=jax.ShapeDtypeStruct((pages * size, padded(width + MIDS)), bf16),
        in_specs=[HBM] * 5,
        out_specs=VMEM,
        scratch_shapes=[pltpu.SMEM(t.shape, i32) for t in tables]
        + [pltpu.VMEM(prefix_pool.shape, bf16), pltpu.SemaphoreType.DMA((5,))],
        compiler_params=PARAMS,
        name="pool_rows",
    )(*in_hbm((*tables, prefix_pool)))


def half_start(rows, half):
    parity = lax.rem(lax.axis_index("tp"), 2)
    return (parity if half else 1 - parity) * (rows // 2)


def fold(scores, values, state):
    top = functools.reduce(jnp.maximum, [jnp.max(s, axis=1, keepdims=True) for s in scores])
    if state is not None:
        top = jnp.maximum(top, state[0])
    total, weighted = None, None
    for s, v in zip(scores, values):
        raised = jnp.exp2((s - top) * RATE)
        part = jnp.sum(raised, axis=1, keepdims=True)
        mixed = jnp.dot(raised.astype(bf16), v, preferred_element_type=f32)
        total = part if total is None else total + part
        weighted = mixed if weighted is None else weighted + mixed
    if state is not None:
        factor = jnp.exp2((state[0] - top) * RATE)
        total = total + state[1] * factor
        weighted = weighted + state[2] * factor
    return top, total, weighted


def pack(top, total, weighted):
    lane = lax.broadcasted_iota(i32, weighted.shape, 1)
    return jnp.where(lane == 0, top, jnp.where(lane == 1, total, weighted))


def unpack(state):
    return state[:, 0:1], state[:, 1:2], state


def local_kernel(
    count_hbm, mid_hbm, leaf_len_hbm, query_ref, keyval_ref, leaf_ref, *refs, chunks
):
    pool_refs = refs[:chunks]
    aug_ref, state_ref, count_ref, mid_ref, leaf_len_ref, sems = refs[chunks:]
    pairs = ((count_hbm, count_ref), (mid_hbm, mid_ref), (leaf_len_hbm, leaf_len_ref))
    for copy in fetch(pairs, sems):
        copy.wait()
    rows = query_ref.shape[0]
    part = rows // 2
    width = keyval_ref.shape[1]
    requests, slots, _ = leaf_ref.shape
    kv_local = width // (2 * HD)
    group = query_ref.shape[1] // (kv_local * HD)
    lane = lax.broadcasted_iota(i32, (part, LANES), 1)
    zero = jnp.zeros((part, LANES), i32)
    leaf_all = leaf_ref[...].reshape(requests * slots, width)
    leaf_at = lax.broadcasted_iota(i32, (part, requests * slots), 1)
    for half in range(2):
        first = half_start(rows, half)
        row = lax.broadcasted_iota(i32, (part, LANES), 0) + first
        start, low, high, mid = zero, zero, zero, zero
        begin = jnp.int32(0)
        for r in range(requests):
            here = row >= begin
            start = jnp.where(here, begin, start)
            low = jnp.where(here, r * slots, low)
            high = jnp.where(here, r * slots + leaf_len_ref[r], high)
            mid = jnp.where(here, mid_ref[r], mid)
            begin = begin + count_ref[0, r]
        chosen = jnp.where(lane == width % LANES + mid, 1.0, 0.0).astype(bf16)
        leaf_ok = (leaf_at >= low[:, 0:1]) & (leaf_at < high[:, 0:1])
        new_ok = (lane >= start) & (lane <= row)
        tokens = query_ref[pl.ds(pl.multiple_of(first, part), part), :]
        for c in range(kv_local):
            base = (half * kv_local + c) * group * part
            block = slice(base, base + group * part)
            key0, val0 = key_start(c), value_start(c)
            shift = key_shift(c)
            for g in range(group):
                h = c * group + g
                at = slice(base + g * part, base + (g + 1) * part)
                aug_ref[at, :LANES] = jnp.zeros((part, LANES), bf16)
                aug_ref[at, shift : shift + HD] = tokens[:, h * HD : (h + 1) * HD]
                aug_ref[at, LANES:] = chosen
            query = aug_ref[block, :]
            narrow = query[:, :LANES]
            s_leaf = scores_of(narrow, leaf_all[:, key0 : key0 + LANES])
            s_leaf = jnp.where(leaf_ok[None], s_leaf.reshape(group, part, -1), MASKED)
            s_new = scores_of(narrow, keyval_ref[:, key0 : key0 + LANES])
            s_new = jnp.where(new_ok[None], s_new.reshape(group, part, -1), MASKED)
            scores = [s_leaf.reshape(group * part, -1), s_new.reshape(group * part, -1)]
            stop = min(val0 + 2 * LANES, width)
            fill = val0 + 2 * LANES - stop
            values = [leaf_all[:, val0:stop], keyval_ref[:, val0:stop]]
            if fill:
                values = [
                    jnp.concatenate([v, jnp.zeros((v.shape[0], fill), bf16)], axis=1) for v in values
                ]
            for pool_ref in pool_refs:
                scores.append(scores_of(query, key_window(pool_ref, c)))
                values.append(value_window(pool_ref, c))
            state_ref[block, :] = pack(*fold(scores, values, None))


def start_attention(new_query, new_keyval, leaf, leaf_length, counts, request_mid, pools):
    rows, query_width = new_query.shape
    heads = query_width // HD
    tables = (counts, request_mid, leaf_length)
    keys = leaf.shape[0] * leaf.shape[1] + rows + sum(item.shape[0] for item in pools)
    return pl.pallas_call(
        functools.partial(local_kernel, chunks=len(pools)),
        out_shape=(
            jax.ShapeDtypeStruct((heads * rows, 2 * LANES), bf16),
            jax.ShapeDtypeStruct((heads * rows, 2 * LANES), f32),
        ),
        in_specs=[HBM] * 3 + [VMEM] * (3 + len(pools)),
        out_specs=(VMEM, VMEM),
        scratch_shapes=[pltpu.SMEM(t.shape, i32) for t in tables] + [pltpu.SemaphoreType.DMA((3,))],
        compiler_params=PARAMS,
        cost_estimate=attention_cost(heads * rows, keys),
        name="attend_local",
    )(*in_hbm(tables), new_query, new_keyval, leaf, *pools)


def attention_cost(rows, keys):
    return pl.CostEstimate(
        flops=8 * LANES * rows * keys, bytes_accessed=8 * rows * 2 * LANES, transcendentals=rows * keys
    )


def extended(query, state, pool_refs, c):
    scores = [scores_of(query, key_window(ref, c)) for ref in pool_refs]
    values = [value_window(ref, c) for ref in pool_refs]
    return fold(scores, values, unpack(state))


def chunk_kernel(*refs, blocks):
    aug_ref, state_ref = refs[:2]
    pool_refs, out_ref = refs[2:-1], refs[-1]
    size = aug_ref.shape[0] // blocks
    for b in range(blocks):
        at = slice(b * size, (b + 1) * size)
        state = extended(aug_ref[at, :], state_ref[at, :], pool_refs, b % (blocks // 2))
        out_ref[at, :] = pack(*state)


def extend_attention(aug, state, pools, kv_local):
    keys = sum(item.shape[0] for item in pools)
    return pl.pallas_call(
        functools.partial(chunk_kernel, blocks=2 * kv_local),
        out_shape=jax.ShapeDtypeStruct(state.shape, f32),
        in_specs=[VMEM] * (2 + len(pools)),
        out_specs=VMEM,
        compiler_params=PARAMS,
        cost_estimate=attention_cost(aug.shape[0], keys),
        name="attend_pages",
    )(aug, state, *pools)


def project(out_refs, rows, weight_ref, places):
    for out_ref, k in zip(out_refs, places):
        weight = weight_ref[:, piece(weight_ref.shape[1], k)]
        result = jnp.dot(rows, weight, preferred_element_type=f32)
        out_ref[...] = result.astype(out_ref.dtype)


def finish_kernel(*refs, half, kv_local, chunks, width):
    aug_ref, state_ref = refs[:2]
    pool_refs = refs[2 : 2 + chunks]
    weight_ref = refs[2 + chunks]
    part = aug_ref.shape[0] // (2 * width // HD)
    rest = refs[3 + chunks :]
    att_ref, *proj_refs, mine_ref = rest[2 * half :]
    if half:
        send_refs, proj_refs = proj_refs[: PIECES - 1], proj_refs[PIECES - 1 :]
        proj_refs, res_refs = proj_refs[:PIECES], proj_refs[PIECES:]
        project(send_refs, rest[0][...], weight_ref, range(PIECES - 1))
    group = width // (kv_local * HD)
    size = group * part
    for c in range(kv_local):
        at = slice((half * kv_local + c) * size, (half * kv_local + c + 1) * size)
        if chunks:
            state = extended(aug_ref[at, :], state_ref[at, :], pool_refs, c)
        else:
            state = unpack(state_ref[at, :])
        shift = value_shift(c)
        result = (state[2][:, shift : shift + HD] / state[1]).astype(bf16)
        for g in range(group):
            h = c * group + g
            mine_ref[:, h * HD : (h + 1) * HD] = result[g * part : (g + 1) * part]
    if half:
        mine = pl.multiple_of(half_start(2 * part, 1), part)
        theirs = pl.multiple_of(half_start(2 * part, 0), part)
        att_ref[pl.ds(mine, part), :] = mine_ref[...]
        att_ref[pl.ds(theirs, part), :] = rest[0][...]
        for k, res_ref in enumerate(res_refs):
            res_ref[...] = rest[1][pl.ds(mine, part), piece(rest[1].shape[1], k)]
    else:
        att_ref[...] = mine_ref[...]
    project(proj_refs, mine_ref[...], weight_ref, range(PIECES) if half else [PIECES - 1])


def finish_attention(aug, state, pools, out_weight, half, kv_local, rows, other):
    width = out_weight.shape[0]
    part = rows // 2
    keys = sum(item.shape[0] for item in pools)
    depth = out_weight.shape[1]
    sent = pieces_of(part, depth, bf16)
    if half:
        shapes = (*sent[:-1], *pieces_of(part, depth, f32), *pieces_of(part, depth, bf16))
    else:
        shapes = sent[-1:]
    return pl.pallas_call(
        functools.partial(
            finish_kernel, half=half, kv_local=kv_local, chunks=len(pools), width=width
        ),
        out_shape=(jax.ShapeDtypeStruct((rows if half else part, width), bf16), *shapes),
        in_specs=[VMEM] * (3 + len(pools) + len(other)),
        out_specs=(VMEM,) * (1 + len(shapes)),
        scratch_shapes=[pltpu.VMEM((part, width), bf16)],
        compiler_params=PARAMS,
        cost_estimate=attention_cost(aug.shape[0] // 2, keys + 512),
        name="attend_finish",
    )(aug, state, *pools, out_weight, *other)


def normalized(values_in, gain):
    values = values_in.astype(f32)
    scale = lax.rsqrt(jnp.mean(values * values, axis=-1, keepdims=True) + EPSILON)
    return (values * scale * gain.astype(f32)).astype(bf16)


def stage_kernel(*refs):
    count = len(refs) // 2
    for copy in fetch(zip(refs[:count], refs[count : 2 * count]), refs[-1]):
        copy.wait()


def stage(weights):
    return pl.pallas_call(
        stage_kernel,
        out_shape=tuple(pltpu.VMEM(w.shape, w.dtype) for w in weights),
        in_specs=[HBM] * len(weights),
        out_specs=(VMEM,) * len(weights),
        scratch_shapes=[pltpu.SemaphoreType.DMA((len(weights),))],
        compiler_params=pltpu.CompilerParams(vmem_limit_bytes=1024 * 1024),
        cost_estimate=pl.CostEstimate(
            flops=0, bytes_accessed=sum(2 * w.size for w in weights), transcendentals=0
        ),
        name="stage",
    )(*in_hbm(weights))


def gained(rows, gain_ref, k):
    return (wide(rows) * wide(gain_ref[:, piece(gain_ref.shape[1], k)])).astype(bf16)


def inverse_rms(row_refs):
    squares = [jnp.sum(wide(ref[...]) ** 2, axis=-1, keepdims=True) for ref in row_refs]
    depth = sum(ref.shape[1] for ref in row_refs)
    return lax.rsqrt(sum(squares) / depth + EPSILON)


def times(rows, weight_ref, k, flipped=False):
    if flipped:
        return scores_of(weight_ref[:, piece(weight_ref.shape[1], k)], rows)
    weight = weight_ref[piece(weight_ref.shape[0], k), :]
    return jnp.dot(rows, weight, preferred_element_type=f32)


def early_kernel(*refs, k, flips, terms):
    row_refs, (gain_ref, *refs) = refs[:terms], refs[terms:]
    rows = row_refs[0][...]
    if terms > 1:
        rows = add_rows(rows, row_refs[1][...], row_refs[2][...])
        refs[len(flips)][...] = rows
        refs = (*refs[: len(flips)], *refs[len(flips) + 1 :])
    rows = gained(rows, gain_ref, k)
    count = len(flips)
    for weight_ref, out_ref, flipped in zip(refs[:count], refs[count:], flips):
        out_ref[...] = times(rows, weight_ref, k, flipped)


def early_products(rows, gain, weights, k=0, flips=(False, False)):
    terms = rows if isinstance(rows, tuple) else (rows,)
    rows = terms[0]
    count = rows.shape[0]
    shapes = [
        jax.ShapeDtypeStruct((w.shape[0], count) if flipped else (count, w.shape[1]), f32)
        for w, flipped in zip(weights, flips)
    ]
    if len(terms) > 1:
        shapes.insert(0, jax.ShapeDtypeStruct(rows.shape, bf16))
    return pl.pallas_call(
        functools.partial(early_kernel, k=k, flips=flips, terms=len(terms)),
        out_shape=tuple(shapes),
        in_specs=[VMEM] * (len(terms) + 1 + len(weights)),
        out_specs=(VMEM,) * len(shapes),
        compiler_params=PARAMS,
        name="early_piece",
    )(*terms, gain.reshape(1, -1), *weights)


def mlp_kernel(*refs, second, early):
    row_refs, (gain_ref, gate_ref, up_ref, down_ref) = refs[:PIECES], refs[PIECES : PIECES + 4]
    refs = refs[PIECES + 4 :]
    sums = [0.0, 0.0]
    if early:
        sums, refs = [ref[...] for ref in refs[:2]], refs[2:]
    if second:
        project(refs[1:PIECES], refs[0][...], down_ref, range(PIECES - 1))
    scale = inverse_rms(row_refs)
    for k in range(PIECES - early):
        rows = gained(row_refs[k][...], gain_ref, k)
        sums = [item + times(rows, ref, k) for item, ref in zip(sums, (gate_ref, up_ref))]
    gate, upward = sums
    hidden = (jax.nn.silu(gate * scale) * (upward * scale)).astype(bf16)
    if second:
        project(refs[PIECES:], hidden, down_ref, range(PIECES))
    else:
        refs[0][...] = hidden
        project(refs[1:], hidden, down_ref, [PIECES - 1])


def feed_forward(rows, early, gain, gate_weight, up_weight, down_weight, other=()):
    count = rows[0].shape[0]
    depth, width = gate_weight.shape
    sent = pieces_of(count, depth, bf16)
    if other:
        shapes = (*sent[:-1], *pieces_of(count, depth, f32))
    else:
        shapes = (jax.ShapeDtypeStruct((count, width), bf16), sent[-1])
    return pl.pallas_call(
        functools.partial(mlp_kernel, second=len(other) > 0, early=min(len(early), 1)),
        out_shape=shapes,
        in_specs=[VMEM] * (PIECES + 4 + len(early) + len(other)),
        out_specs=(VMEM,) * len(shapes),
        compiler_params=PARAMS,
        cost_estimate=pl.CostEstimate(
            flops=6 * count * depth * width, bytes_accessed=6 * depth * width, transcendentals=0
        ),
        name="feed_forward",
    )(
        *rows,
        gain.reshape(1, depth),
        *in_vmem((gate_weight, up_weight, down_weight)),
        *early,
        *other,
    )


def next_kernel(*refs, half):
    row_refs, refs = refs[:PIECES], refs[PIECES:]
    gain_ref, query_ref, keyval_ref = refs[:3]
    if half:
        query, keyval = refs[3][...], refs[4][...]
        refs = (*refs[:3], *refs[5:])
        for k in range(PIECES - 1):
            rows = gained(row_refs[k][...], gain_ref, k)
            query = query + times(rows, query_ref, k)
            keyval = keyval + times(rows, keyval_ref, k, True)
        scale = inverse_rms(row_refs)
        across = jnp.broadcast_to(scale, (scale.shape[0], LANES)).T[0:1, :]
        query, keyval = (query * scale).astype(bf16), (keyval * across).astype(bf16)
    else:
        normed = normalized(joined(row_refs), gain_ref[...])
        query = jnp.dot(normed, query_ref[...], preferred_element_type=f32).astype(bf16)
        keyval = scores_of(keyval_ref[...], normed).astype(bf16)
        query_out, keyval_out = refs[3:]
        query_out[...] = query
        keyval_out[...] = keyval
        return
    query_in, keyval_in = refs[3:5]
    query_out, keyval_out, residual_out = refs[5 + PIECES :]
    part = query.shape[0]
    mine = pl.multiple_of(half_start(2 * part, 1), part)
    theirs = pl.multiple_of(half_start(2 * part, 0), part)
    query_out[pl.ds(mine, part), :] = query
    query_out[pl.ds(theirs, part), :] = query_in[...]

    @pl.when(mine == 0)
    def _():
        keyval_out[:, :part] = keyval
        keyval_out[:, part:] = keyval_in[...]

    @pl.when(mine != 0)
    def _():
        keyval_out[:, :part] = keyval_in[...]
        keyval_out[:, part:] = keyval

    share = residual_out.shape[0]
    place = lax.axis_index("tp") * share
    at = pl.multiple_of(lax.rem(place, part), share)
    held = (place >= mine) & (place < mine + part)
    for k in range(PIECES):
        ours = row_refs[k][pl.ds(at, share), :]
        others = refs[5 + k][pl.ds(at, share), :]
        residual_out[:, piece(residual_out.shape[1], k)] = jnp.where(held, ours, others)


def next_projections(rows, gain, query_weight, keyval_weight, other):
    count = rows[0].shape[0]
    depth = query_weight.shape[0]
    widths = (query_weight.shape[1], keyval_weight.shape[0])
    half = len(other) > 0
    out_rows = 2 * count if half else count
    shapes = [(out_rows, widths[0]), (widths[1], out_rows)]
    if half:
        shapes.append((out_rows // lax.axis_size("tp"), depth))
    return pl.pallas_call(
        functools.partial(next_kernel, half=half),
        out_shape=tuple(jax.ShapeDtypeStruct(shape, bf16) for shape in shapes),
        in_specs=[VMEM] * (PIECES + 3 + len(other)),
        out_specs=(VMEM,) * len(shapes),
        compiler_params=PARAMS,
        cost_estimate=pl.CostEstimate(
            flops=2 * count * depth * sum(widths),
            bytes_accessed=2 * depth * sum(widths),
            transcendentals=0,
        ),
        name="next_layer",
    )(*rows, gain.reshape(1, depth), *in_vmem([query_weight]), keyval_weight, *other)


def trade(value, axis, bit):
    size = lax.axis_size(axis)
    return lax.ppermute(value, axis, [(i, i ^ bit) for i in range(size)])


def cross(value, even_bit, odd_bit):
    size = lax.axis_size("req")
    pairs = [(i, i ^ (odd_bit if i % 2 else even_bit)) for i in range(size)]
    return lax.ppermute(value, "req", pairs)


def trades(values, bit):
    return [trade(value, "tp", bit) for value in values]


def each(join, *pieces):
    return [join(*items) for items in zip(*pieces)]


def add_pair(mine, got):
    return (mine + wide(got)).astype(bf16)


def pairs_in_turn(mine, got, weights):
    last = add_pair(mine[-1], got[-1])
    _, rest, weights = lax.optimization_barrier((last, got[:-1], weights))
    return [*each(add_pair, mine[:-1], rest), last], weights


def add_rows(pair, rows, got):
    return (wide(rows) + (wide(pair) + wide(got))).astype(bf16)


def wide(value):
    return value.astype(f32)


def per_device(
    new_query,
    new_keyval,
    residual_in,
    leaf_cache,
    leaf_length,
    new_counts,
    request_mid,
    mid_root,
    node_length,
    prefix_pool,
    page_node,
    page_rank,
    out_weight,
    norm_gain,
    gate_weight,
    up_weight,
    down_weight,
    next_gain,
    query_weight,
    keyval_weight,
):
    rows = new_query.shape[0]
    part = rows // 2
    kv_local = new_keyval.shape[1] // (2 * HD)
    pool = prepare(page_node, page_rank, node_length, mid_root, prefix_pool)
    local_args = (new_query, new_keyval, leaf_cache, leaf_length, new_counts, request_mid)
    if lax.axis_size("req") == 8:
        first = cross(pool, 2, 4)
        second = cross(pool, 4, 2)
        beside = trade(pool, "req", 1)
        aug, state = start_attention(*local_args, [pool, beside])
        first, aug, state = lax.optimization_barrier((first, aug, state))
        corner = cross(first, 4, 2)
        first, second = lax.optimization_barrier((first, second))
        near = [first, second, trade(first, "req", 1), trade(second, "req", 1)]
        state = extend_attention(aug, state, near, kv_local)
        state, down_weight = lax.optimization_barrier((state, down_weight))
        corner, state, down_weight = lax.optimization_barrier(
            (corner, state, *stage([down_weight]))
        )
        corner_other = trade(corner, "req", 1)
        state = extend_attention(aug, state, [corner], kv_local)
        pools = [corner_other]
    else:
        every = lax.all_gather(pool, "req", axis=0)
        holders = every.shape[0]
        aug, state = start_attention(*local_args, [pool])
        places = (lax.axis_index("req") + 1 + jnp.arange(holders - 1)) % holders
        step = 4
        for i in range(0, holders - 1, step):
            chunk = every[places[i : i + step]].reshape(-1, pool.shape[1])
            state = extend_attention(aug, state, [chunk], kv_local)
        pools = []

    theirs_att, *theirs_proj = finish_attention(
        aug, state, pools, out_weight, 0, kv_local, rows, ()
    )
    attention, *mine_proj = finish_attention(
        aug, state, pools, out_weight, 1, kv_local, rows, (theirs_att, residual_in)
    )
    theirs_proj = mine_proj[: PIECES - 1] + theirs_proj
    mine_proj, res_mine = mine_proj[PIECES - 1 : -PIECES], mine_proj[-PIECES:]

    mine = half_start(rows, 1)
    theirs = half_start(rows, 0)
    depth = residual_in.shape[1]
    if lax.axis_size("tp") == 4:
        got = trades(theirs_proj, 1)
        pair, (gate_weight, up_weight) = pairs_in_turn(mine_proj, got, (gate_weight, up_weight))
        got = trades(pair, 2)
        got[-1], *staged = lax.optimization_barrier((got[-1], *stage([gate_weight, up_weight])))
        mlp = (*staged, down_weight)
        lead, *early = early_products(
            (pair[-1], res_mine[-1], got[-1]), norm_gain, mlp[:2], PIECES - 1
        )
        mixed_mine = [*each(add_rows, pair[:-1], res_mine[:-1], got[:-1]), lead]
        mixed_theirs = trades(mixed_mine, 1)
        hidden, last = feed_forward(mixed_mine, early, norm_gain, *mlp)
        last = trade(last, "tp", 1)
        early = early_products(mixed_theirs[-1], norm_gain, mlp[:2], PIECES - 1)
        _, mixed_theirs[:-1] = lax.optimization_barrier((early, mixed_theirs[:-1]))
        result = feed_forward(mixed_theirs, early, norm_gain, *mlp, [hidden])
        got = [*trades(result[: PIECES - 1], 1), last]
        mlp_theirs = result[PIECES - 1 :]
        pair, (query_weight,) = pairs_in_turn(mlp_theirs, got, (query_weight,))
        got = trades(pair, 2)
        got[-1], query_weight = lax.optimization_barrier((got[-1], *stage([query_weight])))
        layer_theirs = each(add_rows, pair, mixed_theirs, got)
        layer_mine = trades(layer_theirs, 1)
    else:
        res_mine = jnp.concatenate(res_mine, axis=1)
        res_theirs = lax.dynamic_slice_in_dim(residual_in, theirs, part, 0)

        def in_order(theirs_part, mine_part):
            both = jnp.stack([theirs_part, mine_part])
            return jnp.where(mine == 0, both[::-1], both).reshape(rows, -1)

        theirs_proj = jnp.concatenate([wide(item) for item in theirs_proj], axis=1)
        mine_proj = jnp.concatenate(mine_proj, axis=1)
        total = lax.psum(in_order(theirs_proj, mine_proj), "tp")
        mixed = (wide(in_order(res_theirs, res_mine)) + total).astype(bf16)
        mixed_halves = [
            [mixed[h * part : (h + 1) * part, piece(depth, k)] for k in range(PIECES)]
            for h in range(2)
        ]
        mlp_weights = (gate_weight, up_weight, down_weight)
        hidden, last = feed_forward(mixed_halves[0], (), norm_gain, *mlp_weights)
        result = feed_forward(mixed_halves[1], (), norm_gain, *mlp_weights, [hidden])
        halves = [[*result[: PIECES - 1], last], result[PIECES - 1 :]]
        mlp = [jnp.concatenate([wide(item) for item in half], axis=1) for half in halves]
        mlp = lax.psum(jnp.concatenate(mlp, axis=0), "tp")
        layer = (wide(mixed) + mlp).astype(bf16)
        layer = [layer[:, piece(depth, k)] for k in range(PIECES)]
        layer_mine = [lax.dynamic_slice_in_dim(item, mine, part, 0) for item in layer]
        layer_theirs = [lax.dynamic_slice_in_dim(item, theirs, part, 0) for item in layer]
    weights = (next_gain, query_weight, keyval_weight.T)
    other = next_projections(layer_theirs, *weights, ())
    _, arrived = lax.optimization_barrier((other, layer_mine[-1]))
    early = early_products(arrived, next_gain, weights[1:], PIECES - 1, (False, True))
    next_query, next_keyval, residual_out = next_projections(
        layer_mine, *weights, (*early, *other, *layer_theirs)
    )
    return (attention, residual_out, next_query, next_keyval.T)


def solution(mesh):
    in_specs = (
        P("req", "tp"),
        P("req", "tp"),
        P("req", None),
        P("req", None, "tp"),
        P("req"),
        P("req", None),
        P("req"),
        P(),
        P(),
        P("req", None, "tp"),
        P("req"),
        P("req"),
        P("tp", None),
        P(),
        P(None, "tp"),
        P(None, "tp"),
        P("tp", None),
        P(),
        P(None, "tp"),
        P(None, "tp"),
    )
    out_specs = (P("req", "tp"), P(("req", "tp"), None), P("req", "tp"), P("req", "tp"))
    return jax.shard_map(
        per_device, mesh=mesh, in_specs=in_specs, out_specs=out_specs, check_vma=False
    )
```

```python
import functools
import math

import jax
import jax.numpy as jnp
from jax import lax
from jax.experimental import pallas as pl
from jax.experimental.pallas import tpu as pltpu
from jax.sharding import PartitionSpec as P

HD = 80
ROOTS = 2
MIDS = 6
LANES = 128
MASKED = -1e30
EPSILON = 1e-05
RATE = math.log2(math.e) / math.sqrt(HD)

PIECES = 2

bf16 = jnp.bfloat16
f32 = jnp.float32
i32 = jnp.int32
HBM = pl.BlockSpec(memory_space=pltpu.HBM)
VMEM = pl.BlockSpec(memory_space=pltpu.VMEM)
SMEM = pl.BlockSpec(memory_space=pltpu.SMEM)
PARAMS = pltpu.CompilerParams(vmem_limit_bytes=24 * 1024 * 1024)


def padded(width):
    return -(-width // LANES) * LANES


def key_start(c):
    return c * 2 * HD // LANES * LANES


def key_shift(c):
    return c * 2 * HD % LANES


def value_start(c):
    return (c * 2 * HD + HD) // LANES * LANES


def value_shift(c):
    return (c * 2 * HD + HD) % LANES


def key_window(ref, c):
    first = ref[:, key_start(c) : key_start(c) + LANES]
    last = ref[:, ref.shape[1] - LANES :]
    return jnp.concatenate([first, last], axis=1)


def value_window(ref, c):
    stop = min(value_start(c) + 2 * LANES, ref.shape[1])
    return ref[:, value_start(c) : stop]


def scores_of(query, keys):
    return lax.dot_general(query, keys, (((1,), (1,)), ((), ())), preferred_element_type=f32)


def fetch(pairs, sems):
    copies = [pltpu.make_async_copy(a, b, sems.at[i]) for i, (a, b) in enumerate(pairs)]
    for copy in copies:
        copy.start()
    return copies


def piece(width, k):
    cut = width * 2 // 5
    return slice(cut, width) if k else slice(0, cut)


def pieces_of(rows, width, dtype):
    places = [piece(width, k) for k in range(PIECES)]
    return tuple(jax.ShapeDtypeStruct((rows, p.stop - p.start), dtype) for p in places)


def joined(refs):
    return jnp.concatenate([ref[...] for ref in refs], axis=1)


def in_hbm(values):
    return [pltpu.with_memory_space_constraint(value, pltpu.HBM) for value in values]


def in_vmem(values):
    return [pltpu.with_memory_space_constraint(value, pltpu.VMEM) for value in values]


def prep_kernel(
    node_hbm, rank_hbm, length_hbm, root_hbm, pool_hbm, out_ref,
    node_ref, rank_ref, length_ref, root_ref, pool_ref, sems,
):
    pairs = (
        (pool_hbm, pool_ref),
        (node_hbm, node_ref),
        (rank_hbm, rank_ref),
        (length_hbm, length_ref),
        (root_hbm, root_ref),
    )
    pool_copy, *copies = fetch(pairs, sems)
    for copy in copies:
        copy.wait()
    pages, size, width = pool_ref.shape
    free = out_ref.shape[1] - width
    lane = lax.broadcasted_iota(i32, (size, free), 1)
    slot = lax.broadcasted_iota(i32, (size, free), 0)
    root = jnp.full((size, free), -2, i32)
    for m in range(MIDS):
        root = jnp.where(lane == m, root_ref[m], root)
    hidden = jnp.where(lane < MIDS, MASKED, 0.0)
    for p in range(pages):
        node = node_ref[p]
        left = length_ref[jnp.maximum(node, 0)] - size * rank_ref[p]
        seen = ((root == node) | (lane + ROOTS == node)) & (slot < left)
        rows = slice(p * size, (p + 1) * size)
        out_ref[rows, width:] = jnp.where(seen, 0.0, hidden).astype(bf16)
    pool_copy.wait()
    out_ref[:, :width] = pool_ref[...].reshape(pages * size, width)


def prepare(page_node, page_rank, node_length, mid_root, prefix_pool):
    pages, size, width = prefix_pool.shape
    tables = (page_node, page_rank, node_length, mid_root)
    return pl.pallas_call(
        prep_kernel,
        out_shape=jax.ShapeDtypeStruct((pages * size, padded(width + MIDS)), bf16),
        in_specs=[HBM] * 5,
        out_specs=VMEM,
        scratch_shapes=[pltpu.SMEM(t.shape, i32) for t in tables]
        + [pltpu.VMEM(prefix_pool.shape, bf16), pltpu.SemaphoreType.DMA((5,))],
        compiler_params=PARAMS,
        name="pool_rows",
    )(*in_hbm((*tables, prefix_pool)))


def half_start(rows, half):
    parity = lax.rem(lax.axis_index("tp"), 2)
    return (parity if half else 1 - parity) * (rows // 2)


def fold(scores, values, state):
    top = functools.reduce(jnp.maximum, [jnp.max(s, axis=1, keepdims=True) for s in scores])
    if state is not None:
        top = jnp.maximum(top, state[0])
    total, weighted = None, None
    for s, v in zip(scores, values):
        raised = jnp.exp2((s - top) * RATE)
        part = jnp.sum(raised, axis=1, keepdims=True)
        mixed = jnp.dot(raised.astype(bf16), v, preferred_element_type=f32)
        total = part if total is None else total + part
        weighted = mixed if weighted is None else weighted + mixed
    if state is not None:
        factor = jnp.exp2((state[0] - top) * RATE)
        total = total + state[1] * factor
        weighted = weighted + state[2] * factor
    return top, total, weighted


def pack(top, total, weighted):
    lane = lax.broadcasted_iota(i32, weighted.shape, 1)
    return jnp.where(lane == 0, top, jnp.where(lane == 1, total, weighted))


def unpack(state):
    return state[:, 0:1], state[:, 1:2], state


def local_kernel(
    count_hbm, mid_hbm, leaf_len_hbm, query_ref, keyval_ref, leaf_ref, *refs, chunks
):
    pool_refs = refs[:chunks]
    aug_ref, state_ref, count_ref, mid_ref, leaf_len_ref, sems = refs[chunks:]
    pairs = ((count_hbm, count_ref), (mid_hbm, mid_ref), (leaf_len_hbm, leaf_len_ref))
    for copy in fetch(pairs, sems):
        copy.wait()
    rows = query_ref.shape[0]
    part = rows // 2
    width = keyval_ref.shape[1]
    requests, slots, _ = leaf_ref.shape
    kv_local = width // (2 * HD)
    group = query_ref.shape[1] // (kv_local * HD)
    lane = lax.broadcasted_iota(i32, (part, LANES), 1)
    zero = jnp.zeros((part, LANES), i32)
    leaf_all = leaf_ref[...].reshape(requests * slots, width)
    leaf_at = lax.broadcasted_iota(i32, (part, requests * slots), 1)
    for half in range(2):
        first = half_start(rows, half)
        row = lax.broadcasted_iota(i32, (part, LANES), 0) + first
        start, low, high, mid = zero, zero, zero, zero
        begin = jnp.int32(0)
        for r in range(requests):
            here = row >= begin
            start = jnp.where(here, begin, start)
            low = jnp.where(here, r * slots, low)
            high = jnp.where(here, r * slots + leaf_len_ref[r], high)
            mid = jnp.where(here, mid_ref[r], mid)
            begin = begin + count_ref[0, r]
        chosen = jnp.where(lane == width % LANES + mid, 1.0, 0.0).astype(bf16)
        leaf_ok = (leaf_at >= low[:, 0:1]) & (leaf_at < high[:, 0:1])
        new_ok = (lane >= start) & (lane <= row)
        tokens = query_ref[pl.ds(pl.multiple_of(first, part), part), :]
        for c in range(kv_local):
            base = (half * kv_local + c) * group * part
            block = slice(base, base + group * part)
            key0, val0 = key_start(c), value_start(c)
            shift = key_shift(c)
            for g in range(group):
                h = c * group + g
                at = slice(base + g * part, base + (g + 1) * part)
                aug_ref[at, :LANES] = jnp.zeros((part, LANES), bf16)
                aug_ref[at, shift : shift + HD] = tokens[:, h * HD : (h + 1) * HD]
                aug_ref[at, LANES:] = chosen
            query = aug_ref[block, :]
            narrow = query[:, :LANES]
            s_leaf = scores_of(narrow, leaf_all[:, key0 : key0 + LANES])
            s_leaf = jnp.where(leaf_ok[None], s_leaf.reshape(group, part, -1), MASKED)
            s_new = scores_of(narrow, keyval_ref[:, key0 : key0 + LANES])
            s_new = jnp.where(new_ok[None], s_new.reshape(group, part, -1), MASKED)
            scores = [s_leaf.reshape(group * part, -1), s_new.reshape(group * part, -1)]
            stop = min(val0 + 2 * LANES, width)
            fill = val0 + 2 * LANES - stop
            values = [leaf_all[:, val0:stop], keyval_ref[:, val0:stop]]
            if fill:
                values = [
                    jnp.concatenate([v, jnp.zeros((v.shape[0], fill), bf16)], axis=1) for v in values
                ]
            for pool_ref in pool_refs:
                scores.append(scores_of(query, key_window(pool_ref, c)))
                values.append(value_window(pool_ref, c))
            state_ref[block, :] = pack(*fold(scores, values, None))


def start_attention(new_query, new_keyval, leaf, leaf_length, counts, request_mid, pools):
    rows, query_width = new_query.shape
    heads = query_width // HD
    tables = (counts, request_mid, leaf_length)
    keys = leaf.shape[0] * leaf.shape[1] + rows + sum(item.shape[0] for item in pools)
    return pl.pallas_call(
        functools.partial(local_kernel, chunks=len(pools)),
        out_shape=(
            jax.ShapeDtypeStruct((heads * rows, 2 * LANES), bf16),
            jax.ShapeDtypeStruct((heads * rows, 2 * LANES), f32),
        ),
        in_specs=[HBM] * 3 + [VMEM] * (3 + len(pools)),
        out_specs=(VMEM, VMEM),
        scratch_shapes=[pltpu.SMEM(t.shape, i32) for t in tables] + [pltpu.SemaphoreType.DMA((3,))],
        compiler_params=PARAMS,
        cost_estimate=attention_cost(heads * rows, keys),
        name="attend_local",
    )(*in_hbm(tables), new_query, new_keyval, leaf, *pools)


def attention_cost(rows, keys):
    return pl.CostEstimate(
        flops=8 * LANES * rows * keys, bytes_accessed=8 * rows * 2 * LANES, transcendentals=rows * keys
    )


def extended(query, state, pool_refs, c):
    scores = [scores_of(query, key_window(ref, c)) for ref in pool_refs]
    values = [value_window(ref, c) for ref in pool_refs]
    return fold(scores, values, unpack(state))


def chunk_kernel(*refs, blocks):
    aug_ref, state_ref = refs[:2]
    pool_refs, out_ref = refs[2:-1], refs[-1]
    size = aug_ref.shape[0] // blocks
    for b in range(blocks):
        at = slice(b * size, (b + 1) * size)
        state = extended(aug_ref[at, :], state_ref[at, :], pool_refs, b % (blocks // 2))
        out_ref[at, :] = pack(*state)


def extend_attention(aug, state, pools, kv_local):
    keys = sum(item.shape[0] for item in pools)
    return pl.pallas_call(
        functools.partial(chunk_kernel, blocks=2 * kv_local),
        out_shape=jax.ShapeDtypeStruct(state.shape, f32),
        in_specs=[VMEM] * (2 + len(pools)),
        out_specs=VMEM,
        compiler_params=PARAMS,
        cost_estimate=attention_cost(aug.shape[0], keys),
        name="attend_pages",
    )(aug, state, *pools)


def project(out_refs, rows, weight_ref, places):
    for out_ref, k in zip(out_refs, places):
        weight = weight_ref[:, piece(weight_ref.shape[1], k)]
        result = jnp.dot(rows, weight, preferred_element_type=f32)
        out_ref[...] = result.astype(out_ref.dtype)


def finish_kernel(*refs, half, kv_local, chunks, width):
    aug_ref, state_ref = refs[:2]
    pool_refs = refs[2 : 2 + chunks]
    weight_ref = refs[2 + chunks]
    part = aug_ref.shape[0] // (2 * width // HD)
    rest = refs[3 + chunks :]
    att_ref, *proj_refs, mine_ref = rest[2 * half :]
    if half:
        send_refs, proj_refs = proj_refs[: PIECES - 1], proj_refs[PIECES - 1 :]
        proj_refs, res_refs = proj_refs[:PIECES], proj_refs[PIECES:]
        project(send_refs, rest[0][...], weight_ref, range(PIECES - 1))
    group = width // (kv_local * HD)
    size = group * part
    for c in range(kv_local):
        at = slice((half * kv_local + c) * size, (half * kv_local + c + 1) * size)
        if chunks:
            state = extended(aug_ref[at, :], state_ref[at, :], pool_refs, c)
        else:
            state = unpack(state_ref[at, :])
        shift = value_shift(c)
        result = (state[2][:, shift : shift + HD] / state[1]).astype(bf16)
        for g in range(group):
            h = c * group + g
            mine_ref[:, h * HD : (h + 1) * HD] = result[g * part : (g + 1) * part]
    if half:
        mine = pl.multiple_of(half_start(2 * part, 1), part)
        theirs = pl.multiple_of(half_start(2 * part, 0), part)
        att_ref[pl.ds(mine, part), :] = mine_ref[...]
        att_ref[pl.ds(theirs, part), :] = rest[0][...]
        for k, res_ref in enumerate(res_refs):
            res_ref[...] = rest[1][pl.ds(mine, part), piece(rest[1].shape[1], k)]
    else:
        att_ref[...] = mine_ref[...]
    project(proj_refs, mine_ref[...], weight_ref, range(PIECES) if half else [PIECES - 1])


def finish_attention(aug, state, pools, out_weight, half, kv_local, rows, other):
    width = out_weight.shape[0]
    part = rows // 2
    keys = sum(item.shape[0] for item in pools)
    depth = out_weight.shape[1]
    sent = pieces_of(part, depth, bf16)
    if half:
        shapes = (*sent[:-1], *pieces_of(part, depth, f32), *pieces_of(part, depth, bf16))
    else:
        shapes = sent[-1:]
    return pl.pallas_call(
        functools.partial(
            finish_kernel, half=half, kv_local=kv_local, chunks=len(pools), width=width
        ),
        out_shape=(jax.ShapeDtypeStruct((rows if half else part, width), bf16), *shapes),
        in_specs=[VMEM] * (3 + len(pools) + len(other)),
        out_specs=(VMEM,) * (1 + len(shapes)),
        scratch_shapes=[pltpu.VMEM((part, width), bf16)],
        compiler_params=PARAMS,
        cost_estimate=attention_cost(aug.shape[0] // 2, keys + 512),
        name="attend_finish",
    )(aug, state, *pools, out_weight, *other)


def normalized(values_in, gain):
    values = values_in.astype(f32)
    scale = lax.rsqrt(jnp.mean(values * values, axis=-1, keepdims=True) + EPSILON)
    return (values * scale * gain.astype(f32)).astype(bf16)


def stage_kernel(*refs):
    count = len(refs) // 2
    for copy in fetch(zip(refs[:count], refs[count : 2 * count]), refs[-1]):
        copy.wait()


def stage(weights):
    return pl.pallas_call(
        stage_kernel,
        out_shape=tuple(pltpu.VMEM(w.shape, w.dtype) for w in weights),
        in_specs=[HBM] * len(weights),
        out_specs=(VMEM,) * len(weights),
        scratch_shapes=[pltpu.SemaphoreType.DMA((len(weights),))],
        compiler_params=pltpu.CompilerParams(vmem_limit_bytes=1024 * 1024),
        cost_estimate=pl.CostEstimate(
            flops=0, bytes_accessed=sum(2 * w.size for w in weights), transcendentals=0
        ),
        name="stage",
    )(*in_hbm(weights))


def gained(rows, gain_ref, k):
    return (wide(rows) * wide(gain_ref[:, piece(gain_ref.shape[1], k)])).astype(bf16)


def inverse_rms(row_refs):
    squares = [jnp.sum(wide(ref[...]) ** 2, axis=-1, keepdims=True) for ref in row_refs]
    depth = sum(ref.shape[1] for ref in row_refs)
    return lax.rsqrt(sum(squares) / depth + EPSILON)


def times(rows, weight_ref, k, flipped=False):
    if flipped:
        return scores_of(weight_ref[:, piece(weight_ref.shape[1], k)], rows)
    weight = weight_ref[piece(weight_ref.shape[0], k), :]
    return jnp.dot(rows, weight, preferred_element_type=f32)


def early_kernel(*refs, k, flips, terms):
    row_refs, (gain_ref, *refs) = refs[:terms], refs[terms:]
    rows = row_refs[0][...]
    if terms > 1:
        rows = add_rows(rows, row_refs[1][...], row_refs[2][...])
        refs[len(flips)][...] = rows
        refs = (*refs[: len(flips)], *refs[len(flips) + 1 :])
    rows = gained(rows, gain_ref, k)
    count = len(flips)
    for weight_ref, out_ref, flipped in zip(refs[:count], refs[count:], flips):
        out_ref[...] = times(rows, weight_ref, k, flipped)


def early_products(rows, gain, weights, k=0, flips=(False, False)):
    terms = rows if isinstance(rows, tuple) else (rows,)
    rows = terms[0]
    count = rows.shape[0]
    shapes = [
        jax.ShapeDtypeStruct((w.shape[0], count) if flipped else (count, w.shape[1]), f32)
        for w, flipped in zip(weights, flips)
    ]
    if len(terms) > 1:
        shapes.insert(0, jax.ShapeDtypeStruct(rows.shape, bf16))
    return pl.pallas_call(
        functools.partial(early_kernel, k=k, flips=flips, terms=len(terms)),
        out_shape=tuple(shapes),
        in_specs=[VMEM] * (len(terms) + 1 + len(weights)),
        out_specs=(VMEM,) * len(shapes),
        compiler_params=PARAMS,
        name="early_piece",
    )(*terms, gain.reshape(1, -1), *weights)


def mlp_kernel(*refs, second, early):
    row_refs, (gain_ref, gate_ref, up_ref, down_ref) = refs[:PIECES], refs[PIECES : PIECES + 4]
    refs = refs[PIECES + 4 :]
    sums = [0.0, 0.0]
    if early:
        sums, refs = [ref[...] for ref in refs[:2]], refs[2:]
    if second:
        project(refs[1:PIECES], refs[0][...], down_ref, range(PIECES - 1))
    scale = inverse_rms(row_refs)
    for k in range(PIECES - early):
        rows = gained(row_refs[k][...], gain_ref, k)
        sums = [item + times(rows, ref, k) for item, ref in zip(sums, (gate_ref, up_ref))]
    gate, upward = sums
    hidden = (jax.nn.silu(gate * scale) * (upward * scale)).astype(bf16)
    if second:
        project(refs[PIECES:], hidden, down_ref, range(PIECES))
    else:
        refs[0][...] = hidden
        project(refs[1:], hidden, down_ref, [PIECES - 1])


def feed_forward(rows, early, gain, gate_weight, up_weight, down_weight, other=()):
    count = rows[0].shape[0]
    depth, width = gate_weight.shape
    sent = pieces_of(count, depth, bf16)
    if other:
        shapes = (*sent[:-1], *pieces_of(count, depth, f32))
    else:
        shapes = (jax.ShapeDtypeStruct((count, width), bf16), sent[-1])
    return pl.pallas_call(
        functools.partial(mlp_kernel, second=len(other) > 0, early=min(len(early), 1)),
        out_shape=shapes,
        in_specs=[VMEM] * (PIECES + 4 + len(early) + len(other)),
        out_specs=(VMEM,) * len(shapes),
        compiler_params=PARAMS,
        cost_estimate=pl.CostEstimate(
            flops=6 * count * depth * width, bytes_accessed=6 * depth * width, transcendentals=0
        ),
        name="feed_forward",
    )(
        *rows,
        gain.reshape(1, depth),
        *in_vmem((gate_weight, up_weight, down_weight)),
        *early,
        *other,
    )


def next_kernel(*refs, half):
    row_refs, refs = refs[:PIECES], refs[PIECES:]
    gain_ref, query_ref, keyval_ref = refs[:3]
    if half:
        query, keyval = refs[3][...], refs[4][...]
        refs = (*refs[:3], *refs[5:])
        for k in range(PIECES - 1):
            rows = gained(row_refs[k][...], gain_ref, k)
            query = query + times(rows, query_ref, k)
            keyval = keyval + times(rows, keyval_ref, k, True)
        scale = inverse_rms(row_refs)
        across = jnp.broadcast_to(scale, (scale.shape[0], LANES)).T[0:1, :]
        query, keyval = (query * scale).astype(bf16), (keyval * across).astype(bf16)
    else:
        normed = normalized(joined(row_refs), gain_ref[...])
        query = jnp.dot(normed, query_ref[...], preferred_element_type=f32).astype(bf16)
        keyval = scores_of(keyval_ref[...], normed).astype(bf16)
        query_out, keyval_out = refs[3:]
        query_out[...] = query
        keyval_out[...] = keyval
        return
    query_in, keyval_in = refs[3:5]
    query_out, keyval_out, residual_out = refs[5 + PIECES :]
    part = query.shape[0]
    mine = pl.multiple_of(half_start(2 * part, 1), part)
    theirs = pl.multiple_of(half_start(2 * part, 0), part)
    query_out[pl.ds(mine, part), :] = query
    query_out[pl.ds(theirs, part), :] = query_in[...]

    @pl.when(mine == 0)
    def _():
        keyval_out[:, :part] = keyval
        keyval_out[:, part:] = keyval_in[...]

    @pl.when(mine != 0)
    def _():
        keyval_out[:, :part] = keyval_in[...]
        keyval_out[:, part:] = keyval

    share = residual_out.shape[0]
    place = lax.axis_index("tp") * share
    at = pl.multiple_of(lax.rem(place, part), share)
    held = (place >= mine) & (place < mine + part)
    for k in range(PIECES):
        ours = row_refs[k][pl.ds(at, share), :]
        others = refs[5 + k][pl.ds(at, share), :]
        residual_out[:, piece(residual_out.shape[1], k)] = jnp.where(held, ours, others)


def next_projections(rows, gain, query_weight, keyval_weight, other):
    count = rows[0].shape[0]
    depth = query_weight.shape[0]
    widths = (query_weight.shape[1], keyval_weight.shape[0])
    half = len(other) > 0
    out_rows = 2 * count if half else count
    shapes = [(out_rows, widths[0]), (widths[1], out_rows)]
    if half:
        shapes.append((out_rows // lax.axis_size("tp"), depth))
    return pl.pallas_call(
        functools.partial(next_kernel, half=half),
        out_shape=tuple(jax.ShapeDtypeStruct(shape, bf16) for shape in shapes),
        in_specs=[VMEM] * (PIECES + 3 + len(other)),
        out_specs=(VMEM,) * len(shapes),
        compiler_params=PARAMS,
        cost_estimate=pl.CostEstimate(
            flops=2 * count * depth * sum(widths),
            bytes_accessed=2 * depth * sum(widths),
            transcendentals=0,
        ),
        name="next_layer",
    )(*rows, gain.reshape(1, depth), *in_vmem([query_weight]), keyval_weight, *other)


def trade(value, axis, bit):
    size = lax.axis_size(axis)
    return lax.ppermute(value, axis, [(i, i ^ bit) for i in range(size)])


def cross(value, even_bit, odd_bit):
    size = lax.axis_size("req")
    pairs = [(i, i ^ (odd_bit if i % 2 else even_bit)) for i in range(size)]
    return lax.ppermute(value, "req", pairs)


def trades(values, bit):
    return [trade(value, "tp", bit) for value in values]


def each(join, *pieces):
    return [join(*items) for items in zip(*pieces)]


def add_pair(mine, got):
    return (mine + wide(got)).astype(bf16)


def pairs_in_turn(mine, got, weights):
    last = add_pair(mine[-1], got[-1])
    _, rest, weights = lax.optimization_barrier((last, got[:-1], weights))
    return [*each(add_pair, mine[:-1], rest), last], weights


def add_rows(pair, rows, got):
    return (wide(rows) + (wide(pair) + wide(got))).astype(bf16)


def wide(value):
    return value.astype(f32)


def per_device(
    new_query,
    new_keyval,
    residual_in,
    leaf_cache,
    leaf_length,
    new_counts,
    request_mid,
    mid_root,
    node_length,
    prefix_pool,
    page_node,
    page_rank,
    out_weight,
    norm_gain,
    gate_weight,
    up_weight,
    down_weight,
    next_gain,
    query_weight,
    keyval_weight,
):
    rows = new_query.shape[0]
    part = rows // 2
    kv_local = new_keyval.shape[1] // (2 * HD)
    pool = prepare(page_node, page_rank, node_length, mid_root, prefix_pool)
    local_args = (new_query, new_keyval, leaf_cache, leaf_length, new_counts, request_mid)
    if lax.axis_size("req") == 8:
        first = cross(pool, 2, 4)
        second = cross(pool, 4, 2)
        beside = trade(pool, "req", 1)
        aug, state = start_attention(*local_args, [pool, beside])
        first, aug, state = lax.optimization_barrier((first, aug, state))
        corner = cross(first, 4, 2)
        first, second = lax.optimization_barrier((first, second))
        near = [first, second, trade(first, "req", 1), trade(second, "req", 1)]
        state = extend_attention(aug, state, near, kv_local)
        state, down_weight = lax.optimization_barrier((state, down_weight))
        corner, state, down_weight = lax.optimization_barrier(
            (corner, state, *stage([down_weight]))
        )
        corner_other = trade(corner, "req", 1)
        state = extend_attention(aug, state, [corner], kv_local)
        pools = [corner_other]
    else:
        every = lax.all_gather(pool, "req", axis=0)
        holders = every.shape[0]
        aug, state = start_attention(*local_args, [pool])
        places = (lax.axis_index("req") + 1 + jnp.arange(holders - 1)) % holders
        step = 4
        for i in range(0, holders - 1, step):
            chunk = every[places[i : i + step]].reshape(-1, pool.shape[1])
            state = extend_attention(aug, state, [chunk], kv_local)
        pools = []

    theirs_att, *theirs_proj = finish_attention(
        aug, state, pools, out_weight, 0, kv_local, rows, ()
    )
    attention, *mine_proj = finish_attention(
        aug, state, pools, out_weight, 1, kv_local, rows, (theirs_att, residual_in)
    )
    theirs_proj = mine_proj[: PIECES - 1] + theirs_proj
    mine_proj, res_mine = mine_proj[PIECES - 1 : -PIECES], mine_proj[-PIECES:]

    mine = half_start(rows, 1)
    theirs = half_start(rows, 0)
    depth = residual_in.shape[1]
    if lax.axis_size("tp") == 4:
        got = trades(theirs_proj, 1)
        pair, (gate_weight, up_weight) = pairs_in_turn(mine_proj, got, (gate_weight, up_weight))
        got = trades(pair, 2)
        got[-1], *staged = lax.optimization_barrier((got[-1], *stage([gate_weight, up_weight])))
        mlp = (*staged, down_weight)
        lead, *early = early_products(
            (pair[-1], res_mine[-1], got[-1]), norm_gain, mlp[:2], PIECES - 1
        )
        mixed_mine = [*each(add_rows, pair[:-1], res_mine[:-1], got[:-1]), lead]
        mixed_theirs = trades(mixed_mine, 1)
        hidden, last = feed_forward(mixed_mine, early, norm_gain, *mlp)
        last = trade(last, "tp", 1)
        early = early_products(mixed_theirs[-1], norm_gain, mlp[:2], PIECES - 1)
        _, mixed_theirs[:-1] = lax.optimization_barrier((early, mixed_theirs[:-1]))
        result = feed_forward(mixed_theirs, early, norm_gain, *mlp, [hidden])
        got = [*trades(result[: PIECES - 1], 1), last]
        mlp_theirs = result[PIECES - 1 :]
        pair, (query_weight,) = pairs_in_turn(mlp_theirs, got, (query_weight,))
        got = trades(pair, 2)
        got[-1], query_weight = lax.optimization_barrier((got[-1], *stage([query_weight])))
        layer_theirs = each(add_rows, pair, mixed_theirs, got)
        layer_mine = trades(layer_theirs, 1)
    else:
        res_mine = jnp.concatenate(res_mine, axis=1)
        res_theirs = lax.dynamic_slice_in_dim(residual_in, theirs, part, 0)

        def in_order(theirs_part, mine_part):
            both = jnp.stack([theirs_part, mine_part])
            return jnp.where(mine == 0, both[::-1], both).reshape(rows, -1)

        theirs_proj = jnp.concatenate([wide(item) for item in theirs_proj], axis=1)
        mine_proj = jnp.concatenate(mine_proj, axis=1)
        total = lax.psum(in_order(theirs_proj, mine_proj), "tp")
        mixed = (wide(in_order(res_theirs, res_mine)) + total).astype(bf16)
        mixed_halves = [
            [mixed[h * part : (h + 1) * part, piece(depth, k)] for k in range(PIECES)]
            for h in range(2)
        ]
        mlp_weights = (gate_weight, up_weight, down_weight)
        hidden, last = feed_forward(mixed_halves[0], (), norm_gain, *mlp_weights)
        result = feed_forward(mixed_halves[1], (), norm_gain, *mlp_weights, [hidden])
        halves = [[*result[: PIECES - 1], last], result[PIECES - 1 :]]
        mlp = [jnp.concatenate([wide(item) for item in half], axis=1) for half in halves]
        mlp = lax.psum(jnp.concatenate(mlp, axis=0), "tp")
        layer = (wide(mixed) + mlp).astype(bf16)
        layer = [layer[:, piece(depth, k)] for k in range(PIECES)]
        layer_mine = [lax.dynamic_slice_in_dim(item, mine, part, 0) for item in layer]
        layer_theirs = [lax.dynamic_slice_in_dim(item, theirs, part, 0) for item in layer]
    weights = (next_gain, query_weight, keyval_weight.T)
    other = next_projections(layer_theirs, *weights, ())
    _, arrived = lax.optimization_barrier((other, layer_mine[-1]))
    early = early_products(arrived, next_gain, weights[1:], PIECES - 1, (False, True))
    next_query, next_keyval, residual_out = next_projections(
        layer_mine, *weights, (*early, *other, *layer_theirs)
    )
    return (attention, residual_out, next_query, next_keyval.T)


def solution(mesh):
    in_specs = (
        P("req", "tp"),
        P("req", "tp"),
        P("req", None),
        P("req", None, "tp"),
        P("req"),
        P("req", None),
        P("req"),
        P(),
        P(),
        P("req", None, "tp"),
        P("req"),
        P("req"),
        P("tp", None),
        P(),
        P(None, "tp"),
        P(None, "tp"),
        P("tp", None),
        P(),
        P(None, "tp"),
        P(None, "tp"),
    )
    out_specs = (P("req", "tp"), P(("req", "tp"), None), P("req", "tp"), P("req", "tp"))
    return jax.shard_map(
        per_device, mesh=mesh, in_specs=in_specs, out_specs=out_specs, check_vma=False
    )
```
